128 devices in a mesh: gx: 4 (over y), gy: 32 (over z, x, core).
Axes of the slice: x: 4, y: 4, z: 4, core: 2. Of those that a mesh axis runs over, the one named last changes fastest.
Arguments:
- populations: float32 [19, 128, 256, 256], P(None, 'gx', 'gy'), may hold values from 0.02 to 0.08
- mass: float32 [256, 4096], P('gx', 'gy'), may hold values from 0.2 to 1
- modulus: float32 [256, 4096], P('gx', 'gy'), may hold values from 0.1 to 0.5
- cell_live: int32 [256, 4096], P('gx', 'gy'), may hold values 0 or 1
- stiff_ref: float32 [12, 12], replicated, as said below
- rec_block: int32 [524288], P(('gx', 'gy')), may hold values from 0 to 255
- rec_owner: int32 [524288, 1], P(('gx', 'gy')), may hold values from 0 to 127; in each aligned block of 4096 rows (0 to 4095, 4096 to 8191, ...) at most 64 rows name the same one
- rec_node: int32 [524288], P(('gx', 'gy')), may hold values from 0 to 8191
- rbf_weight: float32 [524288, 256], P(('gx', 'gy')), may hold values from 0 to 2
Outputs:
- populations_next: float32 [19, 128, 256, 256], P(None, 'gx', 'gy')
- displacement: float32 [3, 256, 4096], P(None, 'gx', 'gy')
The draws below stay inside these ranges and needn't reach their ends.
Inputs may be any that keep to these rules, and one draw needn't show every extreme that they name: `rec_owner`: in the records of one device no owner is named more than 64 times, and every owner is named by some record. `stiff_ref`: symmetric with a positive diagonal that exceeds the sum of magnitudes of each row's other entries.
All inputs are finite; a program needn't handle non-finite values. No bound on the sum of `cell_live` on one device may be relied on, other than what follows from the above.
Results may differ from the reference program's by a relative error of at most 0.0003.
Values sent between devices are 32-bit elements; how exact they have to be, the bound alone decides.
No kernel may reach another device: no remote copies, remote signals or barrier semaphores. Data moves between devices by JAX's collectives and lax.ppermute only.
A program may use at most 128 MiB of HBM per device.

```python
import math
import jax
import jax.numpy as jnp
import numpy as np
from jax import lax

CX = 32
CY = 8
CZ = 256
PU = 64
PV = 128
R_DEV = 4096
ITERS = 2
NX = 128
NY = 256
NZ = 256
NU = 256
NV = 4096
CAP = 64
R_TOTAL = 524288
N_GX = 4
N_GY = 32
DEVICES = 128


def draw_stiff_ref(key, part):
    first_key, second_key = jax.random.split(jax.random.fold_in(key, 17))
    offdiag = jax.random.uniform(first_key, (12, 12), jnp.float32, -0.3, 0.3)
    offdiag = (offdiag + offdiag.T) * 0.5 * (1.0 - jnp.eye(12, dtype=jnp.float32))
    diagonal = jnp.sum(jnp.abs(offdiag), axis=1) + jax.random.uniform(second_key, (12,), jnp.float32, 0.3, 0.8)
    return offdiag + jnp.diag(diagonal)


def plant(values, rng, smallest, top_value):
    extent = values.shape
    index_at = [jax.random.randint(jax.random.fold_in(rng, axis), (), 0, extent[axis]) for axis in range(len(extent))]
    values = values.at[tuple(index_at)].set(smallest)
    longest = extent.index(max(extent))
    index_at[longest] = (index_at[longest] + 1) % extent[longest]
    return values.at[tuple(index_at)].set(top_value)


def steps_of(stream_key, extent, pieces, low, high):
    gain = 1.0
    for axis_at, parts in pieces:
        draws = jax.random.uniform(jax.random.fold_in(jax.random.fold_in(stream_key, 6), axis_at), (parts,), jnp.float32, low / len(pieces), high / len(pieces))
        gain = gain * jnp.repeat(jnp.exp(draws), extent[axis_at] // parts).reshape((-1,) + (1,) * (len(extent) - 1 - axis_at))
    return gain


def deal_out(own_key, own, number, rows, number_of, top, bound, slope):
    order = jax.random.permutation(own_key, number_of)
    crowded, common = portions_of(number_of, rows * top, bound, slope, True), portions_of(number_of, rows * top, bound, slope, False)
    places = jnp.arange(number_of)

    def named(tallies, rotation):
        used = int((tallies > 0).sum())
        fixed = max(1, used // 4)
        moved = fixed + (places - fixed + rotation * (used - fixed)) % max(1, number_of - fixed)
        return jnp.zeros((number_of,), jnp.int32).at[order[jnp.where(places < fixed, places, moved)]].set(jnp.asarray(tallies, jnp.int32))

    tallies = jnp.where(number % 4 == 0, named(crowded, number // 4), named(common, number - number // 4 - 1))
    mixed = jax.random.permutation(jax.random.fold_in(own, 3), number_of)
    donor, taker = mixed[0:number_of // 2 * 2:2], mixed[1:number_of // 2 * 2:2]
    slack = jnp.minimum(tallies[donor] - 1, bound - tallies[taker]) // 2
    slack = jnp.where((donor == order[0]) | (taker == order[0]) | (tallies[taker] == 0), 0, jnp.maximum(slack, 0))
    moved = jax.random.randint(jax.random.fold_in(own, 4), (number_of // 2,), 0, 1 << 20) % (slack + 1)
    tallies = tallies.at[donor].add(-moved).at[taker].add(moved)
    members = jnp.searchsorted(jnp.cumsum(tallies), jnp.arange(rows * top), side="right").astype(jnp.int32)
    grid = members.reshape(top, rows).T
    grid = grid[jax.random.permutation(jax.random.fold_in(own, 1), rows)]
    rotation = jax.random.randint(jax.random.fold_in(own, 2), (rows, 1), 0, top)
    return jnp.take_along_axis(grid, (jnp.arange(top)[None, :] + rotation) % top, axis=1)


def portions_of(amount, total, reach, lean, full):
    portions = [(1 << 20) // math.isqrt(standing ** lean) + 1 for standing in range(1, amount + 1)]
    largest = reach if full else min(reach, max(-(-total // amount), total * portions[0] // sum(portions)))
    least = 1 if total - largest >= amount - 1 else 0
    holding, rest = [largest] + [least] * (amount - 1), total - largest - least * (amount - 1)
    while rest > 0:
        movable = [i for i in range(1, amount) if holding[i] < largest] or [i for i in range(1, amount) if holding[i] < reach]
        pool, budget = sum([portions[i] for i in movable]), rest
        for i in movable:
            extra = min(reach - holding[i], max(1, budget * portions[i] // pool), rest)
            holding[i] = holding[i] + extra
            rest = rest - extra
    return np.array(holding)


def setup_inputs(seed: int = 0) -> dict:
    seeds = jax.random.split(jax.random.key(seed), 10)
    populations = jnp.clip(0.02 + 0.06 * jax.random.uniform(seeds[0], (19, NX, NY, NZ), jnp.float32) ** steps_of(seeds[0], (19, NX, NY, NZ), ((1, 4), (2, 32)), -0.2, 0.2), 0.02, 0.08)
    mass = jnp.clip(jnp.exp(math.log(1.0) - 1.609438 * jax.random.uniform(seeds[1], (NU, NV), jnp.float32) ** steps_of(seeds[1], (NU, NV), ((0, 4), (1, 32)), -0.2, 0.2)), 0.2, 1.0)
    modulus = jnp.clip(jnp.exp(math.log(0.5) - 1.609438 * jax.random.uniform(seeds[2], (NU, NV), jnp.float32) ** steps_of(seeds[2], (NU, NV), ((0, 4), (1, 32)), -0.2, 0.2)), 0.1, 0.5)
    cell_live = plant((jax.random.randint(seeds[3], (NU, NV), 0, 8) < 7).astype(jnp.int32), jax.random.fold_in(seeds[3], 1), 0, 1)
    stiff_ref = draw_stiff_ref(jax.random.fold_in(seeds[9], 71), 0)
    rec_block = plant(jax.random.randint(seeds[5], (R_TOTAL,), 0, CX * CY), jax.random.fold_in(seeds[5], 1), 0, (CX * CY) - 1).astype(jnp.int32)
    rec_owner_keys = jax.random.split(jax.random.fold_in(seeds[6], 1), R_TOTAL // R_DEV)
    rec_owner_turns = jax.random.permutation(jax.random.fold_in(seeds[6], 3), R_TOTAL // R_DEV)
    rec_owner = jax.vmap(lambda own, number: deal_out(jax.random.fold_in(seeds[6], 2), own, number, R_DEV, DEVICES, 1, CAP, 2))(rec_owner_keys, rec_owner_turns).reshape((R_TOTAL, 1))
    rec_node = plant(jax.random.randint(seeds[7], (R_TOTAL,), 0, PU * PV), jax.random.fold_in(seeds[7], 1), 0, (PU * PV) - 1).astype(jnp.int32)
    rbf_weight = jnp.clip(2.0 * jax.random.uniform(seeds[8], (R_TOTAL, CZ), jnp.float32) ** steps_of(seeds[8], (R_TOTAL, CZ), ((0, 128),), -0.2, 0.2), 0.0, 2.0)
    return {"populations": populations, "mass": mass, "modulus": modulus, "cell_live": cell_live, "stiff_ref": stiff_ref, "rec_block": rec_block, "rec_owner": rec_owner, "rec_node": rec_node, "rbf_weight": rbf_weight}


lattice_dirs = ((0, 0, 0), (1, 0, 0), (-1, 0, 0), (0, 1, 0), (0, -1, 0), (0, 0, 1), (0, 0, -1),
                (1, 1, 0), (-1, -1, 0), (1, -1, 0), (-1, 1, 0), (1, 0, 1), (-1, 0, -1), (1, 0, -1),
                (-1, 0, 1), (0, 1, 1), (0, -1, -1), (0, 1, -1), (0, -1, 1))
lattice_weights = (1.0 / 3.0,) + (1.0 / 18.0,) * 6 + (1.0 / 36.0,) * 12
relax_rate = 1.25
coupling = 0.1


def combine_dirs(fields, direction):
    total = None
    for axis_pos in range(3):
        if direction[axis_pos] != 0:
            term = direction[axis_pos] * fields[axis_pos]
            total = term if total is None else total + term
    return total


def collide(populations):
    density = populations[0]
    for number in range(1, 19):
        density = density + populations[number]
    moment = []
    for axis_pos in range(3):
        total = None
        for number in range(19):
            if lattice_dirs[number][axis_pos] != 0:
                term = lattice_dirs[number][axis_pos] * populations[number]
                total = term if total is None else total + term
        moment.append(total)
    velocity = [moment[axis_pos] / density for axis_pos in range(3)]
    squared = velocity[0] * velocity[0] + velocity[1] * velocity[1] + velocity[2] * velocity[2]
    relaxed = []
    for number in range(19):
        projected = combine_dirs(velocity, lattice_dirs[number])
        if projected is None:
            bracket = 1.0 - 1.5 * squared
        else:
            bracket = 1.0 + 3.0 * projected + 4.5 * projected * projected - 1.5 * squared
        equilibrium = lattice_weights[number] * density * bracket
        relaxed.append(populations[number] - relax_rate * (populations[number] - equilibrium))
    return jnp.stack(relaxed), jnp.stack(moment)


def apply_forcing(read, forcing):
    result = []
    for number in range(19):
        projected = combine_dirs(forcing, lattice_dirs[number])
        if projected is None:
            result.append(read[number])
        else:
            result.append(read[number] + 3.0 * lattice_weights[number] * projected)
    return jnp.stack(result)


def stiffness(field, scale, stiff_ref):
    corners = jnp.concatenate([field, jnp.roll(field, -1, 1), jnp.roll(field, -1, 2),
                               jnp.roll(jnp.roll(field, -1, 1), -1, 2)], 0)
    result = scale[None] * jnp.einsum('kl,lab->kab', stiff_ref, corners, precision=lax.Precision.HIGHEST)
    return (result[0:3] + jnp.roll(result[3:6], 1, 1) + jnp.roll(result[6:9], 1, 2)
            + jnp.roll(jnp.roll(result[9:12], 1, 1), 1, 2))


def reference(populations, mass, modulus, cell_live, stiff_ref, rec_block, rec_owner, rec_node, rbf_weight):
    relaxed, moment = collide(populations)
    read = jnp.stack([jnp.roll(relaxed[number], lattice_dirs[number], axis=(0, 1, 2)) for number in range(19)])
    blocks_all = moment.reshape(3, N_GX, CX, N_GY, CY, NZ).transpose(1, 3, 0, 2, 4, 5).reshape(DEVICES, 3, CX * CY, NZ)
    block_dev = rec_block.reshape(DEVICES, R_DEV)
    kernel_dev = rbf_weight.reshape(DEVICES, R_DEV, CZ)

    def interpolate(packed):
        blocks, chosen, kernel = packed
        picked = blocks[:, chosen, :]
        return jnp.sum(picked * kernel[None], axis=2)

    loads = lax.map(interpolate, (blocks_all, block_dev, kernel_dev))
    loads_flat = loads.transpose(1, 0, 2).reshape(3, R_TOTAL)
    owners = rec_owner[:, 0]
    owner_x = owners // N_GY
    owner_y = owners % N_GY
    target = (owner_x * PU + rec_node // PV) * NV + owner_y * PV + rec_node % PV
    force = jax.ops.segment_sum(loads_flat.T, target, num_segments=NU * NV).T.reshape(3, NU, NV)
    scale = cell_live.astype(jnp.float32) * (modulus + jnp.roll(modulus, -1, 0) + jnp.roll(modulus, -1, 1)
                                             + jnp.roll(jnp.roll(modulus, -1, 0), -1, 1)) * 0.25

    def operate(field):
        return mass[None] * field + stiffness(field, scale, stiff_ref)

    displacement = jnp.zeros((3, NU, NV), jnp.float32)
    residual = force
    direction = force
    norm_now = jnp.sum(residual * residual)
    for step in range(ITERS):
        image = operate(direction)
        step_size = norm_now / jnp.sum(direction * image)
        displacement = displacement + step_size * direction
        residual = residual - step_size * image
        if step + 1 < ITERS:
            norm_next = jnp.sum(residual * residual)
            direction = residual + (norm_next / norm_now) * direction
            norm_now = norm_next
    moved = displacement.reshape(3, NU * NV)[:, target]
    moved_dev = moved.reshape(3, DEVICES, R_DEV).transpose(1, 0, 2)

    def spread(packed):
        chosen, kernel, shifted = packed
        empty = jnp.zeros((3, CX * CY, CZ), jnp.float32)
        return empty.at[:, chosen, :].add(coupling * kernel[None] * shifted[:, :, None])

    forcing = lax.map(spread, (block_dev, kernel_dev, moved_dev))
    forcing = forcing.reshape(N_GX, N_GY, 3, CX, CY, NZ).transpose(2, 0, 3, 1, 4, 5).reshape(3, NX, NY, NZ)
    return apply_forcing(read, forcing), displacement
```

```python
import jax
import jax.numpy as jnp
from jax import lax
from jax.experimental import pallas as pl
from jax.experimental.pallas import tpu as pltpu
from jax.sharding import PartitionSpec as P

F32 = jnp.float32
BF16 = jnp.bfloat16
ALL = ("gx", "gy")
VMEM_LIMIT = 48 * 1024 * 1024

DIRS = (
    (0, 0, 0),
    (1, 0, 0),
    (-1, 0, 0),
    (0, 1, 0),
    (0, -1, 0),
    (0, 0, 1),
    (0, 0, -1),
    (1, 1, 0),
    (-1, -1, 0),
    (1, -1, 0),
    (-1, 1, 0),
    (1, 0, 1),
    (-1, 0, -1),
    (1, 0, -1),
    (-1, 0, 1),
    (0, 1, 1),
    (0, -1, -1),
    (0, 1, -1),
    (0, -1, 1),
)
WEIGHTS = (1.0 / 3.0,) + (1.0 / 18.0,) * 6 + (1.0 / 36.0,) * 12
RATE = 1.25
COUPLING = 0.1
XP = tuple(q for q in range(19) if DIRS[q][0] == 1)
XM = tuple(q for q in range(19) if DIRS[q][0] == -1)
YP = tuple(q for q in range(19) if DIRS[q][1] == 1)
YM = tuple(q for q in range(19) if DIRS[q][1] == -1)

R = 4096
NB = 256
NK = 256
ND = 128
CAP = 64
NU, NV = 64, 128
RB = 512
EU, EV = 72, 256


def iota(shape, dim):
    return lax.broadcasted_iota(jnp.int32, shape, dim)


def halves(x):
    high = x.astype(BF16).astype(F32)
    return high, x - high


def combine(fields, direction):
    total = None
    for axis in range(3):
        if direction[axis] != 0:
            term = fields[axis] if direction[axis] == 1 else -fields[axis]
            total = term if total is None else total + term
    return total


def dot_t(a, b):
    return lax.dot_general(a, b, (((1,), (1,)), ((), ())), preferred_element_type=F32)


def dot(a, b):
    return lax.dot_general(a, b, (((1,), (0,)), ((), ())), preferred_element_type=F32)


def load_kernel(pop_ref, w_ref, blk_ref, own_ref, node_ref, send_ref, rank_ref, m_ref, tri_ref, carry_ref):
    step = pl.program_id(0)

    @pl.when(step == 0)
    def _():
        def rows_of(i, _):
            rows = pl.ds(pl.multiple_of(i * 16, 16), 16)
            pops = [pop_ref[q, rows, :] for q in range(1, 19)]
            for axis in range(3):
                total = None
                for q in range(1, 19):
                    if DIRS[q][axis] != 0:
                        term = pops[q - 1] if DIRS[q][axis] == 1 else -pops[q - 1]
                        total = term if total is None else total + term
                high = total.astype(BF16)
                low = (total - high.astype(F32)).astype(BF16)
                at = pl.ds(pl.multiple_of(axis * NB + i * 16, 16), 16)
                m_ref[at, 0:NK] = high
                m_ref[at, NK : 2 * NK] = low
                m_ref[at, 2 * NK : 3 * NK] = high
            return 0

        lax.fori_loop(0, NB // 16, rows_of, 0)
        before = (iota((256, 256), 0) < iota((256, 256), 1)).astype(F32)
        tri_ref[:, 0:256] = before.astype(BF16)
        tri_ref[:, 256:512] = jnp.ones((256, 256), BF16)
        carry_ref[...] = jnp.zeros_like(carry_ref)
        send_ref[...] = jnp.zeros_like(send_ref)

    w = w_ref[...]
    w_high = w.astype(BF16)
    w_low = (w - w_high.astype(F32)).astype(BF16)
    w_all = jnp.concatenate([w_high, w_high, w_low], axis=1)
    at_block = iota((NB, RB), 0) == blk_ref[...]
    values = []
    for axis in range(3):
        product = dot_t(m_ref[axis * NB : (axis + 1) * NB, :], w_all)
        values.append(jnp.sum(jnp.where(at_block, product, 0.0), axis=0, keepdims=True))
    values.append(node_ref[...].astype(F32))

    named = iota((ND, RB), 0) == own_ref[...]
    named_bf = jnp.where(named, 1.0, 0.0).astype(BF16)
    ranks = []
    for part in range(RB // 256):
        cols = slice(part * 256, (part + 1) * 256)
        counts = dot(named_bf[:, cols], tri_ref[...])
        upto = counts[:, 0:256] + carry_ref[...]
        ranks.append(jnp.sum(jnp.where(named[:, cols], upto, 0.0), axis=0, keepdims=True))
        carry_ref[...] += counts[:, 256:512]
    rank = jnp.concatenate(ranks, axis=1).astype(jnp.int32)
    rank_ref[...] = rank
    in_slot = iota((CAP, RB), 0) == rank
    highs, lows = [], []
    for value in values:
        high, low = halves(value)
        highs.append(jnp.where(in_slot, high, 0.0).astype(BF16))
        lows.append(jnp.where(in_slot, low, 0.0).astype(BF16))
    packed = jnp.concatenate([jnp.concatenate(highs, axis=0), jnp.concatenate(lows, axis=0)], axis=1)
    send_ref[...] += dot_t(jnp.concatenate([named_bf, named_bf], axis=1), packed)


def loads_to_send(pops, weights, block_row, owner_row, node_row):
    row_spec = pl.BlockSpec((1, RB), lambda i: (0, i))
    return pl.pallas_call(
        load_kernel,
        grid=(R // RB,),
        in_specs=[
            pl.BlockSpec((19, NB, NK), lambda i: (0, 0, 0)),
            pl.BlockSpec((RB, NK), lambda i: (i, 0)),
            row_spec,
            row_spec,
            row_spec,
        ],
        out_specs=[pl.BlockSpec((ND, 4 * CAP), lambda i: (0, 0)), row_spec],
        out_shape=[
            jax.ShapeDtypeStruct((ND, 4 * CAP), F32),
            jax.ShapeDtypeStruct((1, R), jnp.int32),
        ],
        scratch_shapes=[
            pltpu.VMEM((3 * NB, 3 * NK), BF16),
            pltpu.VMEM((256, 512), BF16),
            pltpu.VMEM((ND, 256), F32),
        ],
        compiler_params=pltpu.CompilerParams(vmem_limit_bytes=VMEM_LIMIT),
        name="loads",
    )(pops, weights, block_row, owner_row, node_row)


def collide_kernel(pop_ref, read_ref, xp_ref, xm_ref, yp_ref, ym_ref):
    def line(x, _):
        rows = pl.ds(pl.multiple_of(x * 8, 8), 8)
        pops = [pop_ref[q, rows, :] for q in range(19)]
        density = pops[0]
        for q in range(1, 19):
            density = density + pops[q]
        inverse = 1.0 / density
        velocity = []
        for axis in range(3):
            total = None
            for q in range(1, 19):
                if DIRS[q][axis] != 0:
                    term = pops[q] if DIRS[q][axis] == 1 else -pops[q]
                    total = term if total is None else total + term
            velocity.append(total * inverse)
        squared = velocity[0] * velocity[0] + velocity[1] * velocity[1] + velocity[2] * velocity[2]
        base = 1.0 - 1.5 * squared
        for q in range(19):
            cx, cy, cz = DIRS[q]
            along = combine(velocity, DIRS[q])
            bracket = base if along is None else base + along * (3.0 + 4.5 * along)
            relaxed = pops[q] - RATE * (pops[q] - (WEIGHTS[q] * density) * bracket)
            if cz != 0:
                relaxed = pltpu.roll(relaxed, 1 if cz == 1 else NK - 1, 1)
            if cy != 0:
                relaxed = pltpu.roll(relaxed, 1 if cy == 1 else 7, 0)
            if cy == 1:
                yp_ref[YP.index(q), pl.ds(lax.rem(x + cx + 32, 32), 1), :] = relaxed[0:1, :]
            if cy == -1:
                ym_ref[YM.index(q), pl.ds(lax.rem(x + cx + 32, 32), 1), :] = relaxed[7:8, :]
            to = pl.ds(pl.multiple_of(lax.rem(x + cx + 32, 32) * 8, 8), 8)
            read_ref[q, to, :] = relaxed
        return 0

    lax.fori_loop(0, 32, line, 0)
    for i, q in enumerate(XP):
        xp_ref[i] = read_ref[q, 0:8, :]
    for i, q in enumerate(XM):
        xm_ref[i] = read_ref[q, NB - 8 : NB, :]


def collide_and_run(pops):
    return pl.pallas_call(
        collide_kernel,
        out_shape=[
            jax.ShapeDtypeStruct((19, NB, NK), F32),
            jax.ShapeDtypeStruct((5, 8, NK), F32),
            jax.ShapeDtypeStruct((5, 8, NK), F32),
            jax.ShapeDtypeStruct((5, 32, NK), F32),
            jax.ShapeDtypeStruct((5, 32, NK), F32),
        ],
        compiler_params=pltpu.CompilerParams(vmem_limit_bytes=VMEM_LIMIT),
        name="collide",
    )(pops)


def node_rows(recv_t):
    node = recv_t[3 * CAP : 4 * CAP, :].astype(jnp.int32)
    return node >> 7, node & 127


def force_kernel(recv_ref, mass_ref, mod_ref, live_ref, f_ref, low_ref, high_ref, u_ref, v_ref, hl_ref):
    recv_t = recv_ref[...].T
    u_ref[...], v_ref[...] = node_rows(recv_t)
    high, low = halves(recv_t[0 : 3 * CAP, :])
    hl_ref[0 : 3 * CAP, :] = high
    hl_ref[3 * CAP : 6 * CAP, :] = low
    u_of = iota((NU, ND), 0)
    v_of = iota((NV, ND), 0)

    def chunk(i, acc):
        at = pl.multiple_of(i * 8, 8)
        u8 = u_ref[pl.ds(at, 8), :]
        v8 = v_ref[pl.ds(at, 8), :]
        vals = [hl_ref[pl.ds(pl.multiple_of(part * CAP + at, 8), 8), :] for part in range(6)]
        lhs, rhs = [], []
        for r in range(8):
            here = u_of == u8[r : r + 1, :]
            lhs.append(
                jnp.concatenate(
                    [jnp.where(here, vals[part][r : r + 1, :], 0.0).astype(BF16) for part in range(6)], axis=0
                )
            )
            rhs.append(jnp.where(v_of == v8[r : r + 1, :], 1.0, 0.0).astype(BF16))
        return acc + dot_t(jnp.concatenate(lhs, axis=1), jnp.concatenate(rhs, axis=1))

    acc = lax.fori_loop(0, CAP // 8, chunk, jnp.zeros((6 * NU, NV), F32))
    fields = [acc[c * NU : (c + 1) * NU, :] + acc[(3 + c) * NU : (4 + c) * NU, :] for c in range(3)]
    for c in range(3):
        f_ref[c] = fields[c]
    fields = fields + [mass_ref[...], mod_ref[...], live_ref[...].astype(F32)]
    low_ref[...] = jnp.zeros_like(low_ref)
    high_ref[...] = jnp.zeros_like(high_ref)
    for i, field in enumerate(fields):
        low_ref[i : i + 1, :] = field[NU - 1 : NU, :]
        high_ref[2 * i : 2 * i + 2, :] = field[0:2, :]


def force_of(recv, mass, modulus, live):
    return pl.pallas_call(
        force_kernel,
        out_shape=[
            jax.ShapeDtypeStruct((3, NU, NV), F32),
            jax.ShapeDtypeStruct((8, 128), F32),
            jax.ShapeDtypeStruct((16, 128), F32),
        ],
        scratch_shapes=[
            pltpu.VMEM((CAP, ND), jnp.int32),
            pltpu.VMEM((CAP, ND), jnp.int32),
            pltpu.VMEM((6 * CAP, ND), F32),
        ],
        compiler_params=pltpu.CompilerParams(vmem_limit_bytes=VMEM_LIMIT),
        name="force",
    )(recv, mass, modulus, live)


def rim_tile(i, low_ref, high_ref):
    sub = iota((8, 128), 0)
    tile = jnp.where(sub == 0, high_ref[2 * i : 2 * i + 1, :], 0.0)
    tile = jnp.where(sub == 1, high_ref[2 * i + 1 : 2 * i + 2, :], tile)
    return jnp.where(sub == 7, low_ref[i : i + 1, :], tile)


def rim_kernel(f_ref, mass_ref, mod_ref, live_ref, low_ref, high_ref, to_low_ref, to_high_ref):
    fields = [f_ref[0], f_ref[1], f_ref[2], mass_ref[...], mod_ref[...], live_ref[...].astype(F32)]
    to_low_ref[...] = jnp.zeros_like(to_low_ref)
    to_high_ref[...] = jnp.zeros_like(to_high_ref)
    for i, field in enumerate(fields):
        whole = jnp.concatenate(
            [field, rim_tile(i, low_ref, high_ref), jnp.zeros((128 - EU, 128), F32)], axis=0
        )
        turned = whole.T
        to_low_ref[i : i + 1, :] = turned[127:128, :]
        to_high_ref[2 * i : 2 * i + 2, :] = turned[0:2, :]


def rim_columns(force, mass, modulus, live, low, high):
    return pl.pallas_call(
        rim_kernel,
        out_shape=[jax.ShapeDtypeStruct((8, 128), F32), jax.ShapeDtypeStruct((16, 128), F32)],
        name="rim",
    )(force, mass, modulus, live, low, high)


def shell_kernel(
    stiff_ref, f_ref, mass_ref, mod_ref, live_ref, ulow_ref, uhigh_ref, vlow_ref, vhigh_ref, recv_ref,
    y_ref, ret_ref,
    e_ref, c_ref, g_ref, y_ext_ref, fy_ref, u_ref, v_ref, rt_ref,
):
    fields = [f_ref[0], f_ref[1], f_ref[2], mass_ref[...], mod_ref[...], live_ref[...].astype(F32)]
    sub = iota((8, 128), 0)
    for i, field in enumerate(fields):
        e_ref[i, 0:NU, 0:NV] = field
        e_ref[i, NU:EU, 0:NV] = rim_tile(i, ulow_ref, uhigh_ref)
        first = jnp.where(sub == 0, vhigh_ref[2 * i : 2 * i + 1, :], 0.0)
        first = jnp.where(sub == 1, vhigh_ref[2 * i + 1 : 2 * i + 2, :], first)
        last = jnp.where(sub == 7, vlow_ref[i : i + 1, :], 0.0)
        side = jnp.concatenate([first, jnp.zeros((112, 128), F32), last], axis=0).T
        e_ref[i, :, NV:EV] = side[0:EU, :]

    def up(x):
        return pltpu.roll(x, EU - 1, 0)

    def right(x):
        return pltpu.roll(x, EV - 1, 1)

    def down(x):
        return pltpu.roll(x, 1, 0)

    def left(x):
        return pltpu.roll(x, 1, 1)

    mod = e_ref[4]
    mod = mod + up(mod)
    e_ref[5] = e_ref[5] * (mod + right(mod)) * 0.25
    for c in range(3):
        field = e_ref[c]
        moved = up(field)
        c_ref[c] = field
        c_ref[3 + c] = moved
        c_ref[6 + c] = right(field)
        c_ref[9 + c] = right(moved)

    def cells(t, _):
        rows = pl.ds(pl.multiple_of(t * 8, 8), 8)
        corner = [c_ref[k, rows, :] for k in range(12)]
        scale = e_ref[5, rows, :]
        for k in range(12):
            total = stiff_ref[k, 0] * corner[0]
            for m in range(1, 12):
                total = total + stiff_ref[k, m] * corner[m]
            g_ref[k, rows, :] = scale * total
        return 0

    lax.fori_loop(0, EU // 8, cells, 0)
    mass = e_ref[3]
    for c in range(3):
        spread = g_ref[c] + down(g_ref[3 + c])
        beside = g_ref[6 + c] + down(g_ref[9 + c])
        y_ext_ref[c] = mass * e_ref[c] + spread + left(beside)
        y_ref[c] = y_ext_ref[c, 0:NU, 0:NV]
    for c in range(3):
        field = y_ext_ref[c]
        moved = up(field)
        c_ref[c] = field
        c_ref[3 + c] = moved
        c_ref[6 + c] = right(field)
        c_ref[9 + c] = right(moved)

    def energy(t, sums):
        rows = pl.ds(pl.multiple_of(t * 8, 8), 8)
        corner = [c_ref[k, rows, 0:NV] for k in range(12)]
        total = None
        for k in range(12):
            inner = stiff_ref[k, 0] * corner[0]
            for m in range(1, 12):
                inner = inner + stiff_ref[k, m] * corner[m]
            total = corner[k] * inner if total is None else total + corner[k] * inner
        m3 = e_ref[5, rows, 0:NV] * total
        m0, m1, m2 = None, None, None
        for c in range(3):
            f = e_ref[c, rows, 0:NV]
            y = corner[c]
            m0 = f * f if m0 is None else m0 + f * f
            m1 = f * y if m1 is None else m1 + f * y
            m2 = y * y if m2 is None else m2 + y * y
        m3 = m3 + e_ref[3, rows, 0:NV] * m2
        return tuple(s + m for s, m in zip(sums, (m0, m1, m2, m3)))

    zero = jnp.zeros((8, NV), F32)
    sums = lax.fori_loop(0, NU // 8, energy, (zero, zero, zero, zero))
    lane = iota((1, 128), 1)
    moments = jnp.zeros((1, 128), F32)
    for i in range(4):
        whole = jnp.sum(jnp.sum(sums[i], axis=0, keepdims=True), axis=1, keepdims=True)
        moments = jnp.where(lane == i, whole, moments)

    for c in range(3):
        for part, field in ((c, f_ref[c]), (3 + c, y_ref[c])):
            high = field.astype(BF16)
            fy_ref[part * NU : (part + 1) * NU, 0:NV] = high
            fy_ref[part * NU : (part + 1) * NU, NV : 2 * NV] = (field - high.astype(F32)).astype(BF16)
    u_ref[...], v_ref[...] = node_rows(recv_ref[...].T)
    u_of = iota((NU, ND), 0)
    v_of = iota((NV, ND), 0)

    def chunk(i, _):
        at = pl.multiple_of(i * 8, 8)
        u8 = u_ref[pl.ds(at, 8), :]
        v8 = v_ref[pl.ds(at, 8), :]
        rhs = jnp.concatenate(
            [jnp.where(v_of == v8[r : r + 1, :], 1.0, 0.0).astype(BF16) for r in range(8)], axis=1
        )
        picked = dot(fy_ref[...], jnp.concatenate([rhs, rhs], axis=0))
        tiles = [jnp.zeros((8, ND), F32) for _ in range(6)]
        for r in range(8):
            here = u_of == u8[r : r + 1, :]
            for part in range(6):
                block = picked[part * NU : (part + 1) * NU, r * ND : (r + 1) * ND]
                row = jnp.sum(jnp.where(here, block, 0.0), axis=0, keepdims=True)
                tiles[part] = jnp.where(sub == r, row, tiles[part])
        for part in range(6):
            rt_ref[pl.ds(pl.multiple_of(part * CAP + at, 8), 8), :] = tiles[part]
        return 0

    lax.fori_loop(0, CAP // 8, chunk, 0)
    ret_ref[:, 0 : 6 * CAP] = rt_ref[...].T
    ret_ref[:, 6 * CAP : 8 * CAP] = jnp.broadcast_to(moments, (ND, 128))


def shell_of(stiff, force, mass, modulus, live, ulow, uhigh, vlow, vhigh, recv):
    vmem = pl.BlockSpec(memory_space=pltpu.VMEM)
    return pl.pallas_call(
        shell_kernel,
        in_specs=[pl.BlockSpec(memory_space=pltpu.SMEM)] + [vmem] * 9,
        out_specs=[vmem, vmem],
        out_shape=[
            jax.ShapeDtypeStruct((3, NU, NV), F32),
            jax.ShapeDtypeStruct((ND, 8 * CAP), F32),
        ],
        scratch_shapes=[
            pltpu.VMEM((6, EU, EV), F32),
            pltpu.VMEM((12, EU, EV), F32),
            pltpu.VMEM((12, EU, EV), F32),
            pltpu.VMEM((3, EU, EV), F32),
            pltpu.VMEM((6 * NU, 2 * NV), BF16),
            pltpu.VMEM((CAP, ND), jnp.int32),
            pltpu.VMEM((CAP, ND), jnp.int32),
            pltpu.VMEM((6 * CAP, ND), F32),
        ],
        compiler_params=pltpu.CompilerParams(vmem_limit_bytes=VMEM_LIMIT),
        name="shell",
    )(stiff, force, mass, modulus, live, ulow, uhigh, vlow, vhigh, recv)


RSTEPS = R // RB
XS = 4
OSTEPS = 32 // XS


def next_kernel(
    pq_ref, back_ref, w_ref, blk_ref, own_ref, rank_ref, f_ref, y_ref, read_ref, xp_ref, xm_ref, yp_ref, ym_ref,
    next_ref, disp_ref,
    x_ref, force_ref,
):
    step = pl.program_id(0)

    @pl.when(step == 0)
    def _():
        p = pq_ref[0]
        q = pq_ref[1]
        back = p * back_ref[:, 0 : 3 * CAP] + q * back_ref[:, 3 * CAP : 6 * CAP]
        turned = back.T * COUPLING
        high = turned.astype(BF16)
        x_ref[:, 0:ND] = high
        x_ref[:, ND : 2 * ND] = (turned - high.astype(F32)).astype(BF16)
        disp_ref[...] = p * f_ref[...] + q * y_ref[...]
        force_ref[...] = jnp.zeros_like(force_ref)

    @pl.when(step < RSTEPS)
    def _():
        named = jnp.where(iota((ND, RB), 0) == own_ref[...], 1.0, 0.0).astype(BF16)
        picked = dot(x_ref[...], jnp.concatenate([named, named], axis=0))
        in_slot = iota((CAP, RB), 0) == rank_ref[...]
        at_block = iota((NB, RB), 0) == blk_ref[...]
        w = w_ref[...]
        w_high = w.astype(BF16)
        w_low = (w - w_high.astype(F32)).astype(BF16)
        w_all = jnp.concatenate([w_high, w_high, w_low], axis=0)
        for c in range(3):
            moved = jnp.sum(
                jnp.where(in_slot, picked[c * CAP : (c + 1) * CAP, :], 0.0), axis=0, keepdims=True
            )
            high, low = halves(moved)
            high = jnp.where(at_block, high, 0.0).astype(BF16)
            low = jnp.where(at_block, low, 0.0).astype(BF16)
            force_ref[c * NB : (c + 1) * NB, :] += dot(jnp.concatenate([high, low, high], axis=1), w_all)

    @pl.when(step >= RSTEPS)
    def _():
        slab = step - RSTEPS
        sub = iota((8, NK), 0)
        for xx in range(XS):
            x = slab * XS + xx
            forcing = [
                force_ref[pl.ds(pl.multiple_of(c * NB + x * 8, 8), 8), :] for c in range(3)
            ]
            for q in range(19):
                cx, cy, _ = DIRS[q]
                value = read_ref[q, xx * 8 : (xx + 1) * 8, :]
                if cx == 1 and xx == 0:
                    value = jnp.where(x == 0, xp_ref[XP.index(q)], value)
                if cx == -1 and xx == XS - 1:
                    value = jnp.where(x == 31, xm_ref[XM.index(q)], value)
                if cy == 1:
                    value = jnp.where(sub == 0, yp_ref[YP.index(q), pl.ds(x, 1), :], value)
                if cy == -1:
                    value = jnp.where(sub == 7, ym_ref[YM.index(q), pl.ds(x, 1), :], value)
                along = combine(forcing, DIRS[q])
                if along is not None:
                    value = value + (3.0 * WEIGHTS[q]) * along
                next_ref[q, xx * 8 : (xx + 1) * 8, :] = value


def outputs_of(pq, back, weights, block_row, owner_row, rank_row, force, image, read, xp, xm, yp, ym):
    def record(i):
        return jnp.minimum(i, RSTEPS - 1)

    def slab(i):
        return jnp.maximum(i - RSTEPS, 0)

    row_spec = pl.BlockSpec((1, RB), lambda i: (0, record(i)))
    patch = pl.BlockSpec((3, NU, NV), lambda i: (0, 0, 0))
    lines = pl.BlockSpec((19, XS * 8, NK), lambda i: (0, slab(i), 0))
    x_face = pl.BlockSpec((5, 8, NK), lambda i: (0, 0, 0))
    y_face = pl.BlockSpec((5, 32, NK), lambda i: (0, 0, 0))
    return pl.pallas_call(
        next_kernel,
        grid=(RSTEPS + OSTEPS,),
        in_specs=[
            pl.BlockSpec(memory_space=pltpu.SMEM),
            pl.BlockSpec((ND, 8 * CAP), lambda i: (0, 0)),
            pl.BlockSpec((RB, NK), lambda i: (record(i), 0)),
            row_spec,
            row_spec,
            row_spec,
            patch,
            patch,
            lines,
            x_face,
            x_face,
            y_face,
            y_face,
        ],
        out_specs=[lines, patch],
        out_shape=[
            jax.ShapeDtypeStruct((19, NB, NK), F32),
            jax.ShapeDtypeStruct((3, NU, NV), F32),
        ],
        scratch_shapes=[
            pltpu.VMEM((3 * CAP, 2 * ND), BF16),
            pltpu.VMEM((3 * NB, NK), F32),
        ],
        compiler_params=pltpu.CompilerParams(vmem_limit_bytes=VMEM_LIMIT),
        name="outputs",
    )(pq, back, weights, block_row, owner_row, rank_row, force, image, read, xp, xm, yp, ym)


def pass_on(x, axis, shift):
    count = lax.axis_size(axis)
    return lax.ppermute(x, axis, [(i, (i + shift) % count) for i in range(count)])


def padded(field):
    for axis, dim in (("gx", 1), ("gy", 2)):
        size = field.shape[dim]
        head = lax.slice_in_dim(field, 0, 1, axis=dim)
        tail = lax.slice_in_dim(field, size - 1, size, axis=dim)
        field = jnp.concatenate([pass_on(tail, axis, 1), field, pass_on(head, axis, -1)], axis=dim)
    return field


def operate(field, mass, modulus, live, stiff):
    static = padded(jnp.stack([modulus, live.astype(F32)]))
    wide = padded(field)

    def corners(a):
        return a[..., :-1, :-1], a[..., 1:, :-1], a[..., :-1, 1:], a[..., 1:, 1:]

    c0, c1, c2, c3 = corners(static[0])
    scale = static[1, :-1, :-1] * (c0 + c1 + c2 + c3) * 0.25
    vector = jnp.concatenate(corners(wide), axis=0)
    result = scale[None] * jnp.einsum("kl,lab->kab", stiff, vector, precision=lax.Precision.HIGHEST)
    return (
        mass[None] * field
        + result[0:3, 1:, 1:]
        + result[3:6, :-1, 1:]
        + result[6:9, 1:, :-1]
        + result[9:12, :-1, :-1]
    )


def per_device(populations, mass, modulus, live, stiff, rec_block, rec_owner, rec_node, weights):
    pops = populations.reshape(19, NB, NK)
    block_row = rec_block.reshape(1, R)
    owner_row = rec_owner.reshape(1, R)
    node_row = rec_node.reshape(1, R)

    send, rank_row = loads_to_send(pops, weights, block_row, owner_row, node_row)
    recv = lax.all_to_all(send, ALL, 0, 0, tiled=True)

    read, xp, xm, yp, ym = collide_and_run(pops)
    xp = pass_on(xp, "gx", 1)
    xm = pass_on(xm, "gx", -1)
    yp = yp.at[YP.index(7), 0].set(xp[XP.index(7), 0]).at[YP.index(10), 31].set(xm[XM.index(10), 0])
    ym = ym.at[YM.index(9), 0].set(xp[XP.index(9), 7]).at[YM.index(8), 31].set(xm[XM.index(8), 7])
    yp = pass_on(yp, "gy", 1)
    ym = pass_on(ym, "gy", -1)

    force, low, high = force_of(recv, mass, modulus, live)
    ulow = pass_on(low, "gx", 1)
    uhigh = pass_on(high, "gx", -1)
    low, high = rim_columns(force, mass, modulus, live, ulow, uhigh)
    vlow = pass_on(low, "gy", 1)
    vhigh = pass_on(high, "gy", -1)
    image, ret = shell_of(stiff, force, mass, modulus, live, ulow, uhigh, vlow, vhigh, recv)
    back = lax.all_to_all(ret, ALL, 0, 0, tiled=True)

    moments = jnp.sum(back[:, 6 * CAP : 6 * CAP + 4], axis=0)
    m0, m1, m2, m3 = moments[0], moments[1], moments[2], moments[3]
    first = m0 / m1
    left_over = first * first * m2 - m0
    ratio = left_over / m0
    gain = 1.0 + ratio
    curve = gain * gain * m1 - 2.0 * gain * first * m2 + first * first * m3
    sound = (
        (left_over > 1e-3 * m0)
        & (curve > 1e-2 * gain * gain * m1)
        & (curve < 1e30)
        & (m1 > 1e-30)
        & (m0 > 1e-30)
    )

    def quick(_):
        return ratio, left_over / curve

    def careful(operands):
        force, image, mass, modulus, live, stiff = operands
        residual = force - first * image
        norm = lax.psum(jnp.sum(residual * residual), ALL)
        ratio = norm / m0
        direction = residual + ratio * force
        along = operate(direction, mass, modulus, live, stiff)
        return ratio, norm / lax.psum(jnp.sum(direction * along), ALL)

    ratio, second = lax.cond(sound, quick, careful, (force, image, mass, modulus, live, stiff))
    pq = jnp.stack([first + second * (1.0 + ratio), -(first * second)])

    populations_next, displacement = outputs_of(
        pq, back, weights, block_row, owner_row, rank_row, force, image, read, xp, xm, yp, ym
    )
    return populations_next.reshape(19, 32, 8, NK), displacement


def solution(mesh):
    return jax.shard_map(
        per_device,
        mesh=mesh,
        in_specs=(
            P(None, "gx", "gy", None),
            P("gx", "gy"),
            P("gx", "gy"),
            P("gx", "gy"),
            P(),
            P(ALL),
            P(ALL, None),
            P(ALL),
            P(ALL, None),
        ),
        out_specs=(P(None, "gx", "gy", None), P(None, "gx", "gy")),
        check_vma=False,
    )
```

```python
import jax
import jax.numpy as jnp
from jax import lax
from jax.experimental import pallas as pl
from jax.experimental.pallas import tpu as pltpu
from jax.sharding import PartitionSpec as P

F32 = jnp.float32
BF16 = jnp.bfloat16
ALL = ("gx", "gy")
VMEM_LIMIT = 60 * 1024 * 1024
SMALL_LIMIT = 16 * 1024 * 1024

DIRS = (
    (0, 0, 0),
    (1, 0, 0),
    (-1, 0, 0),
    (0, 1, 0),
    (0, -1, 0),
    (0, 0, 1),
    (0, 0, -1),
    (1, 1, 0),
    (-1, -1, 0),
    (1, -1, 0),
    (-1, 1, 0),
    (1, 0, 1),
    (-1, 0, -1),
    (1, 0, -1),
    (-1, 0, 1),
    (0, 1, 1),
    (0, -1, -1),
    (0, 1, -1),
    (0, -1, 1),
)
WEIGHTS = (1.0 / 3.0,) + (1.0 / 18.0,) * 6 + (1.0 / 36.0,) * 12
RATE = 1.25
COUPLING = 0.1
XP = tuple(q for q in range(19) if DIRS[q][0] == 1)
XM = tuple(q for q in range(19) if DIRS[q][0] == -1)
YP = tuple(q for q in range(19) if DIRS[q][1] == 1)
YM = tuple(q for q in range(19) if DIRS[q][1] == -1)

R = 4096
NB = 256
NK = 256
ND = 128
CAP = 64
NU, NV = 64, 128
RB = 1024
EU, EV = 72, 256


def iota(shape, dim):
    return lax.broadcasted_iota(jnp.int32, shape, dim)


def halves(x):
    high = x.astype(BF16).astype(F32)
    return high, x - high


def combine(fields, direction):
    total = None
    for axis in range(3):
        if direction[axis] != 0:
            term = fields[axis] if direction[axis] == 1 else -fields[axis]
            total = term if total is None else total + term
    return total


def dot_t(a, b):
    return lax.dot_general(a, b, (((1,), (1,)), ((), ())), preferred_element_type=F32)


def dot(a, b):
    return lax.dot_general(a, b, (((1,), (0,)), ((), ())), preferred_element_type=F32)


MSTEPS = 2
MROWS = NB // MSTEPS
RSTEPS = R // RB


def block_hot(row):
    return jnp.where(iota((NB, RB), 0) == row, 1.0, 0.0).astype(BF16)


def load_kernel(
    pop_ref, w_ref, blk_ref, own_all_ref, own_ref, node_ref, send_ref, rank_ref, m_ref, mt_ref, tri_ref, carry_ref
):
    step = pl.program_id(0)

    @pl.when(step == 0)
    def _():
        before = (iota((256, 256), 0) < iota((256, 256), 1)).astype(F32)
        tri_ref[:, 0:256] = before.astype(BF16)
        tri_ref[:, 256:512] = jnp.ones((256, 256), BF16)
        carry_ref[...] = jnp.zeros_like(carry_ref)
        send_ref[...] = jnp.zeros_like(send_ref)

    for part in range(MSTEPS):

        @pl.when(step == part)
        def _():
            def rows_of(i, _):
                rows = pl.ds(pl.multiple_of(i * 8, 8), 8)
                pops = [pop_ref[q, rows, :] for q in range(1, 19)]
                for axis in range(3):
                    total = None
                    for q in range(1, 19):
                        if DIRS[q][axis] != 0:
                            term = pops[q - 1] if DIRS[q][axis] == 1 else -pops[q - 1]
                            total = term if total is None else total + term
                    m_ref[axis, rows, :] = total
                return 0

            lax.fori_loop(0, MROWS // 8, rows_of, 0, unroll=2)
            for axis in range(3):
                turned = m_ref[axis].T
                high = turned.astype(BF16)
                at = slice(axis * NK, (axis + 1) * NK)
                mt_ref[at, part * MROWS : (part + 1) * MROWS] = high
                low = (turned - high.astype(F32)).astype(BF16)
                mt_ref[at, NB + part * MROWS : NB + (part + 1) * MROWS] = low
            for k in range(R // 256 // MSTEPS):
                cols = slice((part * (R // 256 // MSTEPS) + k) * 256, (part * (R // 256 // MSTEPS) + k + 1) * 256)
                named = iota((ND, 256), 0) == own_all_ref[:, cols]
                counts = dot(jnp.where(named, 1.0, 0.0).astype(BF16), tri_ref[...])
                upto = jnp.where(named, counts[:, 0:256] + carry_ref[...], 0.0)
                carry_ref[...] += counts[:, 256:512]
                rank_ref[:, cols] = jnp.sum(upto, axis=0, keepdims=True).astype(jnp.int32)

    @pl.when(step >= MSTEPS)
    def _():
        w_t = w_ref[...].T
        hot = block_hot(blk_ref[...])
        picked = dot(mt_ref[...], jnp.concatenate([hot, hot], axis=0))
        values = [
            jnp.sum(picked[axis * NK : (axis + 1) * NK, :] * w_t, axis=0, keepdims=True) for axis in range(3)
        ]
        values.append(node_ref[...].astype(F32))
        named = jnp.where(iota((ND, RB), 0) == own_ref[...], 1.0, 0.0).astype(BF16)
        rank = rank_ref[:, pl.ds(pl.multiple_of((step - MSTEPS) * RB, RB), RB)]
        in_slot = iota((CAP, RB), 0) == rank
        highs, lows = [], []
        for value in values:
            high, low = halves(value)
            highs.append(jnp.where(in_slot, high, 0.0).astype(BF16))
            lows.append(jnp.where(in_slot, low, 0.0).astype(BF16))
        packed = jnp.concatenate([jnp.concatenate(highs, axis=0), jnp.concatenate(lows, axis=0)], axis=1)
        send_ref[...] += dot_t(jnp.concatenate([named, named], axis=1), packed)


def loads_to_send(pops, weights, block_row, owner_row, node_row):
    def record(i):
        return jnp.maximum(i - MSTEPS, 0)

    row_spec = pl.BlockSpec((1, RB), lambda i: (0, record(i)))
    all_rows = pl.BlockSpec((1, R), lambda i: (0, 0))
    return pl.pallas_call(
        load_kernel,
        grid=(MSTEPS + RSTEPS,),
        in_specs=[
            pl.BlockSpec((19, MROWS, NK), lambda i: (0, jnp.minimum(i, MSTEPS - 1), 0)),
            pl.BlockSpec((RB, NK), lambda i: (record(i), 0)),
            row_spec,
            all_rows,
            row_spec,
            row_spec,
        ],
        out_specs=[pl.BlockSpec((ND, 4 * CAP), lambda i: (0, 0)), all_rows],
        out_shape=[
            jax.ShapeDtypeStruct((ND, 4 * CAP), F32),
            jax.ShapeDtypeStruct((1, R), jnp.int32),
        ],
        scratch_shapes=[
            pltpu.VMEM((3, MROWS, NK), F32),
            pltpu.VMEM((3 * NK, 2 * NB), BF16),
            pltpu.VMEM((256, 512), BF16),
            pltpu.VMEM((ND, 256), F32),
        ],
        compiler_params=pltpu.CompilerParams(vmem_limit_bytes=VMEM_LIMIT),
        name="loads",
    )(pops, weights, block_row, owner_row, owner_row, node_row)


def collide_kernel(pop_ref, read_ref, xp_ref, xm_ref, yp_ref, ym_ref):
    def line(x, _):
        rows = pl.ds(pl.multiple_of(x * 8, 8), 8)
        pops = [pop_ref[q, rows, :] for q in range(19)]
        density = pops[0]
        for q in range(1, 19):
            density = density + pops[q]
        inverse = 1.0 / density
        velocity = []
        for axis in range(3):
            total = None
            for q in range(1, 19):
                if DIRS[q][axis] != 0:
                    term = pops[q] if DIRS[q][axis] == 1 else -pops[q]
                    total = term if total is None else total + term
            velocity.append(total * inverse)
        squared = velocity[0] * velocity[0] + velocity[1] * velocity[1] + velocity[2] * velocity[2]
        base = 1.0 - 1.5 * squared
        for q in range(19):
            cx, cy, cz = DIRS[q]
            along = combine(velocity, DIRS[q])
            bracket = base if along is None else base + along * (3.0 + 4.5 * along)
            relaxed = pops[q] - RATE * (pops[q] - (WEIGHTS[q] * density) * bracket)
            if cz != 0:
                relaxed = pltpu.roll(relaxed, 1 if cz == 1 else NK - 1, 1)
            if cy != 0:
                relaxed = pltpu.roll(relaxed, 1 if cy == 1 else 7, 0)
            if cy == 1:
                yp_ref[YP.index(q), pl.ds(lax.rem(x + cx + 32, 32), 1), :] = relaxed[0:1, :]
            if cy == -1:
                ym_ref[YM.index(q), pl.ds(lax.rem(x + cx + 32, 32), 1), :] = relaxed[7:8, :]
            to = pl.ds(pl.multiple_of(lax.rem(x + cx + 32, 32) * 8, 8), 8)
            read_ref[q, to, :] = relaxed
        return 0

    lax.fori_loop(0, 32, line, 0)
    for i, q in enumerate(XP):
        xp_ref[i] = read_ref[q, 0:8, :]
    for i, q in enumerate(XM):
        xm_ref[i] = read_ref[q, NB - 8 : NB, :]


def collide_and_run(pops):
    return pl.pallas_call(
        collide_kernel,
        out_shape=[
            jax.ShapeDtypeStruct((19, NB, NK), F32),
            jax.ShapeDtypeStruct((5, 8, NK), F32),
            jax.ShapeDtypeStruct((5, 8, NK), F32),
            jax.ShapeDtypeStruct((5, 32, NK), F32),
            jax.ShapeDtypeStruct((5, 32, NK), F32),
        ],
        compiler_params=pltpu.CompilerParams(vmem_limit_bytes=VMEM_LIMIT),
        name="collide",
    )(pops)


def node_rows(recv_t):
    node = recv_t[3 * CAP : 4 * CAP, :].astype(jnp.int32)
    return node >> 7, node & 127


def force_kernel(recv_ref, mass_ref, mod_ref, live_ref, f_ref, low_ref, high_ref, u_ref, v_ref, hl_ref):
    recv_t = recv_ref[...].T
    u_ref[...], v_ref[...] = node_rows(recv_t)
    high, low = halves(recv_t[0 : 3 * CAP, :])
    hl_ref[0 : 3 * CAP, :] = high
    hl_ref[3 * CAP : 6 * CAP, :] = low
    u_of = iota((NU, ND), 0)
    v_of = iota((NV, ND), 0)

    def chunk(i, acc):
        at = pl.multiple_of(i * 8, 8)
        u8 = u_ref[pl.ds(at, 8), :]
        v8 = v_ref[pl.ds(at, 8), :]
        vals = [hl_ref[pl.ds(pl.multiple_of(part * CAP + at, 8), 8), :] for part in range(6)]
        lhs, rhs = [], []
        for r in range(8):
            here = u_of == u8[r : r + 1, :]
            lhs.append(
                jnp.concatenate(
                    [jnp.where(here, vals[part][r : r + 1, :], 0.0).astype(BF16) for part in range(6)], axis=0
                )
            )
            rhs.append(jnp.where(v_of == v8[r : r + 1, :], 1.0, 0.0).astype(BF16))
        return acc + dot_t(jnp.concatenate(lhs, axis=1), jnp.concatenate(rhs, axis=1))

    acc = lax.fori_loop(0, CAP // 8, chunk, jnp.zeros((6 * NU, NV), F32))
    fields = [acc[c * NU : (c + 1) * NU, :] + acc[(3 + c) * NU : (4 + c) * NU, :] for c in range(3)]
    for c in range(3):
        f_ref[c] = fields[c]
    fields = fields + [mass_ref[...], mod_ref[...], live_ref[...].astype(F32)]
    low_ref[...] = jnp.zeros_like(low_ref)
    high_ref[...] = jnp.zeros_like(high_ref)
    for i, field in enumerate(fields):
        low_ref[i : i + 1, :] = field[NU - 1 : NU, :]
        high_ref[2 * i : 2 * i + 2, :] = field[0:2, :]


def force_of(recv, mass, modulus, live):
    return pl.pallas_call(
        force_kernel,
        out_shape=[
            jax.ShapeDtypeStruct((3, NU, NV), F32),
            jax.ShapeDtypeStruct((8, 128), F32),
            jax.ShapeDtypeStruct((16, 128), F32),
        ],
        scratch_shapes=[
            pltpu.VMEM((CAP, ND), jnp.int32),
            pltpu.VMEM((CAP, ND), jnp.int32),
            pltpu.VMEM((6 * CAP, ND), F32),
        ],
        compiler_params=pltpu.CompilerParams(vmem_limit_bytes=SMALL_LIMIT),
        name="force",
    )(recv, mass, modulus, live)


def rim_tile(i, low_ref, high_ref):
    sub = iota((8, 128), 0)
    tile = jnp.where(sub == 0, high_ref[2 * i : 2 * i + 1, :], 0.0)
    tile = jnp.where(sub == 1, high_ref[2 * i + 1 : 2 * i + 2, :], tile)
    return jnp.where(sub == 7, low_ref[i : i + 1, :], tile)


def rim_kernel(f_ref, mass_ref, mod_ref, live_ref, low_ref, high_ref, to_low_ref, to_high_ref):
    fields = [f_ref[0], f_ref[1], f_ref[2], mass_ref[...], mod_ref[...], live_ref[...].astype(F32)]
    to_low_ref[...] = jnp.zeros_like(to_low_ref)
    to_high_ref[...] = jnp.zeros_like(to_high_ref)
    for i, field in enumerate(fields):
        whole = jnp.concatenate(
            [field, rim_tile(i, low_ref, high_ref), jnp.zeros((128 - EU, 128), F32)], axis=0
        )
        turned = whole.T
        to_low_ref[i : i + 1, :] = turned[127:128, :]
        to_high_ref[2 * i : 2 * i + 2, :] = turned[0:2, :]


def rim_columns(force, mass, modulus, live, low, high):
    return pl.pallas_call(
        rim_kernel,
        out_shape=[jax.ShapeDtypeStruct((8, 128), F32), jax.ShapeDtypeStruct((16, 128), F32)],
        compiler_params=pltpu.CompilerParams(vmem_limit_bytes=SMALL_LIMIT),
        name="rim",
    )(force, mass, modulus, live, low, high)


def shell_kernel(
    stiff_ref, f_ref, mass_ref, mod_ref, live_ref, ulow_ref, uhigh_ref, vlow_ref, vhigh_ref, recv_ref,
    y_ref, ret_ref,
    e_ref, c_ref, g_ref, y_ext_ref, fy_ref, u_ref, v_ref, rt_ref,
):
    fields = [f_ref[0], f_ref[1], f_ref[2], mass_ref[...], mod_ref[...], live_ref[...].astype(F32)]
    sub = iota((8, 128), 0)
    for i, field in enumerate(fields):
        e_ref[i, 0:NU, 0:NV] = field
        e_ref[i, NU:EU, 0:NV] = rim_tile(i, ulow_ref, uhigh_ref)
        first = jnp.where(sub == 0, vhigh_ref[2 * i : 2 * i + 1, :], 0.0)
        first = jnp.where(sub == 1, vhigh_ref[2 * i + 1 : 2 * i + 2, :], first)
        last = jnp.where(sub == 7, vlow_ref[i : i + 1, :], 0.0)
        side = jnp.concatenate([first, jnp.zeros((112, 128), F32), last], axis=0).T
        e_ref[i, :, NV:EV] = side[0:EU, :]

    def up(x):
        return pltpu.roll(x, EU - 1, 0)

    def right(x):
        return pltpu.roll(x, EV - 1, 1)

    def down(x):
        return pltpu.roll(x, 1, 0)

    def left(x):
        return pltpu.roll(x, 1, 1)

    mod = e_ref[4]
    mod = mod + up(mod)
    e_ref[5] = e_ref[5] * (mod + right(mod)) * 0.25
    for c in range(3):
        field = e_ref[c]
        moved = up(field)
        c_ref[c] = field
        c_ref[3 + c] = moved
        c_ref[6 + c] = right(field)
        c_ref[9 + c] = right(moved)

    def cells(t, _):
        rows = pl.ds(pl.multiple_of(t * 8, 8), 8)
        corner = [c_ref[k, rows, :] for k in range(12)]
        scale = e_ref[5, rows, :]
        for k in range(12):
            total = stiff_ref[k, 0] * corner[0]
            for m in range(1, 12):
                total = total + stiff_ref[k, m] * corner[m]
            g_ref[k, rows, :] = scale * total
        return 0

    lax.fori_loop(0, EU // 8, cells, 0)
    mass = e_ref[3]
    for c in range(3):
        spread = g_ref[c] + down(g_ref[3 + c])
        beside = g_ref[6 + c] + down(g_ref[9 + c])
        y_ext_ref[c] = mass * e_ref[c] + spread + left(beside)
        y_ref[c] = y_ext_ref[c, 0:NU, 0:NV]
    for c in range(3):
        field = y_ext_ref[c]
        moved = up(field)
        c_ref[c] = field
        c_ref[3 + c] = moved
        c_ref[6 + c] = right(field)
        c_ref[9 + c] = right(moved)

    def energy(t, sums):
        rows = pl.ds(pl.multiple_of(t * 8, 8), 8)
        corner = [c_ref[k, rows, 0:NV] for k in range(12)]
        total = None
        for k in range(12):
            inner = stiff_ref[k, 0] * corner[0]
            for m in range(1, 12):
                inner = inner + stiff_ref[k, m] * corner[m]
            total = corner[k] * inner if total is None else total + corner[k] * inner
        m3 = e_ref[5, rows, 0:NV] * total
        m0, m1, m2 = None, None, None
        for c in range(3):
            f = e_ref[c, rows, 0:NV]
            y = corner[c]
            m0 = f * f if m0 is None else m0 + f * f
            m1 = f * y if m1 is None else m1 + f * y
            m2 = y * y if m2 is None else m2 + y * y
        m3 = m3 + e_ref[3, rows, 0:NV] * m2
        return tuple(s + m for s, m in zip(sums, (m0, m1, m2, m3)))

    zero = jnp.zeros((8, NV), F32)
    sums = lax.fori_loop(0, NU // 8, energy, (zero, zero, zero, zero))
    lane = iota((1, 128), 1)
    moments = jnp.zeros((1, 128), F32)
    for i in range(4):
        whole = jnp.sum(jnp.sum(sums[i], axis=0, keepdims=True), axis=1, keepdims=True)
        moments = jnp.where(lane == i, whole, moments)

    for c in range(3):
        for part, field in ((c, f_ref[c]), (3 + c, y_ref[c])):
            high = field.astype(BF16)
            fy_ref[part * NU : (part + 1) * NU, 0:NV] = high
            fy_ref[part * NU : (part + 1) * NU, NV : 2 * NV] = (field - high.astype(F32)).astype(BF16)
    u_ref[...], v_ref[...] = node_rows(recv_ref[...].T)
    u_of = iota((NU, ND), 0)
    v_of = iota((NV, ND), 0)

    def chunk(i, _):
        at = pl.multiple_of(i * 8, 8)
        u8 = u_ref[pl.ds(at, 8), :]
        v8 = v_ref[pl.ds(at, 8), :]
        rhs = jnp.concatenate(
            [jnp.where(v_of == v8[r : r + 1, :], 1.0, 0.0).astype(BF16) for r in range(8)], axis=1
        )
        picked = dot(fy_ref[...], jnp.concatenate([rhs, rhs], axis=0))
        tiles = [jnp.zeros((8, ND), F32) for _ in range(6)]
        for r in range(8):
            here = u_of == u8[r : r + 1, :]
            for part in range(6):
                block = picked[part * NU : (part + 1) * NU, r * ND : (r + 1) * ND]
                row = jnp.sum(jnp.where(here, block, 0.0), axis=0, keepdims=True)
                tiles[part] = jnp.where(sub == r, row, tiles[part])
        for part in range(6):
            rt_ref[pl.ds(pl.multiple_of(part * CAP + at, 8), 8), :] = tiles[part]
        return 0

    lax.fori_loop(0, CAP // 8, chunk, 0)
    ret_ref[:, 0 : 6 * CAP] = rt_ref[...].T
    ret_ref[:, 6 * CAP : 8 * CAP] = jnp.broadcast_to(moments, (ND, 128))


def shell_of(stiff, force, mass, modulus, live, ulow, uhigh, vlow, vhigh, recv):
    vmem = pl.BlockSpec(memory_space=pltpu.VMEM)
    return pl.pallas_call(
        shell_kernel,
        in_specs=[pl.BlockSpec(memory_space=pltpu.SMEM)] + [vmem] * 9,
        out_specs=[vmem, vmem],
        out_shape=[
            jax.ShapeDtypeStruct((3, NU, NV), F32),
            jax.ShapeDtypeStruct((ND, 8 * CAP), F32),
        ],
        scratch_shapes=[
            pltpu.VMEM((6, EU, EV), F32),
            pltpu.VMEM((12, EU, EV), F32),
            pltpu.VMEM((12, EU, EV), F32),
            pltpu.VMEM((3, EU, EV), F32),
            pltpu.VMEM((6 * NU, 2 * NV), BF16),
            pltpu.VMEM((CAP, ND), jnp.int32),
            pltpu.VMEM((CAP, ND), jnp.int32),
            pltpu.VMEM((6 * CAP, ND), F32),
        ],
        compiler_params=pltpu.CompilerParams(vmem_limit_bytes=SMALL_LIMIT),
        name="shell",
    )(stiff, force, mass, modulus, live, ulow, uhigh, vlow, vhigh, recv)


def scalar_kernel(part_ref, pq_ref, sound_ref):
    row = jnp.sum(part_ref[...], axis=0, keepdims=True)
    lane = iota((1, 128), 1)
    m0, m1, m2, m3 = [
        jnp.sum(jnp.where(lane == i, row, 0.0), axis=1, keepdims=True) for i in range(4)
    ]
    first = m0 / m1
    left_over = first * first * m2 - m0
    ratio = left_over / m0
    gain = 1.0 + ratio
    curve = gain * gain * m1 - 2.0 * gain * first * m2 + first * first * m3
    second = left_over / curve
    sound = (
        (left_over > 1e-3 * m0)
        & (curve > 1e-2 * gain * gain * m1)
        & (curve < 1e30)
        & (m1 > 1e-30)
        & (m0 > 1e-30)
    )
    pq_ref[0] = (first + second * gain)[0, 0]
    pq_ref[1] = -(first * second)[0, 0]
    pq_ref[2] = first[0, 0]
    pq_ref[3] = m0[0, 0]
    sound_ref[0] = jnp.where(sound, 1, 0)[0, 0]


def scalars_of(back):
    smem = pl.BlockSpec(memory_space=pltpu.SMEM)
    return pl.pallas_call(
        scalar_kernel,
        grid=(1,),
        in_specs=[pl.BlockSpec((ND, 128), lambda i: (0, 3))],
        out_specs=[smem, smem],
        out_shape=[jax.ShapeDtypeStruct((4,), F32), jax.ShapeDtypeStruct((1,), jnp.int32)],
        name="scalars",
    )(back)


XS = 4
OSTEPS = 32 // XS


def next_kernel(
    pq_ref, back_ref, w_ref, blk_ref, own_ref, rank_ref, f_ref, y_ref, read_ref, xp_ref, xm_ref, yp_ref, ym_ref,
    next_ref, disp_ref,
    x_ref, turned_ref, force_ref,
):
    step = pl.program_id(0)

    @pl.when(step == 0)
    def _():
        p = pq_ref[0]
        q = pq_ref[1]
        back = p * back_ref[:, 0 : 3 * CAP] + q * back_ref[:, 3 * CAP : 6 * CAP]
        turned = back.T * COUPLING
        high = turned.astype(BF16)
        x_ref[:, 0:ND] = high
        x_ref[:, ND : 2 * ND] = (turned - high.astype(F32)).astype(BF16)
        disp_ref[...] = p * f_ref[...] + q * y_ref[...]
        turned_ref[...] = jnp.zeros_like(turned_ref)

    @pl.when(step < RSTEPS)
    def _():
        named = jnp.where(iota((ND, RB), 0) == own_ref[...], 1.0, 0.0).astype(BF16)
        picked = dot(x_ref[...], jnp.concatenate([named, named], axis=0))
        in_slot = iota((CAP, RB), 0) == rank_ref[...]
        w_t = w_ref[...].T
        highs, lows = [], []
        for c in range(3):
            moved = jnp.sum(
                jnp.where(in_slot, picked[c * CAP : (c + 1) * CAP, :], 0.0), axis=0, keepdims=True
            )
            part = w_t * moved
            high = part.astype(BF16)
            highs.append(high)
            lows.append((part - high.astype(F32)).astype(BF16))
        hot = block_hot(blk_ref[...])
        parts = jnp.concatenate([jnp.concatenate(highs, axis=0), jnp.concatenate(lows, axis=0)], axis=1)
        turned_ref[...] += dot_t(parts, jnp.concatenate([hot, hot], axis=1))

    @pl.when(step == RSTEPS)
    def _():
        for c in range(3):
            force_ref[c * NB : (c + 1) * NB, :] = turned_ref[c * NK : (c + 1) * NK, :].T

    @pl.when(step >= RSTEPS)
    def _():
        slab = step - RSTEPS
        sub = iota((8, NK), 0)
        for xx in range(XS):
            x = slab * XS + xx
            forcing = [
                force_ref[pl.ds(pl.multiple_of(c * NB + x * 8, 8), 8), :] for c in range(3)
            ]
            for q in range(19):
                cx, cy, _ = DIRS[q]
                value = read_ref[q, xx * 8 : (xx + 1) * 8, :]
                if cx == 1 and xx == 0:
                    value = jnp.where(x == 0, xp_ref[XP.index(q)], value)
                if cx == -1 and xx == XS - 1:
                    value = jnp.where(x == 31, xm_ref[XM.index(q)], value)
                if cy == 1:
                    value = jnp.where(sub == 0, yp_ref[YP.index(q), pl.ds(x, 1), :], value)
                if cy == -1:
                    value = jnp.where(sub == 7, ym_ref[YM.index(q), pl.ds(x, 1), :], value)
                along = combine(forcing, DIRS[q])
                if along is not None:
                    value = value + (3.0 * WEIGHTS[q]) * along
                next_ref[q, xx * 8 : (xx + 1) * 8, :] = value


def outputs_of(pq, back, weights, block_row, owner_row, rank_row, force, image, read, xp, xm, yp, ym):
    def record(i):
        return jnp.minimum(i, RSTEPS - 1)

    def slab(i):
        return jnp.maximum(i - RSTEPS, 0)

    row_spec = pl.BlockSpec((1, RB), lambda i: (0, record(i)))
    patch = pl.BlockSpec((3, NU, NV), lambda i: (0, 0, 0))
    lines = pl.BlockSpec((19, XS * 8, NK), lambda i: (0, slab(i), 0))
    x_face = pl.BlockSpec((5, 8, NK), lambda i: (0, 0, 0))
    y_face = pl.BlockSpec((5, 32, NK), lambda i: (0, 0, 0))
    return pl.pallas_call(
        next_kernel,
        grid=(RSTEPS + OSTEPS,),
        in_specs=[
            pl.BlockSpec(memory_space=pltpu.SMEM),
            pl.BlockSpec((ND, 8 * CAP), lambda i: (0, 0)),
            pl.BlockSpec((RB, NK), lambda i: (record(i), 0)),
            row_spec,
            row_spec,
            row_spec,
            patch,
            patch,
            lines,
            x_face,
            x_face,
            y_face,
            y_face,
        ],
        out_specs=[lines, patch],
        out_shape=[
            jax.ShapeDtypeStruct((19, NB, NK), F32),
            jax.ShapeDtypeStruct((3, NU, NV), F32),
        ],
        scratch_shapes=[
            pltpu.VMEM((3 * CAP, 2 * ND), BF16),
            pltpu.VMEM((3 * NK, NB), F32),
            pltpu.VMEM((3 * NB, NK), F32),
        ],
        compiler_params=pltpu.CompilerParams(vmem_limit_bytes=VMEM_LIMIT),
        name="outputs",
    )(pq, back, weights, block_row, owner_row, rank_row, force, image, read, xp, xm, yp, ym)


def pass_on(x, axis, shift):
    count = lax.axis_size(axis)
    return lax.ppermute(x, axis, [(i, (i + shift) % count) for i in range(count)])


def padded(field):
    for axis, dim in (("gx", 1), ("gy", 2)):
        size = field.shape[dim]
        head = lax.slice_in_dim(field, 0, 1, axis=dim)
        tail = lax.slice_in_dim(field, size - 1, size, axis=dim)
        field = jnp.concatenate([pass_on(tail, axis, 1), field, pass_on(head, axis, -1)], axis=dim)
    return field


def operate(field, mass, modulus, live, stiff):
    static = padded(jnp.stack([modulus, live.astype(F32)]))
    wide = padded(field)

    def corners(a):
        return a[..., :-1, :-1], a[..., 1:, :-1], a[..., :-1, 1:], a[..., 1:, 1:]

    c0, c1, c2, c3 = corners(static[0])
    scale = static[1, :-1, :-1] * (c0 + c1 + c2 + c3) * 0.25
    vector = jnp.concatenate(corners(wide), axis=0)
    result = scale[None] * jnp.einsum("kl,lab->kab", stiff, vector, precision=lax.Precision.HIGHEST)
    return (
        mass[None] * field
        + result[0:3, 1:, 1:]
        + result[3:6, :-1, 1:]
        + result[6:9, 1:, :-1]
        + result[9:12, :-1, :-1]
    )


def per_device(populations, mass, modulus, live, stiff, rec_block, rec_owner, rec_node, weights):
    pops = populations.reshape(19, NB, NK)
    block_row = rec_block.reshape(1, R)
    owner_row = rec_owner.reshape(1, R)
    node_row = rec_node.reshape(1, R)

    send, rank_row = loads_to_send(pops, weights, block_row, owner_row, node_row)
    recv = lax.all_to_all(send, ALL, 0, 0, tiled=True)

    read, xp, xm, yp, ym = collide_and_run(pops)
    xp = pass_on(xp, "gx", 1)
    xm = pass_on(xm, "gx", -1)
    yp = yp.at[YP.index(7), 0].set(xp[XP.index(7), 0]).at[YP.index(10), 31].set(xm[XM.index(10), 0])
    ym = ym.at[YM.index(9), 0].set(xp[XP.index(9), 7]).at[YM.index(8), 31].set(xm[XM.index(8), 7])
    yp = pass_on(yp, "gy", 1)
    ym = pass_on(ym, "gy", -1)

    force, low, high = force_of(recv, mass, modulus, live)
    ulow = pass_on(low, "gx", 1)
    uhigh = pass_on(high, "gx", -1)
    low, high = rim_columns(force, mass, modulus, live, ulow, uhigh)
    vlow = pass_on(low, "gy", 1)
    vhigh = pass_on(high, "gy", -1)
    image, ret = shell_of(stiff, force, mass, modulus, live, ulow, uhigh, vlow, vhigh, recv)
    back = lax.all_to_all(ret, ALL, 0, 0, tiled=True)

    back, yp, ym = lax.optimization_barrier((back, yp, ym))
    pq, sound = scalars_of(back)

    def quick(operands):
        return operands[0]

    def careful(operands):
        pq, force, image, mass, modulus, live, stiff = operands
        first = pq[2]
        residual = force - first * image
        norm = lax.psum(jnp.sum(residual * residual), ALL)
        ratio = norm / pq[3]
        direction = residual + ratio * force
        along = operate(direction, mass, modulus, live, stiff)
        second = norm / lax.psum(jnp.sum(direction * along), ALL)
        return jnp.stack([first + second * (1.0 + ratio), -(first * second), first, pq[3]])

    pq = lax.cond(sound[0] == 1, quick, careful, (pq, force, image, mass, modulus, live, stiff))

    populations_next, displacement = outputs_of(
        pq, back, weights, block_row, owner_row, rank_row, force, image, read, xp, xm, yp, ym
    )
    return populations_next.reshape(19, 32, 8, NK), displacement


def solution(mesh):
    return jax.shard_map(
        per_device,
        mesh=mesh,
        in_specs=(
            P(None, "gx", "gy", None),
            P("gx", "gy"),
            P("gx", "gy"),
            P("gx", "gy"),
            P(),
            P(ALL),
            P(ALL, None),
            P(ALL),
            P(ALL, None),
        ),
        out_specs=(P(None, "gx", "gy", None), P(None, "gx", "gy")),
        check_vma=False,
    )
```

```python
import jax
import jax.numpy as jnp
from jax import lax
from jax.experimental import pallas as pl
from jax.experimental.pallas import tpu as pltpu
from jax.sharding import PartitionSpec as P

F32 = jnp.float32
BF16 = jnp.bfloat16
ALL = ("gx", "gy")
VMEM_LIMIT = 60 * 1024 * 1024
SMALL_LIMIT = 16 * 1024 * 1024

DIRS = (
    (0, 0, 0),
    (1, 0, 0),
    (-1, 0, 0),
    (0, 1, 0),
    (0, -1, 0),
    (0, 0, 1),
    (0, 0, -1),
    (1, 1, 0),
    (-1, -1, 0),
    (1, -1, 0),
    (-1, 1, 0),
    (1, 0, 1),
    (-1, 0, -1),
    (1, 0, -1),
    (-1, 0, 1),
    (0, 1, 1),
    (0, -1, -1),
    (0, 1, -1),
    (0, -1, 1),
)
WEIGHTS = (1.0 / 3.0,) + (1.0 / 18.0,) * 6 + (1.0 / 36.0,) * 12
RATE = 1.25
COUPLING = 0.1
XP = tuple(q for q in range(19) if DIRS[q][0] == 1)
XM = tuple(q for q in range(19) if DIRS[q][0] == -1)
YP = tuple(q for q in range(19) if DIRS[q][1] == 1)
YM = tuple(q for q in range(19) if DIRS[q][1] == -1)

R = 4096
NB = 256
NK = 256
ND = 128
CAP = 64
RIM = 32
MAIN = 4 * CAP
NU, NV = 64, 128
RB = 1024
EU, EV = 72, 256


def iota(shape, dim):
    return lax.broadcasted_iota(jnp.int32, shape, dim)


def halves(x):
    high = x.astype(BF16).astype(F32)
    return high, x - high


def combine(fields, direction):
    total = None
    for axis in range(3):
        if direction[axis] != 0:
            term = fields[axis] if direction[axis] == 1 else -fields[axis]
            total = term if total is None else total + term
    return total


def dot_t(a, b):
    return lax.dot_general(a, b, (((1,), (1,)), ((), ())), preferred_element_type=F32)


def dot(a, b):
    return lax.dot_general(a, b, (((1,), (0,)), ((), ())), preferred_element_type=F32)


MSTEPS = 2
MROWS = NB // MSTEPS
RSTEPS = R // RB


def block_hot(row):
    return jnp.where(iota((NB, RB), 0) == row, 1.0, 0.0).astype(BF16)


def rim_rows(own, node):
    u, v = node >> 7, node & 127
    ox, oy = own >> 5, own & 31
    su = jnp.where(u == NU - 1, 1, jnp.where(u <= 1, -1, 0))
    sv = jnp.where(v == NV - 1, 1, jnp.where(v <= 1, -1, 0))
    ox2, oy2 = (ox + su) & 3, (oy + sv) & 31
    dests = [
        jnp.where(su != 0, ox2 * 32 + oy, -1),
        jnp.where(sv != 0, ox * 32 + oy2, -1),
        jnp.where((su != 0) & (sv != 0), ox2 * 32 + oy2, -1),
    ]
    row = jnp.where(u == NU - 1, 0, u + 1) * EV
    codes = [
        row + v,
        jnp.where(v == NV - 1, 3, v + 4) * EV + u,
        row + jnp.where(v == NV - 1, EV - 1, v + NV),
    ]
    return dests, codes


def load_kernel(
    pop_ref, w_ref, blk_ref, own_all_ref, node_all_ref, own_ref, node_ref, send_ref, rank_ref,
    m_ref, mt_ref, tri_ref, carry_ref, dest_ref, code_ref, place_ref, over_ref,
):
    step = pl.program_id(0)

    @pl.when(step == 0)
    def _():
        before = (iota((256, 256), 0) < iota((256, 256), 1)).astype(F32)
        tri_ref[:, 0:256] = before.astype(BF16)
        tri_ref[:, 256:512] = jnp.ones((256, 256), BF16)
        carry_ref[...] = jnp.zeros_like(carry_ref)
        send_ref[...] = jnp.zeros_like(send_ref)
        over_ref[...] = jnp.zeros_like(over_ref)
        dests, codes = rim_rows(own_all_ref[...], node_all_ref[...])
        for i in range(3):
            dest_ref[i : i + 1, :] = dests[i]
            code_ref[i : i + 1, :] = codes[i].astype(F32)

    for part in range(MSTEPS):

        @pl.when(step == part)
        def _():
            def rows_of(i, _):
                rows = pl.ds(pl.multiple_of(i * 8, 8), 8)
                pops = [pop_ref[q, rows, :] for q in range(1, 19)]
                for axis in range(3):
                    total = None
                    for q in range(1, 19):
                        if DIRS[q][axis] != 0:
                            term = pops[q - 1] if DIRS[q][axis] == 1 else -pops[q - 1]
                            total = term if total is None else total + term
                    m_ref[axis, rows, :] = total
                return 0

            lax.fori_loop(0, MROWS // 8, rows_of, 0, unroll=2)
            for axis in range(3):
                turned = m_ref[axis].T
                high = turned.astype(BF16)
                at = slice(axis * NK, (axis + 1) * NK)
                mt_ref[at, part * MROWS : (part + 1) * MROWS] = high
                low = (turned - high.astype(F32)).astype(BF16)
                mt_ref[at, NB + part * MROWS : NB + (part + 1) * MROWS] = low
            for k in range(R // 256 // MSTEPS):
                start = (part * (R // 256 // MSTEPS) + k) * 256
                cols = slice(start, start + 256)
                device = iota((ND, 256), 0)
                hots = [device == own_all_ref[:, cols]] + [device == dest_ref[i : i + 1, cols] for i in range(3)]
                main = jnp.where(hots[0], 1.0, 0.0).astype(BF16)
                rims = jnp.where(hots[1] | hots[2] | hots[3], 1.0, 0.0).astype(BF16)
                counts = dot(jnp.concatenate([main, rims], axis=0), tri_ref[...])
                upto = counts[:, 0:256] + carry_ref[...]
                carry_ref[...] += counts[:, 256:512]
                rank_ref[:, cols] = jnp.sum(jnp.where(hots[0], upto[0:ND], 0.0), axis=0, keepdims=True).astype(
                    jnp.int32
                )
                for i in range(3):
                    place = jnp.sum(jnp.where(hots[i + 1], upto[ND : 2 * ND], 0.0), axis=0, keepdims=True)
                    over_ref[...] = jnp.maximum(over_ref[...], place)
                    place_ref[i : i + 1, cols] = jnp.where(place < RIM - 1, place, 2.0 * RIM).astype(jnp.int32)

    @pl.when(step >= MSTEPS)
    def _():
        here = pl.ds(pl.multiple_of((step - MSTEPS) * RB, RB), RB)
        w_t = w_ref[...].T
        hot = block_hot(blk_ref[...])
        picked = dot(mt_ref[...], jnp.concatenate([hot, hot], axis=0))
        values = [
            jnp.sum(picked[axis * NK : (axis + 1) * NK, :] * w_t, axis=0, keepdims=True) for axis in range(3)
        ]
        parts = [halves(value) for value in values]
        node = halves(node_ref[...].astype(F32))

        def placed(in_slot, code):
            both = [
                jnp.concatenate(
                    [jnp.where(in_slot, part[side], 0.0).astype(BF16) for part in parts + [code]], axis=0
                )
                for side in range(2)
            ]
            return jnp.concatenate(both, axis=1)

        named = jnp.where(iota((ND, RB), 0) == own_ref[...], 1.0, 0.0).astype(BF16)
        packed = placed(iota((CAP, RB), 0) == rank_ref[:, here], node)
        send_ref[:, 0:MAIN] += dot_t(jnp.concatenate([named, named], axis=1), packed)
        for i in range(3):
            named = jnp.where(iota((ND, RB), 0) == dest_ref[i : i + 1, here], 1.0, 0.0).astype(BF16)
            packed = placed(iota((RIM, RB), 0) == place_ref[i : i + 1, here], halves(code_ref[i : i + 1, here]))
            send_ref[:, MAIN : MAIN + 4 * RIM] += dot_t(jnp.concatenate([named, named], axis=1), packed)

    @pl.when(step == MSTEPS + RSTEPS - 1)
    def _():
        most = jnp.max(over_ref[...], axis=1, keepdims=True)
        flag = jnp.where(most >= RIM - 1, 1.0, 0.0)
        tail = send_ref[:, MAIN : MAIN + 4 * RIM]
        send_ref[:, MAIN : MAIN + 4 * RIM] = jnp.where(iota((ND, 4 * RIM), 1) == 4 * RIM - 1, flag, tail)


def loads_to_send(pops, weights, block_row, owner_row, node_row):
    def record(i):
        return jnp.maximum(i - MSTEPS, 0)

    row_spec = pl.BlockSpec((1, RB), lambda i: (0, record(i)))
    all_rows = pl.BlockSpec((1, R), lambda i: (0, 0))
    return pl.pallas_call(
        load_kernel,
        grid=(MSTEPS + RSTEPS,),
        in_specs=[
            pl.BlockSpec((19, MROWS, NK), lambda i: (0, jnp.minimum(i, MSTEPS - 1), 0)),
            pl.BlockSpec((RB, NK), lambda i: (record(i), 0)),
            row_spec,
            all_rows,
            all_rows,
            row_spec,
            row_spec,
        ],
        out_specs=[pl.BlockSpec((ND, MAIN + 4 * RIM), lambda i: (0, 0)), all_rows],
        out_shape=[
            jax.ShapeDtypeStruct((ND, MAIN + 4 * RIM), F32),
            jax.ShapeDtypeStruct((1, R), jnp.int32),
        ],
        scratch_shapes=[
            pltpu.VMEM((3, MROWS, NK), F32),
            pltpu.VMEM((3 * NK, 2 * NB), BF16),
            pltpu.VMEM((256, 512), BF16),
            pltpu.VMEM((2 * ND, 256), F32),
            pltpu.VMEM((8, R), jnp.int32),
            pltpu.VMEM((8, R), F32),
            pltpu.VMEM((8, R), jnp.int32),
            pltpu.VMEM((1, 256), F32),
        ],
        compiler_params=pltpu.CompilerParams(vmem_limit_bytes=VMEM_LIMIT),
        name="loads",
    )(pops, weights, block_row, owner_row, node_row, owner_row, node_row)


def collide_kernel(pop_ref, read_ref, xp_ref, xm_ref, yp_ref, ym_ref):
    def line(x, _):
        rows = pl.ds(pl.multiple_of(x * 8, 8), 8)
        pops = [pop_ref[q, rows, :] for q in range(19)]
        density = pops[0]
        for q in range(1, 19):
            density = density + pops[q]
        inverse = 1.0 / density
        velocity = []
        for axis in range(3):
            total = None
            for q in range(1, 19):
                if DIRS[q][axis] != 0:
                    term = pops[q] if DIRS[q][axis] == 1 else -pops[q]
                    total = term if total is None else total + term
            velocity.append(total * inverse)
        squared = velocity[0] * velocity[0] + velocity[1] * velocity[1] + velocity[2] * velocity[2]
        base = 1.0 - 1.5 * squared
        for q in range(19):
            cx, cy, cz = DIRS[q]
            along = combine(velocity, DIRS[q])
            bracket = base if along is None else base + along * (3.0 + 4.5 * along)
            relaxed = pops[q] - RATE * (pops[q] - (WEIGHTS[q] * density) * bracket)
            if cz != 0:
                relaxed = pltpu.roll(relaxed, 1 if cz == 1 else NK - 1, 1)
            if cy != 0:
                relaxed = pltpu.roll(relaxed, 1 if cy == 1 else 7, 0)
            if cy == 1:
                yp_ref[YP.index(q), pl.ds(lax.rem(x + cx + 32, 32), 1), :] = relaxed[0:1, :]
            if cy == -1:
                ym_ref[YM.index(q), pl.ds(lax.rem(x + cx + 32, 32), 1), :] = relaxed[7:8, :]
            to = pl.ds(pl.multiple_of(lax.rem(x + cx + 32, 32) * 8, 8), 8)
            read_ref[q, to, :] = relaxed
        return 0

    lax.fori_loop(0, 32, line, 0)
    for i, q in enumerate(XP):
        xp_ref[i] = read_ref[q, 0:8, :]
    for i, q in enumerate(XM):
        xm_ref[i] = read_ref[q, NB - 8 : NB, :]


def collide_and_run(pops):
    return pl.pallas_call(
        collide_kernel,
        out_shape=[
            jax.ShapeDtypeStruct((19, NB, NK), F32),
            jax.ShapeDtypeStruct((5, 8, NK), F32),
            jax.ShapeDtypeStruct((5, 8, NK), F32),
            jax.ShapeDtypeStruct((5, 32, NK), F32),
            jax.ShapeDtypeStruct((5, 32, NK), F32),
        ],
        compiler_params=pltpu.CompilerParams(vmem_limit_bytes=VMEM_LIMIT),
        name="collide",
    )(pops)


def node_rows(recv_t):
    node = recv_t[3 * CAP : MAIN, :].astype(jnp.int32)
    return node >> 7, node & 127


def force_kernel(recv_ref, f_ref, rim_ref, u_ref, v_ref, hl_ref, ru_ref, rv_ref, rhl_ref):
    recv_t = recv_ref[...].T
    u_ref[...], v_ref[...] = node_rows(recv_t)
    high, low = halves(recv_t[0 : 3 * CAP, :])
    hl_ref[0 : 3 * CAP, :] = high
    hl_ref[3 * CAP : 6 * CAP, :] = low
    code = recv_t[MAIN + 3 * RIM : MAIN + 4 * RIM, :].astype(jnp.int32)
    ru_ref[...] = code >> 8
    rv_ref[...] = code & 255
    high, low = halves(recv_t[MAIN : MAIN + 3 * RIM, :])
    rhl_ref[0 : 3 * RIM, :] = high
    rhl_ref[3 * RIM : 6 * RIM, :] = low

    def chunk_of(rows_ref, cols_ref, vals_ref, slots, height, width):
        u_of = iota((height, ND), 0)
        v_of = iota((width, ND), 0)

        def chunk(i, acc):
            at = pl.multiple_of(i * 8, 8)
            u8 = rows_ref[pl.ds(at, 8), :]
            v8 = cols_ref[pl.ds(at, 8), :]
            vals = [vals_ref[pl.ds(pl.multiple_of(part * slots + at, 8), 8), :] for part in range(6)]
            lhs, rhs = [], []
            for r in range(8):
                here = u_of == u8[r : r + 1, :]
                lhs.append(
                    jnp.concatenate([jnp.where(here, vals[part][r : r + 1, :], 0.0) for part in range(6)], axis=0)
                    .astype(BF16)
                )
                rhs.append(jnp.where(v_of == v8[r : r + 1, :], 1.0, 0.0).astype(BF16))
            return acc + dot_t(jnp.concatenate(lhs, axis=1), jnp.concatenate(rhs, axis=1))

        return lax.fori_loop(0, slots // 8, chunk, jnp.zeros((6 * height, width), F32))

    acc = chunk_of(u_ref, v_ref, hl_ref, CAP, NU, NV)
    for c in range(3):
        f_ref[c] = acc[c * NU : (c + 1) * NU, :] + acc[(3 + c) * NU : (4 + c) * NU, :]
    acc = chunk_of(ru_ref, rv_ref, rhl_ref, RIM, 8, EV)
    for c in range(3):
        rim_ref[c] = acc[c * 8 : (c + 1) * 8, :] + acc[(3 + c) * 8 : (4 + c) * 8, :]


def force_of(recv):
    return pl.pallas_call(
        force_kernel,
        out_shape=[jax.ShapeDtypeStruct((3, NU, NV), F32), jax.ShapeDtypeStruct((3, 8, EV), F32)],
        scratch_shapes=[
            pltpu.VMEM((CAP, ND), jnp.int32),
            pltpu.VMEM((CAP, ND), jnp.int32),
            pltpu.VMEM((6 * CAP, ND), F32),
            pltpu.VMEM((RIM, ND), jnp.int32),
            pltpu.VMEM((RIM, ND), jnp.int32),
            pltpu.VMEM((6 * RIM, ND), F32),
        ],
        compiler_params=pltpu.CompilerParams(vmem_limit_bytes=SMALL_LIMIT),
        name="force",
    )(recv)


def edge_kernel(mass_ref, mod_ref, live_ref, low_ref, high_ref):
    low_ref[...] = jnp.zeros_like(low_ref)
    high_ref[...] = jnp.zeros_like(high_ref)
    for i, field in enumerate([mass_ref[...], mod_ref[...], live_ref[...].astype(F32)]):
        low_ref[i : i + 1, :] = field[NU - 1 : NU, :]
        high_ref[2 * i : 2 * i + 2, :] = field[0:2, :]


def rim_tile(i, low_ref, high_ref):
    sub = iota((8, 128), 0)
    tile = jnp.where(sub == 0, high_ref[2 * i : 2 * i + 1, :], 0.0)
    tile = jnp.where(sub == 1, high_ref[2 * i + 1 : 2 * i + 2, :], tile)
    return jnp.where(sub == 7, low_ref[i : i + 1, :], tile)


def side_kernel(mass_ref, mod_ref, live_ref, low_ref, high_ref, to_low_ref, to_high_ref):
    to_low_ref[...] = jnp.zeros_like(to_low_ref)
    to_high_ref[...] = jnp.zeros_like(to_high_ref)
    for i, field in enumerate([mass_ref[...], mod_ref[...], live_ref[...].astype(F32)]):
        whole = jnp.concatenate(
            [field, rim_tile(i, low_ref, high_ref), jnp.zeros((128 - EU, 128), F32)], axis=0
        )
        turned = whole.T
        to_low_ref[i : i + 1, :] = turned[127:128, :]
        to_high_ref[2 * i : 2 * i + 2, :] = turned[0:2, :]


def edge_call(kernel, name, *args):
    return pl.pallas_call(
        kernel,
        out_shape=[jax.ShapeDtypeStruct((8, 128), F32), jax.ShapeDtypeStruct((8, 128), F32)],
        compiler_params=pltpu.CompilerParams(vmem_limit_bytes=SMALL_LIMIT),
        name=name,
    )(*args)


def static_rims(mass, modulus, live):
    low, high = edge_call(edge_kernel, "edges", mass, modulus, live)
    ulow = pass_on(low, "gx", 1)
    uhigh = pass_on(high, "gx", -1)
    low, high = edge_call(side_kernel, "sides", mass, modulus, live, ulow, uhigh)
    return ulow, uhigh, pass_on(low, "gy", 1), pass_on(high, "gy", -1)


def shell_kernel(
    stiff_ref, f_ref, rim_ref, mass_ref, mod_ref, live_ref, ulow_ref, uhigh_ref, vlow_ref, vhigh_ref, recv_ref,
    y_ref, ret_ref,
    e_ref, c_ref, g_ref, y_ext_ref, fy_ref, u_ref, v_ref, rt_ref,
):
    sub = iota((8, 128), 0)

    def columns(near, far, before):
        first = jnp.where(sub == 0, near, 0.0)
        first = jnp.where(sub == 1, far, first)
        last = jnp.where(sub == 7, before, 0.0)
        return jnp.concatenate([first, jnp.zeros((112, 128), F32), last], axis=0).T

    for i, field in enumerate([mass_ref[...], mod_ref[...], live_ref[...].astype(F32)]):
        e_ref[3 + i, 0:NU, 0:NV] = field
        e_ref[3 + i, NU:EU, 0:NV] = rim_tile(i, ulow_ref, uhigh_ref)
        side = columns(
            vhigh_ref[2 * i : 2 * i + 1, :], vhigh_ref[2 * i + 1 : 2 * i + 2, :], vlow_ref[i : i + 1, :]
        )
        e_ref[3 + i, :, NV:EV] = side[0:EU, :]
    wide = iota((8, EV), 0)
    for i in range(3):
        e_ref[i, 0:NU, 0:NV] = f_ref[i]
        tile = jnp.where(wide == 0, rim_ref[i, 1:2, :], 0.0)
        tile = jnp.where(wide == 1, rim_ref[i, 2:3, :], tile)
        e_ref[i, NU:EU, :] = jnp.where(wide == 7, rim_ref[i, 0:1, :], tile)
        side = columns(rim_ref[i, 4:5, 0:128], rim_ref[i, 5:6, 0:128], rim_ref[i, 3:4, 0:128])
        e_ref[i, 0:NU, NV:EV] = side[0:NU, :]

    def up(x):
        return pltpu.roll(x, EU - 1, 0)

    def right(x):
        return pltpu.roll(x, EV - 1, 1)

    def down(x):
        return pltpu.roll(x, 1, 0)

    def left(x):
        return pltpu.roll(x, 1, 1)

    mod = e_ref[4]
    mod = mod + up(mod)
    e_ref[5] = e_ref[5] * (mod + right(mod)) * 0.25
    for c in range(3):
        field = e_ref[c]
        moved = up(field)
        c_ref[c] = field
        c_ref[3 + c] = moved
        c_ref[6 + c] = right(field)
        c_ref[9 + c] = right(moved)

    def cells(t, _):
        rows = pl.ds(pl.multiple_of(t * 8, 8), 8)
        corner = [c_ref[k, rows, :] for k in range(12)]
        scale = e_ref[5, rows, :]
        for k in range(12):
            total = stiff_ref[k, 0] * corner[0]
            for m in range(1, 12):
                total = total + stiff_ref[k, m] * corner[m]
            g_ref[k, rows, :] = scale * total
        return 0

    lax.fori_loop(0, EU // 8, cells, 0)
    mass = e_ref[3]
    for c in range(3):
        spread = g_ref[c] + down(g_ref[3 + c])
        beside = g_ref[6 + c] + down(g_ref[9 + c])
        y_ext_ref[c] = mass * e_ref[c] + spread + left(beside)
        y_ref[c] = y_ext_ref[c, 0:NU, 0:NV]
    for c in range(3):
        field = y_ext_ref[c]
        moved = up(field)
        c_ref[c] = field
        c_ref[3 + c] = moved
        c_ref[6 + c] = right(field)
        c_ref[9 + c] = right(moved)

    def energy(t, sums):
        rows = pl.ds(pl.multiple_of(t * 8, 8), 8)
        corner = [c_ref[k, rows, 0:NV] for k in range(12)]
        total = None
        for k in range(12):
            inner = stiff_ref[k, 0] * corner[0]
            for m in range(1, 12):
                inner = inner + stiff_ref[k, m] * corner[m]
            total = corner[k] * inner if total is None else total + corner[k] * inner
        m3 = e_ref[5, rows, 0:NV] * total
        m0, m1, m2 = None, None, None
        for c in range(3):
            f = e_ref[c, rows, 0:NV]
            y = corner[c]
            m0 = f * f if m0 is None else m0 + f * f
            m1 = f * y if m1 is None else m1 + f * y
            m2 = y * y if m2 is None else m2 + y * y
        m3 = m3 + e_ref[3, rows, 0:NV] * m2
        return tuple(s + m for s, m in zip(sums, (m0, m1, m2, m3)))

    zero = jnp.zeros((8, NV), F32)
    sums = lax.fori_loop(0, NU // 8, energy, (zero, zero, zero, zero))
    lane = iota((1, 128), 1)
    moments = jnp.zeros((1, 128), F32)
    for i in range(4):
        whole = jnp.sum(jnp.sum(sums[i], axis=0, keepdims=True), axis=1, keepdims=True)
        moments = jnp.where(lane == i, whole, moments)
    over = jnp.max(recv_ref[:, MAIN + 4 * RIM - 1 : MAIN + 4 * RIM], axis=0, keepdims=True)
    moments = jnp.where(lane == 4, over, moments)

    for c in range(3):
        for part, field in ((c, f_ref[c]), (3 + c, y_ref[c])):
            high = field.astype(BF16)
            fy_ref[part * NU : (part + 1) * NU, 0:NV] = high
            fy_ref[part * NU : (part + 1) * NU, NV : 2 * NV] = (field - high.astype(F32)).astype(BF16)
    u_ref[...], v_ref[...] = node_rows(recv_ref[:, 0:MAIN].T)
    u_of = iota((NU, ND), 0)
    v_of = iota((NV, ND), 0)

    def chunk(i, _):
        at = pl.multiple_of(i * 8, 8)
        u8 = u_ref[pl.ds(at, 8), :]
        v8 = v_ref[pl.ds(at, 8), :]
        rhs = jnp.concatenate(
            [jnp.where(v_of == v8[r : r + 1, :], 1.0, 0.0).astype(BF16) for r in range(8)], axis=1
        )
        picked = dot(fy_ref[...], jnp.concatenate([rhs, rhs], axis=0))
        tiles = [jnp.zeros((8, ND), F32) for _ in range(6)]
        for r in range(8):
            here = u_of == u8[r : r + 1, :]
            for part in range(6):
                block = picked[part * NU : (part + 1) * NU, r * ND : (r + 1) * ND]
                row = jnp.sum(jnp.where(here, block, 0.0), axis=0, keepdims=True)
                tiles[part] = jnp.where(sub == r, row, tiles[part])
        for part in range(6):
            rt_ref[pl.ds(pl.multiple_of(part * CAP + at, 8), 8), :] = tiles[part]
        return 0

    lax.fori_loop(0, CAP // 8, chunk, 0)
    ret_ref[:, 0 : 6 * CAP] = rt_ref[...].T
    ret_ref[:, 6 * CAP : 8 * CAP] = jnp.broadcast_to(moments, (ND, 128))


def shell_of(stiff, force, rim, mass, modulus, live, rims, recv):
    vmem = pl.BlockSpec(memory_space=pltpu.VMEM)
    return pl.pallas_call(
        shell_kernel,
        in_specs=[pl.BlockSpec(memory_space=pltpu.SMEM)] + [vmem] * 10,
        out_specs=[vmem, vmem],
        out_shape=[
            jax.ShapeDtypeStruct((3, NU, NV), F32),
            jax.ShapeDtypeStruct((ND, 8 * CAP), F32),
        ],
        scratch_shapes=[
            pltpu.VMEM((6, EU, EV), F32),
            pltpu.VMEM((12, EU, EV), F32),
            pltpu.VMEM((12, EU, EV), F32),
            pltpu.VMEM((3, EU, EV), F32),
            pltpu.VMEM((6 * NU, 2 * NV), BF16),
            pltpu.VMEM((CAP, ND), jnp.int32),
            pltpu.VMEM((CAP, ND), jnp.int32),
            pltpu.VMEM((6 * CAP, ND), F32),
        ],
        compiler_params=pltpu.CompilerParams(vmem_limit_bytes=SMALL_LIMIT),
        name="shell",
    )(stiff, force, rim, mass, modulus, live, *rims, recv)


def scalar_kernel(part_ref, pq_ref, sound_ref):
    row = jnp.sum(part_ref[...], axis=0, keepdims=True)
    lane = iota((1, 128), 1)
    m0, m1, m2, m3, over = [
        jnp.sum(jnp.where(lane == i, row, 0.0), axis=1, keepdims=True) for i in range(5)
    ]
    first = m0 / m1
    left_over = first * first * m2 - m0
    ratio = left_over / m0
    gain = 1.0 + ratio
    curve = gain * gain * m1 - 2.0 * gain * first * m2 + first * first * m3
    second = left_over / curve
    sound = (
        (over == 0.0)
        & (left_over > 1e-3 * m0)
        & (curve > 1e-2 * gain * gain * m1)
        & (curve < 1e30)
        & (m1 > 1e-30)
        & (m0 > 1e-30)
    )
    pq_ref[0] = (first + second * gain)[0, 0]
    pq_ref[1] = -(first * second)[0, 0]
    sound_ref[0] = jnp.where(sound, 1, 0)[0, 0]


def scalars_of(back):
    smem = pl.BlockSpec(memory_space=pltpu.SMEM)
    return pl.pallas_call(
        scalar_kernel,
        grid=(1,),
        in_specs=[pl.BlockSpec((ND, 128), lambda i: (0, 3))],
        out_specs=[smem, smem],
        out_shape=[jax.ShapeDtypeStruct((2,), F32), jax.ShapeDtypeStruct((1,), jnp.int32)],
        name="scalars",
    )(back)


XS = 4
OSTEPS = 32 // XS


def next_kernel(
    pq_ref, back_ref, w_ref, blk_ref, own_ref, rank_ref, f_ref, y_ref, read_ref, xp_ref, xm_ref, yp_ref, ym_ref,
    next_ref, disp_ref,
    x_ref, turned_ref, force_ref,
):
    step = pl.program_id(0)

    @pl.when(step == 0)
    def _():
        p = pq_ref[0]
        q = pq_ref[1]
        back = p * back_ref[:, 0 : 3 * CAP] + q * back_ref[:, 3 * CAP : 6 * CAP]
        turned = back.T * COUPLING
        high = turned.astype(BF16)
        x_ref[:, 0:ND] = high
        x_ref[:, ND : 2 * ND] = (turned - high.astype(F32)).astype(BF16)
        disp_ref[...] = p * f_ref[...] + q * y_ref[...]
        turned_ref[...] = jnp.zeros_like(turned_ref)

    @pl.when(step < RSTEPS)
    def _():
        named = jnp.where(iota((ND, RB), 0) == own_ref[...], 1.0, 0.0).astype(BF16)
        picked = dot(x_ref[...], jnp.concatenate([named, named], axis=0))
        in_slot = iota((CAP, RB), 0) == rank_ref[...]
        w_t = w_ref[...].T
        highs, lows = [], []
        for c in range(3):
            moved = jnp.sum(
                jnp.where(in_slot, picked[c * CAP : (c + 1) * CAP, :], 0.0), axis=0, keepdims=True
            )
            part = w_t * moved
            high = part.astype(BF16)
            highs.append(high)
            lows.append((part - high.astype(F32)).astype(BF16))
        hot = block_hot(blk_ref[...])
        parts = jnp.concatenate([jnp.concatenate(highs, axis=0), jnp.concatenate(lows, axis=0)], axis=1)
        turned_ref[...] += dot_t(parts, jnp.concatenate([hot, hot], axis=1))

    @pl.when(step == RSTEPS)
    def _():
        for c in range(3):
            force_ref[c * NB : (c + 1) * NB, :] = turned_ref[c * NK : (c + 1) * NK, :].T

    @pl.when(step >= RSTEPS)
    def _():
        slab = step - RSTEPS
        sub = iota((8, NK), 0)
        for xx in range(XS):
            x = slab * XS + xx
            forcing = [
                force_ref[pl.ds(pl.multiple_of(c * NB + x * 8, 8), 8), :] for c in range(3)
            ]
            for q in range(19):
                cx, cy, _ = DIRS[q]
                value = read_ref[q, xx * 8 : (xx + 1) * 8, :]
                if cx == 1 and xx == 0:
                    value = jnp.where(x == 0, xp_ref[XP.index(q)], value)
                if cx == -1 and xx == XS - 1:
                    value = jnp.where(x == 31, xm_ref[XM.index(q)], value)
                if cy == 1:
                    value = jnp.where(sub == 0, yp_ref[YP.index(q), pl.ds(x, 1), :], value)
                if cy == -1:
                    value = jnp.where(sub == 7, ym_ref[YM.index(q), pl.ds(x, 1), :], value)
                along = combine(forcing, DIRS[q])
                if along is not None:
                    value = value + (3.0 * WEIGHTS[q]) * along
                next_ref[q, xx * 8 : (xx + 1) * 8, :] = value


def outputs_of(pq, back, weights, block_row, owner_row, rank_row, force, image, read, xp, xm, yp, ym):
    def record(i):
        return jnp.minimum(i, RSTEPS - 1)

    def slab(i):
        return jnp.maximum(i - RSTEPS, 0)

    row_spec = pl.BlockSpec((1, RB), lambda i: (0, record(i)))
    patch = pl.BlockSpec((3, NU, NV), lambda i: (0, 0, 0))
    lines = pl.BlockSpec((19, XS * 8, NK), lambda i: (0, slab(i), 0))
    x_face = pl.BlockSpec((5, 8, NK), lambda i: (0, 0, 0))
    y_face = pl.BlockSpec((5, 32, NK), lambda i: (0, 0, 0))
    return pl.pallas_call(
        next_kernel,
        grid=(RSTEPS + OSTEPS,),
        in_specs=[
            pl.BlockSpec(memory_space=pltpu.SMEM),
            pl.BlockSpec((ND, 8 * CAP), lambda i: (0, 0)),
            pl.BlockSpec((RB, NK), lambda i: (record(i), 0)),
            row_spec,
            row_spec,
            row_spec,
            patch,
            patch,
            lines,
            x_face,
            x_face,
            y_face,
            y_face,
        ],
        out_specs=[lines, patch],
        out_shape=[
            jax.ShapeDtypeStruct((19, NB, NK), F32),
            jax.ShapeDtypeStruct((3, NU, NV), F32),
        ],
        scratch_shapes=[
            pltpu.VMEM((3 * CAP, 2 * ND), BF16),
            pltpu.VMEM((3 * NK, NB), F32),
            pltpu.VMEM((3 * NB, NK), F32),
        ],
        compiler_params=pltpu.CompilerParams(vmem_limit_bytes=VMEM_LIMIT),
        name="outputs",
    )(pq, back, weights, block_row, owner_row, rank_row, force, image, read, xp, xm, yp, ym)


def pass_on(x, axis, shift):
    count = lax.axis_size(axis)
    return lax.ppermute(x, axis, [(i, (i + shift) % count) for i in range(count)])


def padded(field):
    for axis, dim in (("gx", 1), ("gy", 2)):
        size = field.shape[dim]
        head = lax.slice_in_dim(field, 0, 1, axis=dim)
        tail = lax.slice_in_dim(field, size - 1, size, axis=dim)
        field = jnp.concatenate([pass_on(tail, axis, 1), field, pass_on(head, axis, -1)], axis=dim)
    return field


def operate(field, mass, modulus, live, stiff):
    static = padded(jnp.stack([modulus, live.astype(F32)]))
    wide = padded(field)

    def corners(a):
        return a[..., :-1, :-1], a[..., 1:, :-1], a[..., :-1, 1:], a[..., 1:, 1:]

    c0, c1, c2, c3 = corners(static[0])
    scale = static[1, :-1, :-1] * (c0 + c1 + c2 + c3) * 0.25
    vector = jnp.concatenate(corners(wide), axis=0)
    result = scale[None] * jnp.einsum("kl,lab->kab", stiff, vector, precision=lax.Precision.HIGHEST)
    return (
        mass[None] * field
        + result[0:3, 1:, 1:]
        + result[3:6, :-1, 1:]
        + result[6:9, 1:, :-1]
        + result[9:12, :-1, :-1]
    )


def rim_of(force):
    before = pass_on(force[:, NU - 1 : NU, :], "gx", 1)
    after = pass_on(force[:, 0:2, :], "gx", -1)
    tall = jnp.concatenate([force, after, before], axis=1)
    left = pass_on(tall[:, :, NV - 1 : NV], "gy", 1)
    right = pass_on(tall[:, :, 0:2], "gy", -1)
    gap = jnp.zeros((3, EV - NV - 3), F32)
    rows = [
        jnp.concatenate([tall[:, r], right[:, r], gap, left[:, r]], axis=1) for r in (NU + 2, NU, NU + 1)
    ]
    beside = [
        jnp.concatenate([column[:, 0:NU], jnp.zeros((3, EV - NU), F32)], axis=1)
        for column in (left[:, :, 0], right[:, :, 0], right[:, :, 1])
    ]
    empty = jnp.zeros((3, EV), F32)
    return jnp.stack(rows + beside + [empty, empty], axis=1)


def exchange(x):
    return lax.all_to_all(x, ALL, 0, 0, tiled=True)


def per_device(populations, mass, modulus, live, stiff, rec_block, rec_owner, rec_node, weights):
    pops = populations.reshape(19, NB, NK)
    block_row = rec_block.reshape(1, R)
    owner_row = rec_owner.reshape(1, R)
    node_row = rec_node.reshape(1, R)

    rims = static_rims(mass, modulus, live)
    send, rank_row = loads_to_send(pops, weights, block_row, owner_row, node_row)
    recv = exchange(send)

    read, xp, xm, yp, ym = collide_and_run(pops)
    xp = pass_on(xp, "gx", 1)
    xm = pass_on(xm, "gx", -1)
    yp = yp.at[YP.index(7), 0].set(xp[XP.index(7), 0]).at[YP.index(10), 31].set(xm[XM.index(10), 0])
    ym = ym.at[YM.index(9), 0].set(xp[XP.index(9), 7]).at[YM.index(8), 31].set(xm[XM.index(8), 7])
    yp = pass_on(yp, "gy", 1)
    ym = pass_on(ym, "gy", -1)

    force, rim = force_of(recv)
    image, ret = shell_of(stiff, force, rim, mass, modulus, live, rims, recv)
    back = exchange(ret)

    back, yp, ym = lax.optimization_barrier((back, yp, ym))
    pq, sound = scalars_of(back)

    def quick(operands):
        return operands[0:3]

    def careful(operands):
        _, _, _, force, mass, modulus, live, stiff, rims, recv = operands
        image, ret = shell_of(stiff, force, rim_of(force), mass, modulus, live, rims, recv)
        back = exchange(ret)
        start = lax.psum(jnp.sum(force * force), ALL)
        first = start / lax.psum(jnp.sum(force * image), ALL)
        residual = force - first * image
        norm = lax.psum(jnp.sum(residual * residual), ALL)
        ratio = norm / start
        direction = residual + ratio * force
        along = operate(direction, mass, modulus, live, stiff)
        second = norm / lax.psum(jnp.sum(direction * along), ALL)
        return jnp.stack([first + second * (1.0 + ratio), -(first * second)]), image, back

    pq, image, back = lax.cond(
        sound[0] == 1, quick, careful, (pq, image, back, force, mass, modulus, live, stiff, rims, recv)
    )

    populations_next, displacement = outputs_of(
        pq, back, weights, block_row, owner_row, rank_row, force, image, read, xp, xm, yp, ym
    )
    return populations_next.reshape(19, 32, 8, NK), displacement


def solution(mesh):
    return jax.shard_map(
        per_device,
        mesh=mesh,
        in_specs=(
            P(None, "gx", "gy", None),
            P("gx", "gy"),
            P("gx", "gy"),
            P("gx", "gy"),
            P(),
            P(ALL),
            P(ALL, None),
            P(ALL),
            P(ALL, None),
        ),
        out_specs=(P(None, "gx", "gy", None), P(None, "gx", "gy")),
        check_vma=False,
    )
```

```python
import jax
import jax.numpy as jnp
from jax import lax
from jax.experimental import pallas as pl
from jax.experimental.pallas import tpu as pltpu
from jax.sharding import PartitionSpec as P

F32 = jnp.float32
BF16 = jnp.bfloat16
ALL = ("gx", "gy")
VMEM_LIMIT = 60 * 1024 * 1024
SMALL_LIMIT = 16 * 1024 * 1024

DIRS = (
    (0, 0, 0),
    (1, 0, 0),
    (-1, 0, 0),
    (0, 1, 0),
    (0, -1, 0),
    (0, 0, 1),
    (0, 0, -1),
    (1, 1, 0),
    (-1, -1, 0),
    (1, -1, 0),
    (-1, 1, 0),
    (1, 0, 1),
    (-1, 0, -1),
    (1, 0, -1),
    (-1, 0, 1),
    (0, 1, 1),
    (0, -1, -1),
    (0, 1, -1),
    (0, -1, 1),
)
WEIGHTS = (1.0 / 3.0,) + (1.0 / 18.0,) * 6 + (1.0 / 36.0,) * 12
RATE = 1.25
COUPLING = 0.1
XP = tuple(q for q in range(19) if DIRS[q][0] == 1)
XM = tuple(q for q in range(19) if DIRS[q][0] == -1)
YP = tuple(q for q in range(19) if DIRS[q][1] == 1)
YM = tuple(q for q in range(19) if DIRS[q][1] == -1)

R = 4096
NB = 256
NK = 256
ND = 128
CAP = 64
RIM = 32
MAIN = 4 * CAP
NU, NV = 64, 128
RB = 1024
EU, EV = 72, 256


def iota(shape, dim):
    return lax.broadcasted_iota(jnp.int32, shape, dim)


def halves(x):
    high = x.astype(BF16).astype(F32)
    return high, x - high


def combine(fields, direction):
    total = None
    for axis in range(3):
        if direction[axis] != 0:
            term = fields[axis] if direction[axis] == 1 else -fields[axis]
            total = term if total is None else total + term
    return total


def dot_t(a, b):
    return lax.dot_general(a, b, (((1,), (1,)), ((), ())), preferred_element_type=F32)


def dot(a, b):
    return lax.dot_general(a, b, (((1,), (0,)), ((), ())), preferred_element_type=F32)


MSTEPS = 2
MROWS = NB // MSTEPS
RSTEPS = R // RB


def block_hot(row):
    return jnp.where(iota((NB, RB), 0) == row, 1.0, 0.0).astype(BF16)


def rim_rows(own, node):
    u, v = node >> 7, node & 127
    ox, oy = own >> 5, own & 31
    su = jnp.where(u == NU - 1, 1, jnp.where(u <= 1, -1, 0))
    sv = jnp.where(v == NV - 1, 1, jnp.where(v <= 1, -1, 0))
    ox2, oy2 = (ox + su) & 3, (oy + sv) & 31
    dests = [
        jnp.where(su != 0, ox2 * 32 + oy, -1),
        jnp.where(sv != 0, ox * 32 + oy2, -1),
        jnp.where((su != 0) & (sv != 0), ox2 * 32 + oy2, -1),
    ]
    row = jnp.where(u == NU - 1, 0, u + 1) * EV
    codes = [
        row + v,
        jnp.where(v == NV - 1, 3, v + 4) * EV + u,
        row + jnp.where(v == NV - 1, EV - 1, v + NV),
    ]
    return dests, codes


def load_kernel(
    pop_ref, w_ref, blk_ref, own_all_ref, node_all_ref, own_ref, node_ref, send_ref, rank_ref,
    m_ref, mt_ref, tri_ref, carry_ref, dest_ref, code_ref, place_ref, over_ref,
):
    step = pl.program_id(0)

    @pl.when(step == 0)
    def _():
        before = (iota((256, 256), 0) < iota((256, 256), 1)).astype(F32)
        tri_ref[:, 0:256] = before.astype(BF16)
        tri_ref[:, 256:512] = jnp.ones((256, 256), BF16)
        carry_ref[...] = jnp.zeros_like(carry_ref)
        send_ref[...] = jnp.zeros_like(send_ref)
        over_ref[...] = jnp.zeros_like(over_ref)
        dests, codes = rim_rows(own_all_ref[...], node_all_ref[...])
        for i in range(3):
            dest_ref[i : i + 1, :] = dests[i]
            code_ref[i : i + 1, :] = codes[i].astype(F32)

    for part in range(MSTEPS):

        @pl.when(step == part)
        def _():
            def rows_of(i, _):
                rows = pl.ds(pl.multiple_of(i * 8, 8), 8)
                pops = [pop_ref[q, rows, :] for q in range(1, 19)]
                for axis in range(3):
                    total = None
                    for q in range(1, 19):
                        if DIRS[q][axis] != 0:
                            term = pops[q - 1] if DIRS[q][axis] == 1 else -pops[q - 1]
                            total = term if total is None else total + term
                    m_ref[axis, rows, :] = total
                return 0

            lax.fori_loop(0, MROWS // 8, rows_of, 0, unroll=2)
            for axis in range(3):
                turned = m_ref[axis].T
                high = turned.astype(BF16)
                at = slice(axis * NK, (axis + 1) * NK)
                mt_ref[at, part * MROWS : (part + 1) * MROWS] = high
                low = (turned - high.astype(F32)).astype(BF16)
                mt_ref[at, NB + part * MROWS : NB + (part + 1) * MROWS] = low
            for k in range(R // 256 // MSTEPS):
                start = (part * (R // 256 // MSTEPS) + k) * 256
                cols = slice(start, start + 256)
                device = iota((ND, 256), 0)
                hots = [device == own_all_ref[:, cols]] + [device == dest_ref[i : i + 1, cols] for i in range(3)]
                main = jnp.where(hots[0], 1.0, 0.0).astype(BF16)
                rims = jnp.where(hots[1] | hots[2] | hots[3], 1.0, 0.0).astype(BF16)
                counts = dot(jnp.concatenate([main, rims], axis=0), tri_ref[...])
                upto = counts[:, 0:256] + carry_ref[...]
                carry_ref[...] += counts[:, 256:512]
                rank_ref[:, cols] = jnp.sum(jnp.where(hots[0], upto[0:ND], 0.0), axis=0, keepdims=True).astype(
                    jnp.int32
                )
                for i in range(3):
                    place = jnp.sum(jnp.where(hots[i + 1], upto[ND : 2 * ND], 0.0), axis=0, keepdims=True)
                    over_ref[...] = jnp.maximum(over_ref[...], place)
                    place_ref[i : i + 1, cols] = jnp.where(place < RIM - 1, place, 2.0 * RIM).astype(jnp.int32)

    @pl.when(step >= MSTEPS)
    def _():
        here = pl.ds(pl.multiple_of((step - MSTEPS) * RB, RB), RB)
        w_t = w_ref[...].T
        hot = block_hot(blk_ref[...])
        picked = dot(mt_ref[...], jnp.concatenate([hot, hot], axis=0))
        values = [
            jnp.sum(picked[axis * NK : (axis + 1) * NK, :] * w_t, axis=0, keepdims=True) for axis in range(3)
        ]
        parts = [halves(value) for value in values]
        node = halves(node_ref[...].astype(F32))

        def placed(in_slot, code):
            both = [
                jnp.concatenate(
                    [jnp.where(in_slot, part[side], 0.0).astype(BF16) for part in parts + [code]], axis=0
                )
                for side in range(2)
            ]
            return jnp.concatenate(both, axis=1)

        named = jnp.where(iota((ND, RB), 0) == own_ref[...], 1.0, 0.0).astype(BF16)
        packed = placed(iota((CAP, RB), 0) == rank_ref[:, here], node)
        send_ref[:, 0:MAIN] += dot_t(jnp.concatenate([named, named], axis=1), packed)
        for i in range(3):
            named = jnp.where(iota((ND, RB), 0) == dest_ref[i : i + 1, here], 1.0, 0.0).astype(BF16)
            packed = placed(iota((RIM, RB), 0) == place_ref[i : i + 1, here], halves(code_ref[i : i + 1, here]))
            send_ref[:, MAIN : MAIN + 4 * RIM] += dot_t(jnp.concatenate([named, named], axis=1), packed)

    @pl.when(step == MSTEPS + RSTEPS - 1)
    def _():
        most = jnp.max(over_ref[...], axis=1, keepdims=True)
        flag = jnp.where(most >= RIM - 1, 1.0, 0.0)
        tail = send_ref[:, MAIN : MAIN + 4 * RIM]
        send_ref[:, MAIN : MAIN + 4 * RIM] = jnp.where(iota((ND, 4 * RIM), 1) == 4 * RIM - 1, flag, tail)


def loads_to_send(pops, weights, block_row, owner_row, node_row):
    def record(i):
        return jnp.maximum(i - MSTEPS, 0)

    row_spec = pl.BlockSpec((1, RB), lambda i: (0, record(i)))
    all_rows = pl.BlockSpec((1, R), lambda i: (0, 0))
    return pl.pallas_call(
        load_kernel,
        grid=(MSTEPS + RSTEPS,),
        in_specs=[
            pl.BlockSpec((19, MROWS, NK), lambda i: (0, jnp.minimum(i, MSTEPS - 1), 0)),
            pl.BlockSpec((RB, NK), lambda i: (record(i), 0)),
            row_spec,
            all_rows,
            all_rows,
            row_spec,
            row_spec,
        ],
        out_specs=[pl.BlockSpec((ND, MAIN + 4 * RIM), lambda i: (0, 0)), all_rows],
        out_shape=[
            jax.ShapeDtypeStruct((ND, MAIN + 4 * RIM), F32),
            jax.ShapeDtypeStruct((1, R), jnp.int32),
        ],
        scratch_shapes=[
            pltpu.VMEM((3, MROWS, NK), F32),
            pltpu.VMEM((3 * NK, 2 * NB), BF16),
            pltpu.VMEM((256, 512), BF16),
            pltpu.VMEM((2 * ND, 256), F32),
            pltpu.VMEM((8, R), jnp.int32),
            pltpu.VMEM((8, R), F32),
            pltpu.VMEM((8, R), jnp.int32),
            pltpu.VMEM((1, 256), F32),
        ],
        compiler_params=pltpu.CompilerParams(vmem_limit_bytes=VMEM_LIMIT),
        name="loads",
    )(pops, weights, block_row, owner_row, node_row, owner_row, node_row)


def collide_kernel(pop_ref, read_ref, xp_ref, xm_ref, yp_ref, ym_ref):
    def line(x, _):
        rows = pl.ds(pl.multiple_of(x * 8, 8), 8)
        pops = [pop_ref[q, rows, :] for q in range(19)]
        density = pops[0]
        for q in range(1, 19):
            density = density + pops[q]
        inverse = 1.0 / density
        velocity = []
        for axis in range(3):
            total = None
            for q in range(1, 19):
                if DIRS[q][axis] != 0:
                    term = pops[q] if DIRS[q][axis] == 1 else -pops[q]
                    total = term if total is None else total + term
            velocity.append(total * inverse)
        squared = velocity[0] * velocity[0] + velocity[1] * velocity[1] + velocity[2] * velocity[2]
        base = 1.0 - 1.5 * squared
        for q in range(19):
            cx, cy, cz = DIRS[q]
            along = combine(velocity, DIRS[q])
            bracket = base if along is None else base + along * (3.0 + 4.5 * along)
            relaxed = pops[q] - RATE * (pops[q] - (WEIGHTS[q] * density) * bracket)
            if cz != 0:
                relaxed = pltpu.roll(relaxed, 1 if cz == 1 else NK - 1, 1)
            if cy != 0:
                relaxed = pltpu.roll(relaxed, 1 if cy == 1 else 7, 0)
            if cy == 1:
                yp_ref[YP.index(q), pl.ds(lax.rem(x + cx + 32, 32), 1), :] = relaxed[0:1, :]
            if cy == -1:
                ym_ref[YM.index(q), pl.ds(lax.rem(x + cx + 32, 32), 1), :] = relaxed[7:8, :]
            to = pl.ds(pl.multiple_of(lax.rem(x + cx + 32, 32) * 8, 8), 8)
            read_ref[q, to, :] = relaxed
        return 0

    lax.fori_loop(0, 32, line, 0, unroll=4)
    for i, q in enumerate(XP):
        xp_ref[i] = read_ref[q, 0:8, :]
    for i, q in enumerate(XM):
        xm_ref[i] = read_ref[q, NB - 8 : NB, :]


def collide_and_run(pops):
    return pl.pallas_call(
        collide_kernel,
        out_shape=[
            jax.ShapeDtypeStruct((19, NB, NK), F32),
            jax.ShapeDtypeStruct((5, 8, NK), F32),
            jax.ShapeDtypeStruct((5, 8, NK), F32),
            jax.ShapeDtypeStruct((5, 32, NK), F32),
            jax.ShapeDtypeStruct((5, 32, NK), F32),
        ],
        compiler_params=pltpu.CompilerParams(vmem_limit_bytes=VMEM_LIMIT),
        name="collide",
    )(pops)


def node_rows(recv_t):
    node = recv_t[3 * CAP : MAIN, :].astype(jnp.int32)
    return node >> 7, node & 127


def force_kernel(recv_ref, f_ref, rim_ref, u_ref, v_ref, hl_ref, ru_ref, rv_ref, rhl_ref):
    recv_t = recv_ref[...].T
    u_ref[...], v_ref[...] = node_rows(recv_t)
    high, low = halves(recv_t[0 : 3 * CAP, :])
    hl_ref[0 : 3 * CAP, :] = high
    hl_ref[3 * CAP : 6 * CAP, :] = low
    code = recv_t[MAIN + 3 * RIM : MAIN + 4 * RIM, :].astype(jnp.int32)
    ru_ref[...] = code >> 8
    rv_ref[...] = code & 255
    high, low = halves(recv_t[MAIN : MAIN + 3 * RIM, :])
    rhl_ref[0 : 3 * RIM, :] = high
    rhl_ref[3 * RIM : 6 * RIM, :] = low

    def chunk_of(rows_ref, cols_ref, vals_ref, slots, height, width):
        u_of = iota((height, ND), 0)
        v_of = iota((width, ND), 0)

        def chunk(i, acc):
            at = pl.multiple_of(i * 8, 8)
            u8 = rows_ref[pl.ds(at, 8), :]
            v8 = cols_ref[pl.ds(at, 8), :]
            vals = [vals_ref[pl.ds(pl.multiple_of(part * slots + at, 8), 8), :] for part in range(6)]
            lhs, rhs = [], []
            for r in range(8):
                here = u_of == u8[r : r + 1, :]
                lhs.append(
                    jnp.concatenate([jnp.where(here, vals[part][r : r + 1, :], 0.0) for part in range(6)], axis=0)
                    .astype(BF16)
                )
                rhs.append(jnp.where(v_of == v8[r : r + 1, :], 1.0, 0.0).astype(BF16))
            return acc + dot_t(jnp.concatenate(lhs, axis=1), jnp.concatenate(rhs, axis=1))

        return lax.fori_loop(0, slots // 8, chunk, jnp.zeros((6 * height, width), F32))

    acc = chunk_of(u_ref, v_ref, hl_ref, CAP, NU, NV)
    for c in range(3):
        f_ref[c] = acc[c * NU : (c + 1) * NU, :] + acc[(3 + c) * NU : (4 + c) * NU, :]
    acc = chunk_of(ru_ref, rv_ref, rhl_ref, RIM, 8, EV)
    for c in range(3):
        rim_ref[c] = acc[c * 8 : (c + 1) * 8, :] + acc[(3 + c) * 8 : (4 + c) * 8, :]


def force_of(recv):
    return pl.pallas_call(
        force_kernel,
        out_shape=[jax.ShapeDtypeStruct((3, NU, NV), F32), jax.ShapeDtypeStruct((3, 8, EV), F32)],
        scratch_shapes=[
            pltpu.VMEM((CAP, ND), jnp.int32),
            pltpu.VMEM((CAP, ND), jnp.int32),
            pltpu.VMEM((6 * CAP, ND), F32),
            pltpu.VMEM((RIM, ND), jnp.int32),
            pltpu.VMEM((RIM, ND), jnp.int32),
            pltpu.VMEM((6 * RIM, ND), F32),
        ],
        compiler_params=pltpu.CompilerParams(vmem_limit_bytes=SMALL_LIMIT),
        name="force",
    )(recv)


def edge_kernel(mass_ref, mod_ref, live_ref, low_ref, high_ref):
    low_ref[...] = jnp.zeros_like(low_ref)
    high_ref[...] = jnp.zeros_like(high_ref)
    for i, field in enumerate([mass_ref[...], mod_ref[...], live_ref[...].astype(F32)]):
        low_ref[i : i + 1, :] = field[NU - 1 : NU, :]
        high_ref[2 * i : 2 * i + 2, :] = field[0:2, :]


def rim_tile(i, low_ref, high_ref):
    sub = iota((8, 128), 0)
    tile = jnp.where(sub == 0, high_ref[2 * i : 2 * i + 1, :], 0.0)
    tile = jnp.where(sub == 1, high_ref[2 * i + 1 : 2 * i + 2, :], tile)
    return jnp.where(sub == 7, low_ref[i : i + 1, :], tile)


def side_kernel(mass_ref, mod_ref, live_ref, low_ref, high_ref, to_low_ref, to_high_ref):
    to_low_ref[...] = jnp.zeros_like(to_low_ref)
    to_high_ref[...] = jnp.zeros_like(to_high_ref)
    for i, field in enumerate([mass_ref[...], mod_ref[...], live_ref[...].astype(F32)]):
        whole = jnp.concatenate(
            [field, rim_tile(i, low_ref, high_ref), jnp.zeros((128 - EU, 128), F32)], axis=0
        )
        turned = whole.T
        to_low_ref[i : i + 1, :] = turned[127:128, :]
        to_high_ref[2 * i : 2 * i + 2, :] = turned[0:2, :]


def edge_call(kernel, name, *args):
    return pl.pallas_call(
        kernel,
        out_shape=[jax.ShapeDtypeStruct((8, 128), F32), jax.ShapeDtypeStruct((8, 128), F32)],
        compiler_params=pltpu.CompilerParams(vmem_limit_bytes=SMALL_LIMIT),
        name=name,
    )(*args)


def shell_kernel(
    stiff_ref, f_ref, rim_ref, mass_ref, mod_ref, live_ref, ulow_ref, uhigh_ref, vlow_ref, vhigh_ref, recv_ref,
    y_ref, ret_ref,
    e_ref, c_ref, g_ref, y_ext_ref, fy_ref, u_ref, v_ref, rt_ref,
):
    sub = iota((8, 128), 0)

    def columns(near, far, before):
        first = jnp.where(sub == 0, near, 0.0)
        first = jnp.where(sub == 1, far, first)
        last = jnp.where(sub == 7, before, 0.0)
        return jnp.concatenate([first, jnp.zeros((112, 128), F32), last], axis=0).T

    for i, field in enumerate([mass_ref[...], mod_ref[...], live_ref[...].astype(F32)]):
        e_ref[3 + i, 0:NU, 0:NV] = field
        e_ref[3 + i, NU:EU, 0:NV] = rim_tile(i, ulow_ref, uhigh_ref)
        side = columns(
            vhigh_ref[2 * i : 2 * i + 1, :], vhigh_ref[2 * i + 1 : 2 * i + 2, :], vlow_ref[i : i + 1, :]
        )
        e_ref[3 + i, :, NV:EV] = side[0:EU, :]
    wide = iota((8, EV), 0)
    for i in range(3):
        e_ref[i, 0:NU, 0:NV] = f_ref[i]
        tile = jnp.where(wide == 0, rim_ref[i, 1:2, :], 0.0)
        tile = jnp.where(wide == 1, rim_ref[i, 2:3, :], tile)
        e_ref[i, NU:EU, :] = jnp.where(wide == 7, rim_ref[i, 0:1, :], tile)
        side = columns(rim_ref[i, 4:5, 0:128], rim_ref[i, 5:6, 0:128], rim_ref[i, 3:4, 0:128])
        e_ref[i, 0:NU, NV:EV] = side[0:NU, :]

    def up(x):
        return pltpu.roll(x, EU - 1, 0)

    def right(x):
        return pltpu.roll(x, EV - 1, 1)

    def down(x):
        return pltpu.roll(x, 1, 0)

    def left(x):
        return pltpu.roll(x, 1, 1)

    mod = e_ref[4]
    mod = mod + up(mod)
    e_ref[5] = e_ref[5] * (mod + right(mod)) * 0.25
    for c in range(3):
        field = e_ref[c]
        moved = up(field)
        c_ref[c] = field
        c_ref[3 + c] = moved
        c_ref[6 + c] = right(field)
        c_ref[9 + c] = right(moved)

    def cells(t, _):
        rows = pl.ds(pl.multiple_of(t * 8, 8), 8)
        corner = [c_ref[k, rows, :] for k in range(12)]
        scale = e_ref[5, rows, :]
        for k in range(12):
            total = stiff_ref[k, 0] * corner[0]
            for m in range(1, 12):
                total = total + stiff_ref[k, m] * corner[m]
            g_ref[k, rows, :] = scale * total
        return 0

    lax.fori_loop(0, EU // 8, cells, 0)
    mass = e_ref[3]
    for c in range(3):
        spread = g_ref[c] + down(g_ref[3 + c])
        beside = g_ref[6 + c] + down(g_ref[9 + c])
        y_ext_ref[c] = mass * e_ref[c] + spread + left(beside)
        y_ref[c] = y_ext_ref[c, 0:NU, 0:NV]
    for c in range(3):
        field = y_ext_ref[c]
        moved = up(field)
        c_ref[c] = field
        c_ref[3 + c] = moved
        c_ref[6 + c] = right(field)
        c_ref[9 + c] = right(moved)

    def energy(t, sums):
        rows = pl.ds(pl.multiple_of(t * 8, 8), 8)
        corner = [c_ref[k, rows, 0:NV] for k in range(12)]
        total = None
        for k in range(12):
            inner = stiff_ref[k, 0] * corner[0]
            for m in range(1, 12):
                inner = inner + stiff_ref[k, m] * corner[m]
            total = corner[k] * inner if total is None else total + corner[k] * inner
        m3 = e_ref[5, rows, 0:NV] * total
        m0, m1, m2 = None, None, None
        for c in range(3):
            f = e_ref[c, rows, 0:NV]
            y = corner[c]
            m0 = f * f if m0 is None else m0 + f * f
            m1 = f * y if m1 is None else m1 + f * y
            m2 = y * y if m2 is None else m2 + y * y
        m3 = m3 + e_ref[3, rows, 0:NV] * m2
        return tuple(s + m for s, m in zip(sums, (m0, m1, m2, m3)))

    zero = jnp.zeros((8, NV), F32)
    sums = lax.fori_loop(0, NU // 8, energy, (zero, zero, zero, zero))
    lane = iota((1, 128), 1)
    moments = jnp.zeros((1, 128), F32)
    for i in range(4):
        whole = jnp.sum(jnp.sum(sums[i], axis=0, keepdims=True), axis=1, keepdims=True)
        moments = jnp.where(lane == i, whole, moments)
    over = jnp.max(recv_ref[:, MAIN + 4 * RIM - 1 : MAIN + 4 * RIM], axis=0, keepdims=True)
    moments = jnp.where(lane == 4, over, moments)

    for c in range(3):
        for part, field in ((c, f_ref[c]), (3 + c, y_ref[c])):
            high = field.astype(BF16)
            fy_ref[part * NU : (part + 1) * NU, 0:NV] = high
            fy_ref[part * NU : (part + 1) * NU, NV : 2 * NV] = (field - high.astype(F32)).astype(BF16)
    u_ref[...], v_ref[...] = node_rows(recv_ref[:, 0:MAIN].T)
    u_of = iota((NU, ND), 0)
    v_of = iota((NV, ND), 0)

    def chunk(i, _):
        at = pl.multiple_of(i * 8, 8)
        u8 = u_ref[pl.ds(at, 8), :]
        v8 = v_ref[pl.ds(at, 8), :]
        rhs = jnp.concatenate(
            [jnp.where(v_of == v8[r : r + 1, :], 1.0, 0.0).astype(BF16) for r in range(8)], axis=1
        )
        picked = dot(fy_ref[...], jnp.concatenate([rhs, rhs], axis=0))
        tiles = [jnp.zeros((8, ND), F32) for _ in range(6)]
        for r in range(8):
            here = u_of == u8[r : r + 1, :]
            for part in range(6):
                block = picked[part * NU : (part + 1) * NU, r * ND : (r + 1) * ND]
                row = jnp.sum(jnp.where(here, block, 0.0), axis=0, keepdims=True)
                tiles[part] = jnp.where(sub == r, row, tiles[part])
        for part in range(6):
            rt_ref[pl.ds(pl.multiple_of(part * CAP + at, 8), 8), :] = tiles[part]
        return 0

    lax.fori_loop(0, CAP // 8, chunk, 0)
    ret_ref[:, 0 : 6 * CAP] = rt_ref[...].T
    ret_ref[:, 6 * CAP : 8 * CAP] = jnp.broadcast_to(moments, (ND, 128))


def shell_of(stiff, force, rim, mass, modulus, live, rims, recv):
    vmem = pl.BlockSpec(memory_space=pltpu.VMEM)
    return pl.pallas_call(
        shell_kernel,
        in_specs=[pl.BlockSpec(memory_space=pltpu.SMEM)] + [vmem] * 10,
        out_specs=[vmem, vmem],
        out_shape=[
            jax.ShapeDtypeStruct((3, NU, NV), F32),
            jax.ShapeDtypeStruct((ND, 8 * CAP), F32),
        ],
        scratch_shapes=[
            pltpu.VMEM((6, EU, EV), F32),
            pltpu.VMEM((12, EU, EV), F32),
            pltpu.VMEM((12, EU, EV), F32),
            pltpu.VMEM((3, EU, EV), F32),
            pltpu.VMEM((6 * NU, 2 * NV), BF16),
            pltpu.VMEM((CAP, ND), jnp.int32),
            pltpu.VMEM((CAP, ND), jnp.int32),
            pltpu.VMEM((6 * CAP, ND), F32),
        ],
        compiler_params=pltpu.CompilerParams(vmem_limit_bytes=SMALL_LIMIT),
        name="shell",
    )(stiff, force, rim, mass, modulus, live, *rims, recv)


def scalar_kernel(part_ref, pq_ref, sound_ref):
    row = jnp.sum(part_ref[...], axis=0, keepdims=True)
    lane = iota((1, 128), 1)
    m0, m1, m2, m3, over = [
        jnp.sum(jnp.where(lane == i, row, 0.0), axis=1, keepdims=True) for i in range(5)
    ]
    first = m0 / m1
    left_over = first * first * m2 - m0
    ratio = left_over / m0
    gain = 1.0 + ratio
    curve = gain * gain * m1 - 2.0 * gain * first * m2 + first * first * m3
    second = left_over / curve
    sound = (
        (over == 0.0)
        & (left_over > 1e-3 * m0)
        & (curve > 1e-2 * gain * gain * m1)
        & (curve < 1e30)
        & (m1 > 1e-30)
        & (m0 > 1e-30)
    )
    pq_ref[0] = (first + second * gain)[0, 0]
    pq_ref[1] = -(first * second)[0, 0]
    sound_ref[0] = jnp.where(sound, 1, 0)[0, 0]


def scalars_of(back):
    smem = pl.BlockSpec(memory_space=pltpu.SMEM)
    return pl.pallas_call(
        scalar_kernel,
        grid=(1,),
        in_specs=[pl.BlockSpec((ND, 128), lambda i: (0, 3))],
        out_specs=[smem, smem],
        out_shape=[jax.ShapeDtypeStruct((2,), F32), jax.ShapeDtypeStruct((1,), jnp.int32)],
        name="scalars",
    )(back)


XS = 4
OSTEPS = 32 // XS


def next_kernel(
    pq_ref, back_ref, w_ref, blk_ref, own_ref, rank_ref, f_ref, y_ref, read_ref, xp_ref, xm_ref, yp_ref, ym_ref,
    next_ref, disp_ref,
    x_ref, turned_ref, force_ref,
):
    step = pl.program_id(0)

    @pl.when(step == 0)
    def _():
        p = pq_ref[0]
        q = pq_ref[1]
        back = p * back_ref[:, 0 : 3 * CAP] + q * back_ref[:, 3 * CAP : 6 * CAP]
        turned = back.T * COUPLING
        high = turned.astype(BF16)
        x_ref[:, 0:ND] = high
        x_ref[:, ND : 2 * ND] = (turned - high.astype(F32)).astype(BF16)
        disp_ref[...] = p * f_ref[...] + q * y_ref[...]
        turned_ref[...] = jnp.zeros_like(turned_ref)

    @pl.when(step < RSTEPS)
    def _():
        named = jnp.where(iota((ND, RB), 0) == own_ref[...], 1.0, 0.0).astype(BF16)
        picked = dot(x_ref[...], jnp.concatenate([named, named], axis=0))
        in_slot = iota((CAP, RB), 0) == rank_ref[...]
        w_t = w_ref[...].T
        highs, lows = [], []
        for c in range(3):
            moved = jnp.sum(
                jnp.where(in_slot, picked[c * CAP : (c + 1) * CAP, :], 0.0), axis=0, keepdims=True
            )
            part = w_t * moved
            high = part.astype(BF16)
            highs.append(high)
            lows.append((part - high.astype(F32)).astype(BF16))
        hot = block_hot(blk_ref[...])
        parts = jnp.concatenate([jnp.concatenate(highs, axis=0), jnp.concatenate(lows, axis=0)], axis=1)
        turned_ref[...] += dot_t(parts, jnp.concatenate([hot, hot], axis=1))

    @pl.when(step == RSTEPS)
    def _():
        for c in range(3):
            force_ref[c * NB : (c + 1) * NB, :] = turned_ref[c * NK : (c + 1) * NK, :].T

    @pl.when(step >= RSTEPS)
    def _():
        slab = step - RSTEPS
        sub = iota((8, NK), 0)
        for xx in range(XS):
            x = slab * XS + xx
            forcing = [
                force_ref[pl.ds(pl.multiple_of(c * NB + x * 8, 8), 8), :] for c in range(3)
            ]
            for q in range(19):
                cx, cy, _ = DIRS[q]
                value = read_ref[q, xx * 8 : (xx + 1) * 8, :]
                if cx == 1 and xx == 0:
                    value = jnp.where(x == 0, xp_ref[XP.index(q)], value)
                if cx == -1 and xx == XS - 1:
                    value = jnp.where(x == 31, xm_ref[XM.index(q)], value)
                if cy == 1:
                    value = jnp.where(sub == 0, yp_ref[YP.index(q), pl.ds(x, 1), :], value)
                if cy == -1:
                    value = jnp.where(sub == 7, ym_ref[YM.index(q), pl.ds(x, 1), :], value)
                along = combine(forcing, DIRS[q])
                if along is not None:
                    value = value + (3.0 * WEIGHTS[q]) * along
                next_ref[q, xx * 8 : (xx + 1) * 8, :] = value


def outputs_of(pq, back, weights, block_row, owner_row, rank_row, force, image, read, xp, xm, yp, ym):
    def record(i):
        return jnp.minimum(i, RSTEPS - 1)

    def slab(i):
        return jnp.maximum(i - RSTEPS, 0)

    row_spec = pl.BlockSpec((1, RB), lambda i: (0, record(i)))
    patch = pl.BlockSpec((3, NU, NV), lambda i: (0, 0, 0))
    lines = pl.BlockSpec((19, XS * 8, NK), lambda i: (0, slab(i), 0))
    x_face = pl.BlockSpec((5, 8, NK), lambda i: (0, 0, 0))
    y_face = pl.BlockSpec((5, 32, NK), lambda i: (0, 0, 0))
    return pl.pallas_call(
        next_kernel,
        grid=(RSTEPS + OSTEPS,),
        in_specs=[
            pl.BlockSpec(memory_space=pltpu.SMEM),
            pl.BlockSpec((ND, 8 * CAP), lambda i: (0, 0)),
            pl.BlockSpec((RB, NK), lambda i: (record(i), 0)),
            row_spec,
            row_spec,
            row_spec,
            patch,
            patch,
            lines,
            x_face,
            x_face,
            y_face,
            y_face,
        ],
        out_specs=[lines, patch],
        out_shape=[
            jax.ShapeDtypeStruct((19, NB, NK), F32),
            jax.ShapeDtypeStruct((3, NU, NV), F32),
        ],
        scratch_shapes=[
            pltpu.VMEM((3 * CAP, 2 * ND), BF16),
            pltpu.VMEM((3 * NK, NB), F32),
            pltpu.VMEM((3 * NB, NK), F32),
        ],
        compiler_params=pltpu.CompilerParams(vmem_limit_bytes=VMEM_LIMIT),
        name="outputs",
    )(pq, back, weights, block_row, owner_row, rank_row, force, image, read, xp, xm, yp, ym)


def pass_on(x, axis, shift):
    count = lax.axis_size(axis)
    return lax.ppermute(x, axis, [(i, (i + shift) % count) for i in range(count)])


def padded(field):
    for axis, dim in (("gx", 1), ("gy", 2)):
        size = field.shape[dim]
        head = lax.slice_in_dim(field, 0, 1, axis=dim)
        tail = lax.slice_in_dim(field, size - 1, size, axis=dim)
        field = jnp.concatenate([pass_on(tail, axis, 1), field, pass_on(head, axis, -1)], axis=dim)
    return field


def operate(field, mass, modulus, live, stiff):
    static = padded(jnp.stack([modulus, live.astype(F32)]))
    wide = padded(field)

    def corners(a):
        return a[..., :-1, :-1], a[..., 1:, :-1], a[..., :-1, 1:], a[..., 1:, 1:]

    c0, c1, c2, c3 = corners(static[0])
    scale = static[1, :-1, :-1] * (c0 + c1 + c2 + c3) * 0.25
    vector = jnp.concatenate(corners(wide), axis=0)
    result = scale[None] * jnp.einsum("kl,lab->kab", stiff, vector, precision=lax.Precision.HIGHEST)
    return (
        mass[None] * field
        + result[0:3, 1:, 1:]
        + result[3:6, :-1, 1:]
        + result[6:9, 1:, :-1]
        + result[9:12, :-1, :-1]
    )


def rim_of(force):
    before = pass_on(force[:, NU - 1 : NU, :], "gx", 1)
    after = pass_on(force[:, 0:2, :], "gx", -1)
    tall = jnp.concatenate([force, after, before], axis=1)
    left = pass_on(tall[:, :, NV - 1 : NV], "gy", 1)
    right = pass_on(tall[:, :, 0:2], "gy", -1)
    gap = jnp.zeros((3, EV - NV - 3), F32)
    rows = [
        jnp.concatenate([tall[:, r], right[:, r], gap, left[:, r]], axis=1) for r in (NU + 2, NU, NU + 1)
    ]
    beside = [
        jnp.concatenate([column[:, 0:NU], jnp.zeros((3, EV - NU), F32)], axis=1)
        for column in (left[:, :, 0], right[:, :, 0], right[:, :, 1])
    ]
    empty = jnp.zeros((3, EV), F32)
    return jnp.stack(rows + beside + [empty, empty], axis=1)


def exchange(x):
    return lax.all_to_all(x, ALL, 0, 0, tiled=True)


def per_device(populations, mass, modulus, live, stiff, rec_block, rec_owner, rec_node, weights):
    pops = populations.reshape(19, NB, NK)
    block_row = rec_block.reshape(1, R)
    owner_row = rec_owner.reshape(1, R)
    node_row = rec_node.reshape(1, R)

    low, high = edge_call(edge_kernel, "edges", mass, modulus, live)
    ulow = pass_on(low, "gx", 1)
    uhigh = pass_on(high, "gx", -1)
    send, rank_row = loads_to_send(pops, weights, block_row, owner_row, node_row)
    send, ulow, uhigh, pops = lax.optimization_barrier((send, ulow, uhigh, pops))
    recv = exchange(send)
    low, high = edge_call(side_kernel, "sides", mass, modulus, live, ulow, uhigh)
    rims = (ulow, uhigh, pass_on(low, "gy", 1), pass_on(high, "gy", -1))

    read, xp, xm, yp, ym = collide_and_run(pops)
    xp = pass_on(xp, "gx", 1)
    xm = pass_on(xm, "gx", -1)

    force, rim = force_of(recv)
    image, ret = shell_of(stiff, force, rim, mass, modulus, live, rims, recv)
    ret, xp, xm = lax.optimization_barrier((ret, xp, xm))
    back = exchange(ret)
    yp = yp.at[YP.index(7), 0].set(xp[XP.index(7), 0]).at[YP.index(10), 31].set(xm[XM.index(10), 0])
    ym = ym.at[YM.index(9), 0].set(xp[XP.index(9), 7]).at[YM.index(8), 31].set(xm[XM.index(8), 7])
    yp = pass_on(yp, "gy", 1)
    ym = pass_on(ym, "gy", -1)

    back, yp, ym = lax.optimization_barrier((back, yp, ym))
    pq, sound = scalars_of(back)

    def quick(operands):
        return operands[0:3]

    def careful(operands):
        _, _, _, force, mass, modulus, live, stiff, rims, recv = operands
        image, ret = shell_of(stiff, force, rim_of(force), mass, modulus, live, rims, recv)
        back = exchange(ret)
        start = lax.psum(jnp.sum(force * force), ALL)
        first = start / lax.psum(jnp.sum(force * image), ALL)
        residual = force - first * image
        norm = lax.psum(jnp.sum(residual * residual), ALL)
        ratio = norm / start
        direction = residual + ratio * force
        along = operate(direction, mass, modulus, live, stiff)
        second = norm / lax.psum(jnp.sum(direction * along), ALL)
        return jnp.stack([first + second * (1.0 + ratio), -(first * second)]), image, back

    pq, image, back = lax.cond(
        sound[0] == 1, quick, careful, (pq, image, back, force, mass, modulus, live, stiff, rims, recv)
    )

    populations_next, displacement = outputs_of(
        pq, back, weights, block_row, owner_row, rank_row, force, image, read, xp, xm, yp, ym
    )
    return populations_next.reshape(19, 32, 8, NK), displacement


def solution(mesh):
    return jax.shard_map(
        per_device,
        mesh=mesh,
        in_specs=(
            P(None, "gx", "gy", None),
            P("gx", "gy"),
            P("gx", "gy"),
            P("gx", "gy"),
            P(),
            P(ALL),
            P(ALL, None),
            P(ALL),
            P(ALL, None),
        ),
        out_specs=(P(None, "gx", "gy", None), P(None, "gx", "gy")),
        check_vma=False,
    )
```

```python
import jax
import jax.numpy as jnp
from jax import lax
from jax.experimental import pallas as pl
from jax.experimental.pallas import tpu as pltpu
from jax.sharding import PartitionSpec as P

F32 = jnp.float32
BF16 = jnp.bfloat16
ALL = ("gx", "gy")
VMEM_LIMIT = 60 * 1024 * 1024
SMALL_LIMIT = 16 * 1024 * 1024

DIRS = (
    (0, 0, 0),
    (1, 0, 0),
    (-1, 0, 0),
    (0, 1, 0),
    (0, -1, 0),
    (0, 0, 1),
    (0, 0, -1),
    (1, 1, 0),
    (-1, -1, 0),
    (1, -1, 0),
    (-1, 1, 0),
    (1, 0, 1),
    (-1, 0, -1),
    (1, 0, -1),
    (-1, 0, 1),
    (0, 1, 1),
    (0, -1, -1),
    (0, 1, -1),
    (0, -1, 1),
)
WEIGHTS = (1.0 / 3.0,) + (1.0 / 18.0,) * 6 + (1.0 / 36.0,) * 12
RATE = 1.25
COUPLING = 0.1
XP = tuple(q for q in range(19) if DIRS[q][0] == 1)
XM = tuple(q for q in range(19) if DIRS[q][0] == -1)
YP = tuple(q for q in range(19) if DIRS[q][1] == 1)
YM = tuple(q for q in range(19) if DIRS[q][1] == -1)

R = 4096
NB = 256
NK = 256
ND = 128
CAP = 64
RIM = 32
MAIN = 4 * CAP
NU, NV = 64, 128
RB = 1024
EU, EV = 72, 256


def iota(shape, dim):
    return lax.broadcasted_iota(jnp.int32, shape, dim)


def halves(x):
    high = x.astype(BF16).astype(F32)
    return high, x - high


def combine(fields, direction):
    total = None
    for axis in range(3):
        if direction[axis] != 0:
            term = fields[axis] if direction[axis] == 1 else -fields[axis]
            total = term if total is None else total + term
    return total


def dot_t(a, b):
    return lax.dot_general(a, b, (((1,), (1,)), ((), ())), preferred_element_type=F32)


def dot(a, b):
    return lax.dot_general(a, b, (((1,), (0,)), ((), ())), preferred_element_type=F32)


CHUNKS = 4
CROWS = NB // CHUNKS
RSTEPS = R // RB


def match(count, row):
    lanes = row.shape[1]
    column = iota((count, 128), 0).astype(F32).astype(BF16)
    wanted = jnp.broadcast_to(row.astype(F32).astype(BF16), (count, lanes))
    return jnp.concatenate([column] * (lanes // 128), axis=1) == wanted


def hot(count, row):
    shape = (count, row.shape[1])
    return jnp.where(match(count, row), jnp.ones(shape, BF16), jnp.zeros(shape, BF16))


def pick(mask, row):
    return jnp.where(mask, jnp.broadcast_to(row, mask.shape), jnp.zeros(mask.shape, BF16))


def rim_rows(own, node):
    u, v = node >> 7, node & 127
    ox, oy = own >> 5, own & 31
    su = jnp.where(u == NU - 1, 1, jnp.where(u <= 1, -1, 0))
    sv = jnp.where(v == NV - 1, 1, jnp.where(v <= 1, -1, 0))
    ox2, oy2 = (ox + su) & 3, (oy + sv) & 31
    dests = [
        jnp.where(su != 0, ox2 * 32 + oy, -1),
        jnp.where(sv != 0, ox * 32 + oy2, -1),
        jnp.where((su != 0) & (sv != 0), ox2 * 32 + oy2, -1),
    ]
    row = jnp.where(u == NU - 1, 0, u + 1) * EV
    codes = [
        row + v,
        jnp.where(v == NV - 1, 3, v + 4) * EV + u,
        row + jnp.where(v == NV - 1, EV - 1, v + NV),
    ]
    return dests, codes


def load_kernel(
    pop_hbm, w_ref, blk_ref, own_all_ref, node_all_ref, own_ref, node_ref, send_ref, rank_ref, wt_ref,
    pop_ref, sems, m_ref, mt_ref, tri_ref, carry_ref, dest_ref, code_ref, place_ref, over_ref, main_ref, rims_ref,
):
    step = pl.program_id(0)

    def fetch(part):
        rows = pl.ds(part * CROWS, CROWS)
        return pltpu.make_async_copy(pop_hbm.at[:, rows, :], pop_ref.at[:, rows, :], sems.at[part])

    @pl.when(step == 0)
    def _():
        for part in range(CHUNKS):
            fetch(part).start()
        before = (iota((256, 256), 0) < iota((256, 256), 1)).astype(F32)
        tri_ref[:, 0:256] = before.astype(BF16)
        tri_ref[:, 256:512] = jnp.ones((256, 256), BF16)
        carry_ref[...] = jnp.zeros_like(carry_ref)
        main_ref[...] = jnp.zeros_like(main_ref)
        rims_ref[...] = jnp.zeros_like(rims_ref)
        over_ref[...] = jnp.zeros_like(over_ref)
        dests, codes = rim_rows(own_all_ref[...], node_all_ref[...])
        for i in range(3):
            dest_ref[i : i + 1, :] = dests[i]
            code_ref[i : i + 1, :] = codes[i].astype(F32)
        for k in range(R // 256):
            cols = slice(k * 256, (k + 1) * 256)
            device = iota((ND, 256), 0)
            hots = [device == own_all_ref[:, cols]] + [device == dest_ref[i : i + 1, cols] for i in range(3)]
            main = jnp.where(hots[0], 1.0, 0.0).astype(BF16)
            rims = jnp.where(hots[1] | hots[2] | hots[3], 1.0, 0.0).astype(BF16)
            counts = dot(jnp.concatenate([main, rims], axis=0), tri_ref[...])
            upto = counts[:, 0:256] + carry_ref[...]
            carry_ref[...] += counts[:, 256:512]
            rank = jnp.sum(jnp.where(hots[0], upto[0:ND], 0.0), axis=0, keepdims=True)
            rank_ref[:, cols] = rank.astype(jnp.int32)
            for i in range(3):
                place = jnp.sum(jnp.where(hots[i + 1], upto[ND : 2 * ND], 0.0), axis=0, keepdims=True)
                over_ref[...] = jnp.maximum(over_ref[...], place)
                place_ref[i : i + 1, cols] = jnp.where(place < RIM - 1, place, 2.0 * RIM).astype(jnp.int32)

        def rows_of(i, _):
            rows = pl.ds(pl.multiple_of(i * 8, 8), 8)
            pops = [pop_ref[q, rows, :] for q in range(1, 19)]
            for axis in range(3):
                total = None
                for q in range(1, 19):
                    if DIRS[q][axis] != 0:
                        term = pops[q - 1] if DIRS[q][axis] == 1 else -pops[q - 1]
                        total = term if total is None else total + term
                m_ref[axis, rows, :] = total
            return 0

        for part in range(CHUNKS):
            fetch(part).wait()
            lax.fori_loop(part * CROWS // 8, (part + 1) * CROWS // 8, rows_of, 0, unroll=2)
        for axis in range(3):
            turned = m_ref[axis].T
            high = turned.astype(BF16)
            at = slice(axis * NK, (axis + 1) * NK)
            mt_ref[at, 0:NB] = high
            mt_ref[at, NB : 2 * NB] = (turned - high.astype(F32)).astype(BF16)

    @pl.when(step >= 1)
    def _():
        here = pl.ds(pl.multiple_of((step - 1) * RB, RB), RB)
        w_t = w_ref[...].T
        in_block = hot(NB, blk_ref[...])
        picked = dot(mt_ref[...], jnp.concatenate([in_block, in_block], axis=0))
        values = [
            jnp.sum(picked[axis * NK : (axis + 1) * NK, :] * w_t, axis=0, keepdims=True) for axis in range(3)
        ]

        def sides(value):
            return [side.astype(BF16) for side in halves(value)]

        parts = [sides(value) for value in values]

        def placed(count, slot, code):
            mask = match(count, slot)
            both = [pick(mask, part[side]) for side in range(2) for part in parts + [sides(code)]]
            return jnp.concatenate(both, axis=0)

        packed = placed(CAP, rank_ref[:, here], node_ref[...].astype(F32))
        main_ref[...] += dot_t(packed, hot(ND, own_ref[...]))
        packed = [placed(RIM, place_ref[i : i + 1, here], code_ref[i : i + 1, here]) for i in range(3)]
        named = [hot(ND, dest_ref[i : i + 1, here]) for i in range(3)]
        rims_ref[...] += dot_t(jnp.concatenate(packed, axis=1), jnp.concatenate(named, axis=1))
        wt_ref[...] = w_t

    @pl.when(step == RSTEPS)
    def _():
        most = jnp.max(over_ref[...], axis=1, keepdims=True)
        flag = jnp.where(most >= RIM - 1, 1.0, 0.0)
        send_ref[:, 0, 0:MAIN] = (main_ref[0:MAIN, :] + main_ref[MAIN : 2 * MAIN, :]).T
        tail = (rims_ref[0 : 4 * RIM, :] + rims_ref[4 * RIM : 8 * RIM, :]).T
        send_ref[:, 0, MAIN : MAIN + 4 * RIM] = jnp.where(iota((ND, 4 * RIM), 1) == 4 * RIM - 1, flag, tail)


def loads_to_send(pops, weights, block_row, owner_row, node_row):
    def record(i):
        return jnp.maximum(i - 1, 0)

    row_spec = pl.BlockSpec((1, RB), lambda i: (0, record(i)))
    all_rows = pl.BlockSpec((1, R), lambda i: (0, 0))
    return pl.pallas_call(
        load_kernel,
        grid=(1 + RSTEPS,),
        in_specs=[
            pl.BlockSpec(memory_space=pl.ANY),
            pl.BlockSpec((RB, NK), lambda i: (record(i), 0)),
            row_spec,
            all_rows,
            all_rows,
            row_spec,
            row_spec,
        ],
        out_specs=[
            pl.BlockSpec((ND, 1, MAIN + 4 * RIM), lambda i: (0, 0, 0)),
            all_rows,
            pl.BlockSpec((NK, RB), lambda i: (0, record(i))),
        ],
        out_shape=[
            jax.ShapeDtypeStruct((ND, 1, MAIN + 4 * RIM), F32),
            jax.ShapeDtypeStruct((1, R), jnp.int32),
            jax.ShapeDtypeStruct((NK, R), F32),
        ],
        scratch_shapes=[
            pltpu.VMEM((19, NB, NK), F32),
            pltpu.SemaphoreType.DMA((CHUNKS,)),
            pltpu.VMEM((3, NB, NK), F32),
            pltpu.VMEM((3 * NK, 2 * NB), BF16),
            pltpu.VMEM((256, 512), BF16),
            pltpu.VMEM((2 * ND, 256), F32),
            pltpu.VMEM((8, R), jnp.int32),
            pltpu.VMEM((8, R), F32),
            pltpu.VMEM((8, R), jnp.int32),
            pltpu.VMEM((1, 256), F32),
            pltpu.VMEM((2 * MAIN, ND), F32),
            pltpu.VMEM((8 * RIM, ND), F32),
        ],
        compiler_params=pltpu.CompilerParams(vmem_limit_bytes=VMEM_LIMIT),
        name="loads",
    )(pops, weights, block_row, owner_row, node_row, owner_row, node_row)


def collide_kernel(pop_ref, read_ref, xp_ref, xm_ref, yp_ref, ym_ref):
    def line(x, _):
        rows = pl.ds(pl.multiple_of(x * 8, 8), 8)
        pops = [pop_ref[q, rows, :] for q in range(19)]
        density = pops[0]
        for q in range(1, 19):
            density = density + pops[q]
        inverse = 1.0 / density
        velocity = []
        for axis in range(3):
            total = None
            for q in range(1, 19):
                if DIRS[q][axis] != 0:
                    term = pops[q] if DIRS[q][axis] == 1 else -pops[q]
                    total = term if total is None else total + term
            velocity.append(total * inverse)
        squared = velocity[0] * velocity[0] + velocity[1] * velocity[1] + velocity[2] * velocity[2]
        base = 1.0 - 1.5 * squared
        for q in range(19):
            cx, cy, cz = DIRS[q]
            along = combine(velocity, DIRS[q])
            bracket = base if along is None else base + along * (3.0 + 4.5 * along)
            relaxed = pops[q] - RATE * (pops[q] - (WEIGHTS[q] * density) * bracket)
            if cz != 0:
                relaxed = pltpu.roll(relaxed, 1 if cz == 1 else NK - 1, 1)
            if cy != 0:
                relaxed = pltpu.roll(relaxed, 1 if cy == 1 else 7, 0)
            if cy == 1:
                yp_ref[YP.index(q), pl.ds(lax.rem(x + cx + 32, 32), 1), :] = relaxed[0:1, :]
            if cy == -1:
                ym_ref[YM.index(q), pl.ds(lax.rem(x + cx + 32, 32), 1), :] = relaxed[7:8, :]
            to = pl.ds(pl.multiple_of(lax.rem(x + cx + 32, 32) * 8, 8), 8)
            read_ref[q, to, :] = relaxed
        return 0

    lax.fori_loop(0, 32, line, 0, unroll=4)
    for i, q in enumerate(XP):
        xp_ref[i] = read_ref[q, 0:8, :]
    for i, q in enumerate(XM):
        xm_ref[i] = read_ref[q, NB - 8 : NB, :]


def collide_and_run(pops):
    return pl.pallas_call(
        collide_kernel,
        out_shape=[
            jax.ShapeDtypeStruct((19, NB, NK), F32),
            jax.ShapeDtypeStruct((5, 8, NK), F32),
            jax.ShapeDtypeStruct((5, 8, NK), F32),
            jax.ShapeDtypeStruct((5, 32, NK), F32),
            jax.ShapeDtypeStruct((5, 32, NK), F32),
        ],
        compiler_params=pltpu.CompilerParams(vmem_limit_bytes=VMEM_LIMIT),
        name="collide",
    )(pops)


def node_rows(recv_t):
    node = recv_t[3 * CAP : MAIN, :].astype(jnp.int32)
    return node >> 7, node & 127


def force_kernel(recv_ref, f_ref, rim_ref, u_ref, v_ref, hl_ref, ru_ref, rv_ref, rhl_ref):
    recv_t = recv_ref[:, 0, :].T
    u_ref[...], v_ref[...] = node_rows(recv_t)
    high, low = halves(recv_t[0 : 3 * CAP, :])
    hl_ref[0 : 3 * CAP, :] = high
    hl_ref[3 * CAP : 6 * CAP, :] = low
    code = recv_t[MAIN + 3 * RIM : MAIN + 4 * RIM, :].astype(jnp.int32)
    ru_ref[...] = code >> 8
    rv_ref[...] = code & 255
    high, low = halves(recv_t[MAIN : MAIN + 3 * RIM, :])
    rhl_ref[0 : 3 * RIM, :] = high
    rhl_ref[3 * RIM : 6 * RIM, :] = low

    def chunk_of(rows_ref, cols_ref, vals_ref, slots, height, width):
        u_of = iota((height, ND), 0)
        v_of = iota((width, ND), 0)

        def chunk(i, acc):
            at = pl.multiple_of(i * 8, 8)
            u8 = rows_ref[pl.ds(at, 8), :]
            v8 = cols_ref[pl.ds(at, 8), :]
            vals = [vals_ref[pl.ds(pl.multiple_of(part * slots + at, 8), 8), :] for part in range(6)]
            lhs, rhs = [], []
            for r in range(8):
                here = u_of == u8[r : r + 1, :]
                lhs.append(
                    jnp.concatenate([jnp.where(here, vals[part][r : r + 1, :], 0.0) for part in range(6)], axis=0)
                    .astype(BF16)
                )
                rhs.append(jnp.where(v_of == v8[r : r + 1, :], 1.0, 0.0).astype(BF16))
            return acc + dot_t(jnp.concatenate(lhs, axis=1), jnp.concatenate(rhs, axis=1))

        return lax.fori_loop(0, slots // 8, chunk, jnp.zeros((6 * height, width), F32))

    acc = chunk_of(u_ref, v_ref, hl_ref, CAP, NU, NV)
    for c in range(3):
        f_ref[c] = acc[c * NU : (c + 1) * NU, :] + acc[(3 + c) * NU : (4 + c) * NU, :]
    acc = chunk_of(ru_ref, rv_ref, rhl_ref, RIM, 8, EV)
    for c in range(3):
        rim_ref[c] = acc[c * 8 : (c + 1) * 8, :] + acc[(3 + c) * 8 : (4 + c) * 8, :]


def force_of(recv):
    return pl.pallas_call(
        force_kernel,
        out_shape=[jax.ShapeDtypeStruct((3, NU, NV), F32), jax.ShapeDtypeStruct((3, 8, EV), F32)],
        scratch_shapes=[
            pltpu.VMEM((CAP, ND), jnp.int32),
            pltpu.VMEM((CAP, ND), jnp.int32),
            pltpu.VMEM((6 * CAP, ND), F32),
            pltpu.VMEM((RIM, ND), jnp.int32),
            pltpu.VMEM((RIM, ND), jnp.int32),
            pltpu.VMEM((6 * RIM, ND), F32),
        ],
        compiler_params=pltpu.CompilerParams(vmem_limit_bytes=SMALL_LIMIT),
        name="force",
    )(recv)


def edge_kernel(mass_ref, mod_ref, live_ref, low_ref, high_ref):
    low_ref[...] = jnp.zeros_like(low_ref)
    high_ref[...] = jnp.zeros_like(high_ref)
    for i, field in enumerate([mass_ref[...], mod_ref[...], live_ref[...].astype(F32)]):
        low_ref[i : i + 1, :] = field[NU - 1 : NU, :]
        high_ref[2 * i : 2 * i + 2, :] = field[0:2, :]


def rim_tile(i, low_ref, high_ref):
    sub = iota((8, 128), 0)
    tile = jnp.where(sub == 0, high_ref[2 * i : 2 * i + 1, :], 0.0)
    tile = jnp.where(sub == 1, high_ref[2 * i + 1 : 2 * i + 2, :], tile)
    return jnp.where(sub == 7, low_ref[i : i + 1, :], tile)


def side_kernel(mass_ref, mod_ref, live_ref, low_ref, high_ref, to_low_ref, to_high_ref):
    to_low_ref[...] = jnp.zeros_like(to_low_ref)
    to_high_ref[...] = jnp.zeros_like(to_high_ref)
    for i, field in enumerate([mass_ref[...], mod_ref[...], live_ref[...].astype(F32)]):
        whole = jnp.concatenate(
            [field, rim_tile(i, low_ref, high_ref), jnp.zeros((128 - EU, 128), F32)], axis=0
        )
        turned = whole.T
        to_low_ref[i : i + 1, :] = turned[127:128, :]
        to_high_ref[2 * i : 2 * i + 2, :] = turned[0:2, :]


def edge_call(kernel, name, *args):
    return pl.pallas_call(
        kernel,
        out_shape=[jax.ShapeDtypeStruct((8, 128), F32), jax.ShapeDtypeStruct((8, 128), F32)],
        compiler_params=pltpu.CompilerParams(vmem_limit_bytes=SMALL_LIMIT),
        name=name,
    )(*args)


def shell_kernel(
    stiff_ref, f_ref, rim_ref, mass_ref, mod_ref, live_ref, ulow_ref, uhigh_ref, vlow_ref, vhigh_ref, recv_ref,
    y_ref, ret_ref,
    e_ref, c_ref, g_ref, y_ext_ref, fy_ref, u_ref, v_ref, rt_ref,
):
    sub = iota((8, 128), 0)

    def columns(near, far, before):
        first = jnp.where(sub == 0, near, 0.0)
        first = jnp.where(sub == 1, far, first)
        last = jnp.where(sub == 7, before, 0.0)
        return jnp.concatenate([first, jnp.zeros((112, 128), F32), last], axis=0).T

    for i, field in enumerate([mass_ref[...], mod_ref[...], live_ref[...].astype(F32)]):
        e_ref[3 + i, 0:NU, 0:NV] = field
        e_ref[3 + i, NU:EU, 0:NV] = rim_tile(i, ulow_ref, uhigh_ref)
        side = columns(
            vhigh_ref[2 * i : 2 * i + 1, :], vhigh_ref[2 * i + 1 : 2 * i + 2, :], vlow_ref[i : i + 1, :]
        )
        e_ref[3 + i, :, NV:EV] = side[0:EU, :]
    wide = iota((8, EV), 0)
    for i in range(3):
        e_ref[i, 0:NU, 0:NV] = f_ref[i]
        tile = jnp.where(wide == 0, rim_ref[i, 1:2, :], 0.0)
        tile = jnp.where(wide == 1, rim_ref[i, 2:3, :], tile)
        e_ref[i, NU:EU, :] = jnp.where(wide == 7, rim_ref[i, 0:1, :], tile)
        side = columns(rim_ref[i, 4:5, 0:128], rim_ref[i, 5:6, 0:128], rim_ref[i, 3:4, 0:128])
        e_ref[i, 0:NU, NV:EV] = side[0:NU, :]

    def up(x):
        return pltpu.roll(x, EU - 1, 0)

    def right(x):
        return pltpu.roll(x, EV - 1, 1)

    def down(x):
        return pltpu.roll(x, 1, 0)

    def left(x):
        return pltpu.roll(x, 1, 1)

    mod = e_ref[4]
    mod = mod + up(mod)
    e_ref[5] = e_ref[5] * (mod + right(mod)) * 0.25
    for c in range(3):
        field = e_ref[c]
        moved = up(field)
        c_ref[c] = field
        c_ref[3 + c] = moved
        c_ref[6 + c] = right(field)
        c_ref[9 + c] = right(moved)

    def cells(t, _):
        rows = pl.ds(pl.multiple_of(t * 8, 8), 8)
        corner = [c_ref[k, rows, :] for k in range(12)]
        scale = e_ref[5, rows, :]
        for k in range(12):
            total = stiff_ref[k, 0] * corner[0]
            for m in range(1, 12):
                total = total + stiff_ref[k, m] * corner[m]
            g_ref[k, rows, :] = scale * total
        return 0

    lax.fori_loop(0, EU // 8, cells, 0)
    mass = e_ref[3]
    for c in range(3):
        spread = g_ref[c] + down(g_ref[3 + c])
        beside = g_ref[6 + c] + down(g_ref[9 + c])
        y_ext_ref[c] = mass * e_ref[c] + spread + left(beside)
        y_ref[c] = y_ext_ref[c, 0:NU, 0:NV]
    for c in range(3):
        field = y_ext_ref[c]
        moved = up(field)
        c_ref[c] = field
        c_ref[3 + c] = moved
        c_ref[6 + c] = right(field)
        c_ref[9 + c] = right(moved)

    def energy(t, sums):
        rows = pl.ds(pl.multiple_of(t * 8, 8), 8)
        corner = [c_ref[k, rows, 0:NV] for k in range(12)]
        total = None
        for k in range(12):
            inner = stiff_ref[k, 0] * corner[0]
            for m in range(1, 12):
                inner = inner + stiff_ref[k, m] * corner[m]
            total = corner[k] * inner if total is None else total + corner[k] * inner
        m3 = e_ref[5, rows, 0:NV] * total
        m0, m1, m2 = None, None, None
        for c in range(3):
            f = e_ref[c, rows, 0:NV]
            y = corner[c]
            m0 = f * f if m0 is None else m0 + f * f
            m1 = f * y if m1 is None else m1 + f * y
            m2 = y * y if m2 is None else m2 + y * y
        m3 = m3 + e_ref[3, rows, 0:NV] * m2
        return tuple(s + m for s, m in zip(sums, (m0, m1, m2, m3)))

    zero = jnp.zeros((8, NV), F32)
    sums = lax.fori_loop(0, NU // 8, energy, (zero, zero, zero, zero))
    lane = iota((1, 128), 1)
    moments = jnp.zeros((1, 128), F32)
    for i in range(4):
        whole = jnp.sum(jnp.sum(sums[i], axis=0, keepdims=True), axis=1, keepdims=True)
        moments = jnp.where(lane == i, whole, moments)
    over = jnp.max(recv_ref[:, 0, MAIN + 3 * RIM :], axis=0, keepdims=True)[:, RIM - 1 :]
    moments = jnp.where(lane == 4, over, moments)

    for c in range(3):
        for part, field in ((c, f_ref[c]), (3 + c, y_ref[c])):
            high = field.astype(BF16)
            fy_ref[part * NU : (part + 1) * NU, 0:NV] = high
            fy_ref[part * NU : (part + 1) * NU, NV : 2 * NV] = (field - high.astype(F32)).astype(BF16)
    u_ref[...], v_ref[...] = node_rows(recv_ref[:, 0, 0:MAIN].T)
    u_of = iota((NU, ND), 0)
    v_of = iota((NV, ND), 0)

    def chunk(i, _):
        at = pl.multiple_of(i * 8, 8)
        u8 = u_ref[pl.ds(at, 8), :]
        v8 = v_ref[pl.ds(at, 8), :]
        rhs = jnp.concatenate(
            [jnp.where(v_of == v8[r : r + 1, :], 1.0, 0.0).astype(BF16) for r in range(8)], axis=1
        )
        picked = dot(fy_ref[...], jnp.concatenate([rhs, rhs], axis=0))
        tiles = [jnp.zeros((8, ND), F32) for _ in range(6)]
        for r in range(8):
            here = u_of == u8[r : r + 1, :]
            for part in range(6):
                block = picked[part * NU : (part + 1) * NU, r * ND : (r + 1) * ND]
                row = jnp.sum(jnp.where(here, block, 0.0), axis=0, keepdims=True)
                tiles[part] = jnp.where(sub == r, row, tiles[part])
        for part in range(6):
            rt_ref[pl.ds(pl.multiple_of(part * CAP + at, 8), 8), :] = tiles[part]
        return 0

    lax.fori_loop(0, CAP // 8, chunk, 0)
    ret_ref[:, 0, 0 : 6 * CAP] = rt_ref[...].T
    ret_ref[:, 0, 6 * CAP : 8 * CAP] = jnp.broadcast_to(moments, (ND, 128))


def shell_of(stiff, force, rim, mass, modulus, live, rims, recv):
    vmem = pl.BlockSpec(memory_space=pltpu.VMEM)
    return pl.pallas_call(
        shell_kernel,
        in_specs=[pl.BlockSpec(memory_space=pltpu.SMEM)] + [vmem] * 10,
        out_specs=[vmem, vmem],
        out_shape=[
            jax.ShapeDtypeStruct((3, NU, NV), F32),
            jax.ShapeDtypeStruct((ND, 1, 8 * CAP), F32),
        ],
        scratch_shapes=[
            pltpu.VMEM((6, EU, EV), F32),
            pltpu.VMEM((12, EU, EV), F32),
            pltpu.VMEM((12, EU, EV), F32),
            pltpu.VMEM((3, EU, EV), F32),
            pltpu.VMEM((6 * NU, 2 * NV), BF16),
            pltpu.VMEM((CAP, ND), jnp.int32),
            pltpu.VMEM((CAP, ND), jnp.int32),
            pltpu.VMEM((6 * CAP, ND), F32),
        ],
        compiler_params=pltpu.CompilerParams(vmem_limit_bytes=SMALL_LIMIT),
        name="shell",
    )(stiff, force, rim, mass, modulus, live, *rims, recv)


def scalar_kernel(part_ref, pq_ref, sound_ref):
    row = jnp.sum(part_ref[:, 0, :], axis=0, keepdims=True)
    lane = iota((1, 128), 1)
    m0, m1, m2, m3, over = [
        jnp.sum(jnp.where(lane == i, row, 0.0), axis=1, keepdims=True) for i in range(5)
    ]
    first = m0 / m1
    left_over = first * first * m2 - m0
    ratio = left_over / m0
    gain = 1.0 + ratio
    curve = gain * gain * m1 - 2.0 * gain * first * m2 + first * first * m3
    second = left_over / curve
    sound = (
        (over == 0.0)
        & (left_over > 1e-3 * m0)
        & (curve > 1e-2 * gain * gain * m1)
        & (curve < 1e30)
        & (m1 > 1e-30)
        & (m0 > 1e-30)
    )
    pq_ref[0] = (first + second * gain)[0, 0]
    pq_ref[1] = -(first * second)[0, 0]
    sound_ref[0] = jnp.where(sound, 1, 0)[0, 0]


def scalars_of(back):
    smem = pl.BlockSpec(memory_space=pltpu.SMEM)
    return pl.pallas_call(
        scalar_kernel,
        grid=(1,),
        in_specs=[pl.BlockSpec((ND, 1, 128), lambda i: (0, 0, 3))],
        out_specs=[smem, smem],
        out_shape=[jax.ShapeDtypeStruct((2,), F32), jax.ShapeDtypeStruct((1,), jnp.int32)],
        name="scalars",
    )(back)


OB = 2048
OREC = R // OB
XS = 8
OSTEPS = 32 // XS


def next_kernel(
    pq_ref, back_ref, w_ref, blk_ref, own_ref, rank_ref, f_ref, y_ref, read_ref, xp_ref, xm_ref, yp_ref, ym_ref,
    next_ref, disp_ref,
    x_ref, turned_ref, force_ref, buf_ref, sems,
):
    step = pl.program_id(0)

    def fetch(slab):
        rows = pl.ds(pl.multiple_of(slab * XS * 8, XS * 8), XS * 8)
        return pltpu.make_async_copy(read_ref.at[:, rows, :], buf_ref.at[:, rows, :], sems.at[slab])

    @pl.when(step == 0)
    def _():
        for slab in range(OSTEPS):
            fetch(slab).start()
        p = pq_ref[0]
        q = pq_ref[1]
        back = p * back_ref[:, 0, 0 : 3 * CAP] + q * back_ref[:, 0, 3 * CAP : 6 * CAP]
        turned = back.T * COUPLING
        high = turned.astype(BF16)
        x_ref[:, 0:ND] = high
        x_ref[:, ND : 2 * ND] = (turned - high.astype(F32)).astype(BF16)
        disp_ref[...] = p * f_ref[...] + q * y_ref[...]
        turned_ref[...] = jnp.zeros_like(turned_ref)

    @pl.when(step < OREC)
    def _():
        named = hot(ND, own_ref[...])
        picked = dot(x_ref[...], jnp.concatenate([named, named], axis=0))
        in_slot = iota((CAP, OB), 0) == rank_ref[...]
        w_t = w_ref[...]
        highs, lows = [], []
        for c in range(3):
            moved = jnp.sum(
                jnp.where(in_slot, picked[c * CAP : (c + 1) * CAP, :], 0.0), axis=0, keepdims=True
            )
            part = w_t * moved
            high = part.astype(BF16)
            highs.append(high)
            lows.append((part - high.astype(F32)).astype(BF16))
        in_block = hot(NB, blk_ref[...])
        parts = jnp.concatenate([jnp.concatenate(highs, axis=0), jnp.concatenate(lows, axis=0)], axis=1)
        turned_ref[...] += dot_t(parts, jnp.concatenate([in_block, in_block], axis=1))

    @pl.when(step == OREC)
    def _():
        for c in range(3):
            force_ref[c * NB : (c + 1) * NB, :] = turned_ref[c * NK : (c + 1) * NK, :].T

    @pl.when(step >= OREC)
    def _():
        slab = step - OREC
        fetch(slab).wait()
        sub = iota((8, NK), 0)
        for xx in range(XS):
            x = slab * XS + xx
            rows = pl.ds(pl.multiple_of(x * 8, 8), 8)
            forcing = [
                force_ref[pl.ds(pl.multiple_of(c * NB + x * 8, 8), 8), :] for c in range(3)
            ]
            for q in range(19):
                cx, cy, _ = DIRS[q]
                value = buf_ref[q, rows, :]
                if cx == 1 and xx == 0:
                    value = jnp.where(x == 0, xp_ref[XP.index(q)], value)
                if cx == -1 and xx == XS - 1:
                    value = jnp.where(x == 31, xm_ref[XM.index(q)], value)
                if cy == 1:
                    value = jnp.where(sub == 0, yp_ref[YP.index(q), pl.ds(x, 1), :], value)
                if cy == -1:
                    value = jnp.where(sub == 7, ym_ref[YM.index(q), pl.ds(x, 1), :], value)
                along = combine(forcing, DIRS[q])
                if along is not None:
                    value = value + (3.0 * WEIGHTS[q]) * along
                next_ref[q, xx * 8 : (xx + 1) * 8, :] = value


def outputs_of(pq, back, weights, block_row, owner_row, rank_row, force, image, read, xp, xm, yp, ym):
    def record(i):
        return jnp.minimum(i, OREC - 1)

    def slab(i):
        return jnp.maximum(i - OREC, 0)

    row_spec = pl.BlockSpec((1, OB), lambda i: (0, record(i)))
    patch = pl.BlockSpec((3, NU, NV), lambda i: (0, 0, 0))
    lines = pl.BlockSpec((19, XS * 8, NK), lambda i: (0, slab(i), 0))
    x_face = pl.BlockSpec((5, 8, NK), lambda i: (0, 0, 0))
    y_face = pl.BlockSpec((5, 32, NK), lambda i: (0, 0, 0))
    return pl.pallas_call(
        next_kernel,
        grid=(OREC + OSTEPS,),
        in_specs=[
            pl.BlockSpec(memory_space=pltpu.SMEM),
            pl.BlockSpec((ND, 1, 8 * CAP), lambda i: (0, 0, 0)),
            pl.BlockSpec((NK, OB), lambda i: (0, record(i))),
            row_spec,
            row_spec,
            row_spec,
            patch,
            patch,
            pl.BlockSpec(memory_space=pl.ANY),
            x_face,
            x_face,
            y_face,
            y_face,
        ],
        out_specs=[lines, patch],
        out_shape=[
            jax.ShapeDtypeStruct((19, NB, NK), F32),
            jax.ShapeDtypeStruct((3, NU, NV), F32),
        ],
        scratch_shapes=[
            pltpu.VMEM((3 * CAP, 2 * ND), BF16),
            pltpu.VMEM((3 * NK, NB), F32),
            pltpu.VMEM((3 * NB, NK), F32),
            pltpu.VMEM((19, NB, NK), F32),
            pltpu.SemaphoreType.DMA((OSTEPS,)),
        ],
        compiler_params=pltpu.CompilerParams(vmem_limit_bytes=VMEM_LIMIT),
        name="outputs",
    )(pq, back, weights, block_row, owner_row, rank_row, force, image, read, xp, xm, yp, ym)


def pass_on(x, axis, shift):
    count = lax.axis_size(axis)
    return lax.ppermute(x, axis, [(i, (i + shift) % count) for i in range(count)])


def padded(field):
    for axis, dim in (("gx", 1), ("gy", 2)):
        size = field.shape[dim]
        head = lax.slice_in_dim(field, 0, 1, axis=dim)
        tail = lax.slice_in_dim(field, size - 1, size, axis=dim)
        field = jnp.concatenate([pass_on(tail, axis, 1), field, pass_on(head, axis, -1)], axis=dim)
    return field


def operate(field, mass, modulus, live, stiff):
    static = padded(jnp.stack([modulus, live.astype(F32)]))
    wide = padded(field)

    def corners(a):
        return a[..., :-1, :-1], a[..., 1:, :-1], a[..., :-1, 1:], a[..., 1:, 1:]

    c0, c1, c2, c3 = corners(static[0])
    scale = static[1, :-1, :-1] * (c0 + c1 + c2 + c3) * 0.25
    vector = jnp.concatenate(corners(wide), axis=0)
    result = scale[None] * jnp.einsum("kl,lab->kab", stiff, vector, precision=lax.Precision.HIGHEST)
    return (
        mass[None] * field
        + result[0:3, 1:, 1:]
        + result[3:6, :-1, 1:]
        + result[6:9, 1:, :-1]
        + result[9:12, :-1, :-1]
    )


def rim_of(force):
    before = pass_on(force[:, NU - 1 : NU, :], "gx", 1)
    after = pass_on(force[:, 0:2, :], "gx", -1)
    tall = jnp.concatenate([force, after, before], axis=1)
    left = pass_on(tall[:, :, NV - 1 : NV], "gy", 1)
    right = pass_on(tall[:, :, 0:2], "gy", -1)
    gap = jnp.zeros((3, EV - NV - 3), F32)
    rows = [
        jnp.concatenate([tall[:, r], right[:, r], gap, left[:, r]], axis=1) for r in (NU + 2, NU, NU + 1)
    ]
    beside = [
        jnp.concatenate([column[:, 0:NU], jnp.zeros((3, EV - NU), F32)], axis=1)
        for column in (left[:, :, 0], right[:, :, 0], right[:, :, 1])
    ]
    empty = jnp.zeros((3, EV), F32)
    return jnp.stack(rows + beside + [empty, empty], axis=1)


def exchange(x):
    return lax.all_to_all(x, ALL, 0, 0, tiled=True)


def per_device(populations, mass, modulus, live, stiff, rec_block, rec_owner, rec_node, weights):
    pops = populations.reshape(19, NB, NK)
    block_row = rec_block.reshape(1, R)
    owner_row = rec_owner.reshape(1, R)
    node_row = rec_node.reshape(1, R)

    low, high = edge_call(edge_kernel, "edges", mass, modulus, live)
    ulow = pass_on(low, "gx", 1)
    uhigh = pass_on(high, "gx", -1)
    send, rank_row, turned = loads_to_send(pops, weights, block_row, owner_row, node_row)
    send, ulow, uhigh, pops = lax.optimization_barrier((send, ulow, uhigh, pops))
    recv = exchange(send)
    low, high = edge_call(side_kernel, "sides", mass, modulus, live, ulow, uhigh)
    rims = (ulow, uhigh, pass_on(low, "gy", 1), pass_on(high, "gy", -1))

    read, xp, xm, yp, ym = collide_and_run(pops)
    xp = pass_on(xp, "gx", 1)
    xm = pass_on(xm, "gx", -1)

    force, rim = force_of(recv)
    image, ret = shell_of(stiff, force, rim, mass, modulus, live, rims, recv)
    ret, xp, xm = lax.optimization_barrier((ret, xp, xm))
    back = exchange(ret)
    yp = yp.at[YP.index(7), 0].set(xp[XP.index(7), 0]).at[YP.index(10), 31].set(xm[XM.index(10), 0])
    ym = ym.at[YM.index(9), 0].set(xp[XP.index(9), 7]).at[YM.index(8), 31].set(xm[XM.index(8), 7])
    yp = pass_on(yp, "gy", 1)
    ym = pass_on(ym, "gy", -1)

    back, yp, ym = lax.optimization_barrier((back, yp, ym))
    pq, sound = scalars_of(back)

    def quick(operands):
        return operands[0:3]

    def careful(operands):
        _, _, _, force, mass, modulus, live, stiff, rims, recv = operands
        image, ret = shell_of(stiff, force, rim_of(force), mass, modulus, live, rims, recv)
        back = exchange(ret)
        start = lax.psum(jnp.sum(force * force), ALL)
        first = start / lax.psum(jnp.sum(force * image), ALL)
        residual = force - first * image
        norm = lax.psum(jnp.sum(residual * residual), ALL)
        ratio = norm / start
        direction = residual + ratio * force
        along = operate(direction, mass, modulus, live, stiff)
        second = norm / lax.psum(jnp.sum(direction * along), ALL)
        return jnp.stack([first + second * (1.0 + ratio), -(first * second)]), image, back

    pq, image, back = lax.cond(
        sound[0] == 1, quick, careful, (pq, image, back, force, mass, modulus, live, stiff, rims, recv)
    )

    populations_next, displacement = outputs_of(
        pq, back, turned, block_row, owner_row, rank_row, force, image, read, xp, xm, yp, ym
    )
    return populations_next.reshape(19, 32, 8, NK), displacement


def solution(mesh):
    return jax.shard_map(
        per_device,
        mesh=mesh,
        in_specs=(
            P(None, "gx", "gy", None),
            P("gx", "gy"),
            P("gx", "gy"),
            P("gx", "gy"),
            P(),
            P(ALL),
            P(ALL, None),
            P(ALL),
            P(ALL, None),
        ),
        out_specs=(P(None, "gx", "gy", None), P(None, "gx", "gy")),
        check_vma=False,
    )
```

```python
import jax
import jax.numpy as jnp
from jax import lax
from jax.experimental import pallas as pl
from jax.experimental.pallas import tpu as pltpu
from jax.sharding import PartitionSpec as P

F32 = jnp.float32
BF16 = jnp.bfloat16
ALL = ("gx", "gy")
VMEM_LIMIT = 60 * 1024 * 1024
SMALL_LIMIT = 16 * 1024 * 1024

DIRS = (
    (0, 0, 0),
    (1, 0, 0),
    (-1, 0, 0),
    (0, 1, 0),
    (0, -1, 0),
    (0, 0, 1),
    (0, 0, -1),
    (1, 1, 0),
    (-1, -1, 0),
    (1, -1, 0),
    (-1, 1, 0),
    (1, 0, 1),
    (-1, 0, -1),
    (1, 0, -1),
    (-1, 0, 1),
    (0, 1, 1),
    (0, -1, -1),
    (0, 1, -1),
    (0, -1, 1),
)
WEIGHTS = (1.0 / 3.0,) + (1.0 / 18.0,) * 6 + (1.0 / 36.0,) * 12
RATE = 1.25
COUPLING = 0.1
XP = tuple(q for q in range(19) if DIRS[q][0] == 1)
XM = tuple(q for q in range(19) if DIRS[q][0] == -1)
YP = tuple(q for q in range(19) if DIRS[q][1] == 1)
YM = tuple(q for q in range(19) if DIRS[q][1] == -1)

R = 4096
NB = 256
NK = 256
ND = 128
CAP = 64
RIM = 32
MAIN = 4 * CAP
NU, NV = 64, 128
RB = 1024
EU, EV = 72, 256


def iota(shape, dim):
    return lax.broadcasted_iota(jnp.int32, shape, dim)


def halves(x):
    high = x.astype(BF16).astype(F32)
    return high, x - high


def combine(fields, direction):
    total = None
    for axis in range(3):
        if direction[axis] != 0:
            term = fields[axis] if direction[axis] == 1 else -fields[axis]
            total = term if total is None else total + term
    return total


def dot_t(a, b):
    return lax.dot_general(a, b, (((1,), (1,)), ((), ())), preferred_element_type=F32)


def dot(a, b):
    return lax.dot_general(a, b, (((1,), (0,)), ((), ())), preferred_element_type=F32)


def relaxed_of(pops, wanted):
    density = pops[0]
    for q in range(1, 19):
        density = density + pops[q]
    inverse = 1.0 / density
    velocity = []
    for axis in range(3):
        total = None
        for q in range(1, 19):
            if DIRS[q][axis] != 0:
                term = pops[q] if DIRS[q][axis] == 1 else -pops[q]
                total = term if total is None else total + term
        velocity.append(total * inverse)
    squared = velocity[0] * velocity[0] + velocity[1] * velocity[1] + velocity[2] * velocity[2]
    base = 1.0 - 1.5 * squared
    result = []
    for q in wanted:
        along = combine(velocity, DIRS[q])
        bracket = base if along is None else base + along * (3.0 + 4.5 * along)
        relaxed = pops[q] - RATE * (pops[q] - (WEIGHTS[q] * density) * bracket)
        if DIRS[q][2] != 0:
            relaxed = pltpu.roll(relaxed, 1 if DIRS[q][2] == 1 else NK - 1, 1)
        result.append(relaxed)
    return result


def turned_y(value, cy):
    return value if cy == 0 else pltpu.roll(value, 1 if cy == 1 else 7, 0)


XMSG = 48
YMSG = 168


CHUNKS = 4
CROWS = NB // CHUNKS
RSTEPS = R // RB


def match(count, row):
    lanes = row.shape[1]
    column = iota((count, 128), 0).astype(F32).astype(BF16)
    wanted = jnp.broadcast_to(row.astype(F32).astype(BF16), (count, lanes))
    return jnp.concatenate([column] * (lanes // 128), axis=1) == wanted


def hot(count, row):
    shape = (count, row.shape[1])
    return jnp.where(match(count, row), jnp.ones(shape, BF16), jnp.zeros(shape, BF16))


def pick(mask, row):
    return jnp.where(mask, jnp.broadcast_to(row, mask.shape), jnp.zeros(mask.shape, BF16))


def rim_rows(own, node):
    u, v = node >> 7, node & 127
    ox, oy = own >> 5, own & 31
    su = jnp.where(u == NU - 1, 1, jnp.where(u <= 1, -1, 0))
    sv = jnp.where(v == NV - 1, 1, jnp.where(v <= 1, -1, 0))
    ox2, oy2 = (ox + su) & 3, (oy + sv) & 31
    dests = [
        jnp.where(su != 0, ox2 * 32 + oy, -1),
        jnp.where(sv != 0, ox * 32 + oy2, -1),
        jnp.where((su != 0) & (sv != 0), ox2 * 32 + oy2, -1),
    ]
    row = jnp.where(u == NU - 1, 0, u + 1) * EV
    codes = [
        row + v,
        jnp.where(v == NV - 1, 3, v + 4) * EV + u,
        row + jnp.where(v == NV - 1, EV - 1, v + NV),
    ]
    return dests, codes


def load_kernel(
    pop_hbm, w_ref, blk_ref, own_all_ref, node_all_ref, own_ref, node_ref, mass_ref, mod_ref, live_ref,
    send_ref, rank_ref, wt_ref, xp_ref, xm_ref, yp_ref, ym_ref,
    pop_ref, sems, m_ref, mt_ref, tri_ref, carry_ref, dest_ref, code_ref, place_ref, over_ref, main_ref, rims_ref,
):
    step = pl.program_id(0)

    def fetch(part):
        rows = pl.ds(part * CROWS, CROWS)
        return pltpu.make_async_copy(pop_hbm.at[:, rows, :], pop_ref.at[:, rows, :], sems.at[part])

    @pl.when(step == 0)
    def _():
        for part in range(CHUNKS):
            fetch(part).start()
        before = (iota((256, 256), 0) < iota((256, 256), 1)).astype(F32)
        tri_ref[:, 0:256] = before.astype(BF16)
        tri_ref[:, 256:512] = jnp.ones((256, 256), BF16)
        carry_ref[...] = jnp.zeros_like(carry_ref)
        main_ref[...] = jnp.zeros_like(main_ref)
        rims_ref[...] = jnp.zeros_like(rims_ref)
        over_ref[...] = jnp.zeros_like(over_ref)
        dests, codes = rim_rows(own_all_ref[...], node_all_ref[...])
        for i in range(3):
            dest_ref[i : i + 1, :] = dests[i]
            code_ref[i : i + 1, :] = codes[i].astype(F32)
        for k in range(R // 256):
            cols = slice(k * 256, (k + 1) * 256)
            device = iota((ND, 256), 0)
            hots = [device == own_all_ref[:, cols]] + [device == dest_ref[i : i + 1, cols] for i in range(3)]
            main = jnp.where(hots[0], 1.0, 0.0).astype(BF16)
            rims = jnp.where(hots[1] | hots[2] | hots[3], 1.0, 0.0).astype(BF16)
            counts = dot(jnp.concatenate([main, rims], axis=0), tri_ref[...])
            upto = counts[:, 0:256] + carry_ref[...]
            carry_ref[...] += counts[:, 256:512]
            rank = jnp.sum(jnp.where(hots[0], upto[0:ND], 0.0), axis=0, keepdims=True)
            rank_ref[:, cols] = rank.astype(jnp.int32)
            for i in range(3):
                place = jnp.sum(jnp.where(hots[i + 1], upto[ND : 2 * ND], 0.0), axis=0, keepdims=True)
                over_ref[...] = jnp.maximum(over_ref[...], place)
                place_ref[i : i + 1, cols] = jnp.where(place < RIM - 1, place, 2.0 * RIM).astype(jnp.int32)

        def rows_of(i, _):
            rows = pl.ds(pl.multiple_of(i * 8, 8), 8)
            pops = [pop_ref[q, rows, :] for q in range(1, 19)]
            for axis in range(3):
                total = None
                for q in range(1, 19):
                    if DIRS[q][axis] != 0:
                        term = pops[q - 1] if DIRS[q][axis] == 1 else -pops[q - 1]
                        total = term if total is None else total + term
                m_ref[axis, rows, :] = total
            return 0

        for part in range(CHUNKS):
            fetch(part).wait()
            lax.fori_loop(part * CROWS // 8, (part + 1) * CROWS // 8, rows_of, 0, unroll=2)
        for face_ref, dirs, x in ((xp_ref, XP, 31), (xm_ref, XM, 0)):
            values = relaxed_of([pop_ref[q, x * 8 : x * 8 + 8, :] for q in range(19)], dirs)
            for i, q in enumerate(dirs):
                face_ref[i * 8 : i * 8 + 8, :] = turned_y(values[i], DIRS[q][1])
            face_ref[40:XMSG, :] = jnp.zeros((XMSG - 40, NK), F32)
        for i, field in enumerate([mass_ref[...], mod_ref[...], live_ref[...].astype(F32)]):
            xp_ref[40 + i : 41 + i, 0:NV] = field[NU - 1 : NU, :]
            xm_ref[40 + 2 * i : 42 + 2 * i, 0:NV] = field[0:2, :]
        sub = iota((8, NK), 0)
        for face_ref, dirs, y in ((yp_ref, YP, 7), (ym_ref, YM, 0)):
            for part in range(4):
                pops = []
                for q in range(19):
                    tile = None
                    for i in range(8):
                        row = jnp.broadcast_to(pop_ref[q, pl.ds(part * 64 + i * 8 + y, 1), :], (8, NK))
                        tile = row if tile is None else jnp.where(sub == i, row, tile)
                    pops.append(tile)
                values = relaxed_of(pops, dirs)
                for i in range(5):
                    face_ref[i * 32 + part * 8 : i * 32 + part * 8 + 8, :] = values[i]
            for i, q in enumerate(dirs):
                if DIRS[q][0] != 0:
                    face = face_ref[i * 32 : i * 32 + 32, :]
                    face_ref[i * 32 : i * 32 + 32, :] = pltpu.roll(face, 1 if DIRS[q][0] == 1 else 31, 0)
        for axis in range(3):
            turned = m_ref[axis].T
            high = turned.astype(BF16)
            at = slice(axis * NK, (axis + 1) * NK)
            mt_ref[at, 0:NB] = high
            mt_ref[at, NB : 2 * NB] = (turned - high.astype(F32)).astype(BF16)

    @pl.when(step >= 1)
    def _():
        here = pl.ds(pl.multiple_of((step - 1) * RB, RB), RB)
        w_t = w_ref[...].T
        in_block = hot(NB, blk_ref[...])
        picked = dot(mt_ref[...], jnp.concatenate([in_block, in_block], axis=0))
        values = [
            jnp.sum(picked[axis * NK : (axis + 1) * NK, :] * w_t, axis=0, keepdims=True) for axis in range(3)
        ]

        def sides(value):
            return [side.astype(BF16) for side in halves(value)]

        parts = [sides(value) for value in values]

        def placed(count, slot, code):
            mask = match(count, slot)
            both = [pick(mask, part[side]) for side in range(2) for part in parts + [sides(code)]]
            return jnp.concatenate(both, axis=0)

        packed = placed(CAP, rank_ref[:, here], node_ref[...].astype(F32))
        main_ref[...] += dot_t(packed, hot(ND, own_ref[...]))
        packed = [placed(RIM, place_ref[i : i + 1, here], code_ref[i : i + 1, here]) for i in range(3)]
        named = [hot(ND, dest_ref[i : i + 1, here]) for i in range(3)]
        rims_ref[...] += dot_t(jnp.concatenate(packed, axis=1), jnp.concatenate(named, axis=1))
        wt_ref[...] = w_t

    @pl.when(step == RSTEPS)
    def _():
        most = jnp.max(over_ref[...], axis=1, keepdims=True)
        flag = jnp.where(most >= RIM - 1, 1.0, 0.0)
        send_ref[:, 0, 0:MAIN] = (main_ref[0:MAIN, :] + main_ref[MAIN : 2 * MAIN, :]).T
        tail = (rims_ref[0 : 4 * RIM, :] + rims_ref[4 * RIM : 8 * RIM, :]).T
        send_ref[:, 0, MAIN : MAIN + 4 * RIM] = jnp.where(iota((ND, 4 * RIM), 1) == 4 * RIM - 1, flag, tail)


def loads_to_send(pops, weights, block_row, owner_row, node_row, mass, modulus, live):
    def record(i):
        return jnp.maximum(i - 1, 0)

    row_spec = pl.BlockSpec((1, RB), lambda i: (0, record(i)))
    all_rows = pl.BlockSpec((1, R), lambda i: (0, 0))

    def whole(*shape):
        return pl.BlockSpec(shape, lambda i: (0, 0))

    return pl.pallas_call(
        load_kernel,
        grid=(1 + RSTEPS,),
        in_specs=[
            pl.BlockSpec(memory_space=pl.ANY),
            pl.BlockSpec((RB, NK), lambda i: (record(i), 0)),
            row_spec,
            all_rows,
            all_rows,
            row_spec,
            row_spec,
            whole(NU, NV),
            whole(NU, NV),
            whole(NU, NV),
        ],
        out_specs=[
            pl.BlockSpec((ND, 1, MAIN + 4 * RIM), lambda i: (0, 0, 0)),
            all_rows,
            pl.BlockSpec((NK, RB), lambda i: (0, record(i))),
            whole(XMSG, NK),
            whole(XMSG, NK),
            whole(160, NK),
            whole(160, NK),
        ],
        out_shape=[
            jax.ShapeDtypeStruct((ND, 1, MAIN + 4 * RIM), F32),
            jax.ShapeDtypeStruct((1, R), jnp.int32),
            jax.ShapeDtypeStruct((NK, R), F32),
            jax.ShapeDtypeStruct((XMSG, NK), F32),
            jax.ShapeDtypeStruct((XMSG, NK), F32),
            jax.ShapeDtypeStruct((160, NK), F32),
            jax.ShapeDtypeStruct((160, NK), F32),
        ],
        scratch_shapes=[
            pltpu.VMEM((19, NB, NK), F32),
            pltpu.SemaphoreType.DMA((CHUNKS,)),
            pltpu.VMEM((3, NB, NK), F32),
            pltpu.VMEM((3 * NK, 2 * NB), BF16),
            pltpu.VMEM((256, 512), BF16),
            pltpu.VMEM((2 * ND, 256), F32),
            pltpu.VMEM((8, R), jnp.int32),
            pltpu.VMEM((8, R), F32),
            pltpu.VMEM((8, R), jnp.int32),
            pltpu.VMEM((1, 256), F32),
            pltpu.VMEM((2 * MAIN, ND), F32),
            pltpu.VMEM((8 * RIM, ND), F32),
        ],
        compiler_params=pltpu.CompilerParams(vmem_limit_bytes=VMEM_LIMIT),
        name="loads",
    )(pops, weights, block_row, owner_row, node_row, owner_row, node_row, mass, modulus, live)


LINES = 8


def collide_kernel(pop_hbm, out_hbm, pop_ref, read_ref, in_sems, out_sems):
    chunks = 32 // LINES

    def fetch(part):
        rows = pl.ds(part * LINES * 8, LINES * 8)
        return pltpu.make_async_copy(pop_hbm.at[:, rows, :], pop_ref.at[:, rows, :], in_sems.at[part])

    def store(part):
        first = max(part * LINES - 1, 0) * 8
        last = NB if part == chunks - 1 else (part * LINES + LINES - 1) * 8
        rows = pl.ds(first, last - first)
        kept = pl.ds(first + 8, last - first)
        return pltpu.make_async_copy(read_ref.at[:, kept, :], out_hbm.at[:, rows, :], out_sems.at[part])

    def line(x, _):
        rows = pl.ds(pl.multiple_of(x * 8, 8), 8)
        values = relaxed_of([pop_ref[q, rows, :] for q in range(19)], range(19))
        for q in range(19):
            cx, cy, _ = DIRS[q]
            to = pl.ds(pl.multiple_of((x + cx + 1) * 8, 8), 8)
            read_ref[q, to, :] = turned_y(values[q], cy)
        return 0

    for part in range(chunks):
        fetch(part).start()
    for q in XP:
        read_ref[q, 8:16, :] = jnp.zeros((8, NK), F32)
    for q in XM:
        read_ref[q, NB : NB + 8, :] = jnp.zeros((8, NK), F32)
    for part in range(chunks):
        fetch(part).wait()
        lax.fori_loop(part * LINES, (part + 1) * LINES, line, 0, unroll=4)
        store(part).start()
    for part in range(chunks):
        store(part).wait()


def collide_and_run(pops):
    return pl.pallas_call(
        collide_kernel,
        in_specs=[pl.BlockSpec(memory_space=pl.ANY)],
        out_specs=pl.BlockSpec(memory_space=pl.ANY),
        out_shape=jax.ShapeDtypeStruct((19, NB, NK), F32),
        scratch_shapes=[
            pltpu.VMEM((19, NB, NK), F32),
            pltpu.VMEM((19, NB + 16, NK), F32),
            pltpu.SemaphoreType.DMA((32 // LINES,)),
            pltpu.SemaphoreType.DMA((32 // LINES,)),
        ],
        compiler_params=pltpu.CompilerParams(vmem_limit_bytes=VMEM_LIMIT),
        name="collide",
    )(pops)


def node_rows(recv_t):
    node = recv_t[3 * CAP : MAIN, :].astype(jnp.int32)
    return node >> 7, node & 127


def force_kernel(recv_ref, f_ref, rim_ref, u_ref, v_ref, hl_ref, ru_ref, rv_ref, rhl_ref):
    recv_t = recv_ref[:, 0, :].T
    u_ref[...], v_ref[...] = node_rows(recv_t)
    high, low = halves(recv_t[0 : 3 * CAP, :])
    hl_ref[0 : 3 * CAP, :] = high
    hl_ref[3 * CAP : 6 * CAP, :] = low
    code = recv_t[MAIN + 3 * RIM : MAIN + 4 * RIM, :].astype(jnp.int32)
    ru_ref[...] = code >> 8
    rv_ref[...] = code & 255
    high, low = halves(recv_t[MAIN : MAIN + 3 * RIM, :])
    rhl_ref[0 : 3 * RIM, :] = high
    rhl_ref[3 * RIM : 6 * RIM, :] = low

    def chunk_of(rows_ref, cols_ref, vals_ref, slots, height, width):
        u_of = iota((height, ND), 0)
        v_of = iota((width, ND), 0)

        def chunk(i, acc):
            at = pl.multiple_of(i * 8, 8)
            u8 = rows_ref[pl.ds(at, 8), :]
            v8 = cols_ref[pl.ds(at, 8), :]
            vals = [vals_ref[pl.ds(pl.multiple_of(part * slots + at, 8), 8), :] for part in range(6)]
            lhs, rhs = [], []
            for r in range(8):
                here = u_of == u8[r : r + 1, :]
                lhs.append(
                    jnp.concatenate([jnp.where(here, vals[part][r : r + 1, :], 0.0) for part in range(6)], axis=0)
                    .astype(BF16)
                )
                rhs.append(jnp.where(v_of == v8[r : r + 1, :], 1.0, 0.0).astype(BF16))
            return acc + dot_t(jnp.concatenate(lhs, axis=1), jnp.concatenate(rhs, axis=1))

        return lax.fori_loop(0, slots // 8, chunk, jnp.zeros((6 * height, width), F32))

    acc = chunk_of(u_ref, v_ref, hl_ref, CAP, NU, NV)
    for c in range(3):
        f_ref[c] = acc[c * NU : (c + 1) * NU, :] + acc[(3 + c) * NU : (4 + c) * NU, :]
    acc = chunk_of(ru_ref, rv_ref, rhl_ref, RIM, 8, EV)
    for c in range(3):
        rim_ref[c] = acc[c * 8 : (c + 1) * 8, :] + acc[(3 + c) * 8 : (4 + c) * 8, :]


def force_of(recv):
    return pl.pallas_call(
        force_kernel,
        out_shape=[jax.ShapeDtypeStruct((3, NU, NV), F32), jax.ShapeDtypeStruct((3, 8, EV), F32)],
        scratch_shapes=[
            pltpu.VMEM((CAP, ND), jnp.int32),
            pltpu.VMEM((CAP, ND), jnp.int32),
            pltpu.VMEM((6 * CAP, ND), F32),
            pltpu.VMEM((RIM, ND), jnp.int32),
            pltpu.VMEM((RIM, ND), jnp.int32),
            pltpu.VMEM((6 * RIM, ND), F32),
        ],
        compiler_params=pltpu.CompilerParams(vmem_limit_bytes=SMALL_LIMIT),
        name="force",
    )(recv)


def rim_tile(i, low, high):
    sub = iota((8, 128), 0)
    tile = jnp.where(sub == 0, high[2 * i : 2 * i + 1, :], 0.0)
    tile = jnp.where(sub == 1, high[2 * i + 1 : 2 * i + 2, :], tile)
    return jnp.where(sub == 7, low[i : i + 1, :], tile)


def side_kernel(mass_ref, mod_ref, live_ref, xp_ref, xm_ref, yp_ref, ym_ref, to_p_ref, to_m_ref):
    to_p_ref[0:160, :] = yp_ref[...]
    to_m_ref[0:160, :] = ym_ref[...]
    for q, line, from_ref in ((7, 0, xp_ref), (10, 31, xm_ref)):
        face = (XP if line == 0 else XM).index(q) * 8
        at = YP.index(q) * 32 + line
        to_p_ref[at : at + 1, :] = from_ref[face : face + 1, :]
    for q, line, from_ref in ((9, 0, xp_ref), (8, 31, xm_ref)):
        face = (XP if line == 0 else XM).index(q) * 8 + 7
        at = YM.index(q) * 32 + line
        to_m_ref[at : at + 1, :] = from_ref[face : face + 1, :]
    to_p_ref[160:YMSG, :] = jnp.zeros((YMSG - 160, NK), F32)
    to_m_ref[160:YMSG, :] = jnp.zeros((YMSG - 160, NK), F32)
    low, high = xp_ref[40:XMSG, 0:NV], xm_ref[40:XMSG, 0:NV]
    for i, field in enumerate([mass_ref[...], mod_ref[...], live_ref[...].astype(F32)]):
        tall = jnp.concatenate([field, rim_tile(i, low, high), jnp.zeros((128 - EU, 128), F32)], axis=0)
        turned = tall.T
        to_p_ref[160 + i : 161 + i, 0:128] = turned[127:128, :]
        to_m_ref[160 + 2 * i : 162 + 2 * i, 0:128] = turned[0:2, :]


def sides_of(mass, modulus, live, xp, xm, yp, ym):
    return pl.pallas_call(
        side_kernel,
        out_shape=[jax.ShapeDtypeStruct((YMSG, NK), F32), jax.ShapeDtypeStruct((YMSG, NK), F32)],
        compiler_params=pltpu.CompilerParams(vmem_limit_bytes=SMALL_LIMIT),
        name="sides",
    )(mass, modulus, live, xp, xm, yp, ym)


def shell_kernel(
    stiff_ref, f_ref, rim_ref, mass_ref, mod_ref, live_ref, ulow_ref, uhigh_ref, vlow_ref, vhigh_ref, recv_ref,
    y_ref, ret_ref,
    e_ref, c_ref, g_ref, y_ext_ref, fy_ref, u_ref, v_ref, rt_ref,
):
    sub = iota((8, 128), 0)

    def columns(near, far, before):
        first = jnp.where(sub == 0, near, 0.0)
        first = jnp.where(sub == 1, far, first)
        last = jnp.where(sub == 7, before, 0.0)
        return jnp.concatenate([first, jnp.zeros((112, 128), F32), last], axis=0).T

    for i, field in enumerate([mass_ref[...], mod_ref[...], live_ref[...].astype(F32)]):
        e_ref[3 + i, 0:NU, 0:NV] = field
        e_ref[3 + i, NU:EU, 0:NV] = rim_tile(i, ulow_ref[:, 0:NV], uhigh_ref[:, 0:NV])
        side = columns(
            vhigh_ref[2 * i : 2 * i + 1, 0:128],
            vhigh_ref[2 * i + 1 : 2 * i + 2, 0:128],
            vlow_ref[i : i + 1, 0:128],
        )
        e_ref[3 + i, :, NV:EV] = side[0:EU, :]
    wide = iota((8, EV), 0)
    for i in range(3):
        e_ref[i, 0:NU, 0:NV] = f_ref[i]
        tile = jnp.where(wide == 0, rim_ref[i, 1:2, :], 0.0)
        tile = jnp.where(wide == 1, rim_ref[i, 2:3, :], tile)
        e_ref[i, NU:EU, :] = jnp.where(wide == 7, rim_ref[i, 0:1, :], tile)
        side = columns(rim_ref[i, 4:5, 0:128], rim_ref[i, 5:6, 0:128], rim_ref[i, 3:4, 0:128])
        e_ref[i, 0:NU, NV:EV] = side[0:NU, :]

    def up(x):
        return pltpu.roll(x, EU - 1, 0)

    def right(x):
        return pltpu.roll(x, EV - 1, 1)

    def down(x):
        return pltpu.roll(x, 1, 0)

    def left(x):
        return pltpu.roll(x, 1, 1)

    mod = e_ref[4]
    mod = mod + up(mod)
    e_ref[5] = e_ref[5] * (mod + right(mod)) * 0.25
    for c in range(3):
        field = e_ref[c]
        moved = up(field)
        c_ref[c] = field
        c_ref[3 + c] = moved
        c_ref[6 + c] = right(field)
        c_ref[9 + c] = right(moved)

    def cells(t, _):
        rows = pl.ds(pl.multiple_of(t * 8, 8), 8)
        corner = [c_ref[k, rows, :] for k in range(12)]
        scale = e_ref[5, rows, :]
        for k in range(12):
            total = stiff_ref[k, 0] * corner[0]
            for m in range(1, 12):
                total = total + stiff_ref[k, m] * corner[m]
            g_ref[k, rows, :] = scale * total
        return 0

    lax.fori_loop(0, EU // 8, cells, 0)
    mass = e_ref[3]
    for c in range(3):
        spread = g_ref[c] + down(g_ref[3 + c])
        beside = g_ref[6 + c] + down(g_ref[9 + c])
        y_ext_ref[c] = mass * e_ref[c] + spread + left(beside)
        y_ref[c] = y_ext_ref[c, 0:NU, 0:NV]
    for c in range(3):
        field = y_ext_ref[c]
        moved = up(field)
        c_ref[c] = field
        c_ref[3 + c] = moved
        c_ref[6 + c] = right(field)
        c_ref[9 + c] = right(moved)

    def energy(t, sums):
        rows = pl.ds(pl.multiple_of(t * 8, 8), 8)
        corner = [c_ref[k, rows, 0:NV] for k in range(12)]
        total = None
        for k in range(12):
            inner = stiff_ref[k, 0] * corner[0]
            for m in range(1, 12):
                inner = inner + stiff_ref[k, m] * corner[m]
            total = corner[k] * inner if total is None else total + corner[k] * inner
        m3 = e_ref[5, rows, 0:NV] * total
        m0, m1, m2 = None, None, None
        for c in range(3):
            f = e_ref[c, rows, 0:NV]
            y = corner[c]
            m0 = f * f if m0 is None else m0 + f * f
            m1 = f * y if m1 is None else m1 + f * y
            m2 = y * y if m2 is None else m2 + y * y
        m3 = m3 + e_ref[3, rows, 0:NV] * m2
        return tuple(s + m for s, m in zip(sums, (m0, m1, m2, m3)))

    zero = jnp.zeros((8, NV), F32)
    sums = lax.fori_loop(0, NU // 8, energy, (zero, zero, zero, zero))
    lane = iota((1, 128), 1)
    moments = jnp.zeros((1, 128), F32)
    for i in range(4):
        whole = jnp.sum(jnp.sum(sums[i], axis=0, keepdims=True), axis=1, keepdims=True)
        moments = jnp.where(lane == i, whole, moments)
    over = jnp.max(recv_ref[:, 0, MAIN + 3 * RIM :], axis=0, keepdims=True)[:, RIM - 1 :]
    moments = jnp.where(lane == 4, over, moments)

    for c in range(3):
        for part, field in ((c, f_ref[c]), (3 + c, y_ref[c])):
            high = field.astype(BF16)
            fy_ref[part * NU : (part + 1) * NU, 0:NV] = high
            fy_ref[part * NU : (part + 1) * NU, NV : 2 * NV] = (field - high.astype(F32)).astype(BF16)
    u_ref[...], v_ref[...] = node_rows(recv_ref[:, 0, 0:MAIN].T)
    u_of = iota((NU, ND), 0)
    v_of = iota((NV, ND), 0)

    def chunk(i, _):
        at = pl.multiple_of(i * 8, 8)
        u8 = u_ref[pl.ds(at, 8), :]
        v8 = v_ref[pl.ds(at, 8), :]
        rhs = jnp.concatenate(
            [jnp.where(v_of == v8[r : r + 1, :], 1.0, 0.0).astype(BF16) for r in range(8)], axis=1
        )
        picked = dot(fy_ref[...], jnp.concatenate([rhs, rhs], axis=0))
        tiles = [jnp.zeros((8, ND), F32) for _ in range(6)]
        for r in range(8):
            here = u_of == u8[r : r + 1, :]
            for part in range(6):
                block = picked[part * NU : (part + 1) * NU, r * ND : (r + 1) * ND]
                row = jnp.sum(jnp.where(here, block, 0.0), axis=0, keepdims=True)
                tiles[part] = jnp.where(sub == r, row, tiles[part])
        for part in range(6):
            rt_ref[pl.ds(pl.multiple_of(part * CAP + at, 8), 8), :] = tiles[part]
        return 0

    lax.fori_loop(0, CAP // 8, chunk, 0)
    ret_ref[:, 0, 0 : 6 * CAP] = rt_ref[...].T
    ret_ref[:, 0, 6 * CAP : 8 * CAP] = jnp.broadcast_to(moments, (ND, 128))


def shell_of(stiff, force, rim, mass, modulus, live, rims, recv):
    vmem = pl.BlockSpec(memory_space=pltpu.VMEM)
    return pl.pallas_call(
        shell_kernel,
        grid=(1,),
        in_specs=[pl.BlockSpec(memory_space=pltpu.SMEM)]
        + [vmem] * 5
        + [pl.BlockSpec((8, NK), lambda i: (5, 0))] * 2
        + [pl.BlockSpec((8, NK), lambda i: (20, 0))] * 2
        + [vmem],
        out_specs=[vmem, vmem],
        out_shape=[
            jax.ShapeDtypeStruct((3, NU, NV), F32),
            jax.ShapeDtypeStruct((ND, 1, 8 * CAP), F32),
        ],
        scratch_shapes=[
            pltpu.VMEM((6, EU, EV), F32),
            pltpu.VMEM((12, EU, EV), F32),
            pltpu.VMEM((12, EU, EV), F32),
            pltpu.VMEM((3, EU, EV), F32),
            pltpu.VMEM((6 * NU, 2 * NV), BF16),
            pltpu.VMEM((CAP, ND), jnp.int32),
            pltpu.VMEM((CAP, ND), jnp.int32),
            pltpu.VMEM((6 * CAP, ND), F32),
        ],
        compiler_params=pltpu.CompilerParams(vmem_limit_bytes=SMALL_LIMIT),
        name="shell",
    )(stiff, force, rim, mass, modulus, live, *rims, recv)


def scalar_kernel(part_ref, pq_ref, sound_ref):
    row = jnp.sum(part_ref[:, 0, :], axis=0, keepdims=True)
    lane = iota((1, 128), 1)
    m0, m1, m2, m3, over = [
        jnp.sum(jnp.where(lane == i, row, 0.0), axis=1, keepdims=True) for i in range(5)
    ]
    first = m0 / m1
    left_over = first * first * m2 - m0
    ratio = left_over / m0
    gain = 1.0 + ratio
    curve = gain * gain * m1 - 2.0 * gain * first * m2 + first * first * m3
    second = left_over / curve
    sound = (
        (over == 0.0)
        & (left_over > 1e-3 * m0)
        & (curve > 1e-2 * gain * gain * m1)
        & (curve < 1e30)
        & (m1 > 1e-30)
        & (m0 > 1e-30)
    )
    pq_ref[0] = (first + second * gain)[0, 0]
    pq_ref[1] = -(first * second)[0, 0]
    sound_ref[0] = jnp.where(sound, 1, 0)[0, 0]


def scalars_of(back):
    smem = pl.BlockSpec(memory_space=pltpu.SMEM)
    return pl.pallas_call(
        scalar_kernel,
        grid=(1,),
        in_specs=[pl.BlockSpec((ND, 1, 128), lambda i: (0, 0, 3))],
        out_specs=[smem, smem],
        out_shape=[jax.ShapeDtypeStruct((2,), F32), jax.ShapeDtypeStruct((1,), jnp.int32)],
        name="scalars",
    )(back)


OB = 2048
OREC = R // OB
XS = 8
OSTEPS = 32 // XS


def next_kernel(
    pq_ref, back_ref, w_ref, blk_ref, own_ref, rank_ref, f_ref, y_ref, read_ref, xp_ref, xm_ref, yp_ref, ym_ref,
    next_ref, disp_ref,
    x_ref, turned_ref, force_ref, buf_ref, sems,
):
    step = pl.program_id(0)

    def fetch(slab):
        rows = pl.ds(pl.multiple_of(slab * XS * 8, XS * 8), XS * 8)
        return pltpu.make_async_copy(read_ref.at[:, rows, :], buf_ref.at[:, rows, :], sems.at[slab])

    @pl.when(step == 0)
    def _():
        for slab in range(OSTEPS):
            fetch(slab).start()
        p = pq_ref[0]
        q = pq_ref[1]
        back = p * back_ref[:, 0, 0 : 3 * CAP] + q * back_ref[:, 0, 3 * CAP : 6 * CAP]
        turned = back.T * COUPLING
        high = turned.astype(BF16)
        x_ref[:, 0:ND] = high
        x_ref[:, ND : 2 * ND] = (turned - high.astype(F32)).astype(BF16)
        disp_ref[...] = p * f_ref[...] + q * y_ref[...]
        turned_ref[...] = jnp.zeros_like(turned_ref)

    @pl.when(step < OREC)
    def _():
        named = hot(ND, own_ref[...])
        picked = dot(x_ref[...], jnp.concatenate([named, named], axis=0))
        in_slot = iota((CAP, OB), 0) == rank_ref[...]
        w_t = w_ref[...]
        highs, lows = [], []
        for c in range(3):
            moved = jnp.sum(
                jnp.where(in_slot, picked[c * CAP : (c + 1) * CAP, :], 0.0), axis=0, keepdims=True
            )
            part = w_t * moved
            high = part.astype(BF16)
            highs.append(high)
            lows.append((part - high.astype(F32)).astype(BF16))
        in_block = hot(NB, blk_ref[...])
        parts = jnp.concatenate([jnp.concatenate(highs, axis=0), jnp.concatenate(lows, axis=0)], axis=1)
        turned_ref[...] += dot_t(parts, jnp.concatenate([in_block, in_block], axis=1))

    @pl.when(step == OREC)
    def _():
        for c in range(3):
            force_ref[c * NB : (c + 1) * NB, :] = turned_ref[c * NK : (c + 1) * NK, :].T

    @pl.when(step >= OREC)
    def _():
        slab = step - OREC
        fetch(slab).wait()
        sub = iota((8, NK), 0)
        for xx in range(XS):
            x = slab * XS + xx
            rows = pl.ds(pl.multiple_of(x * 8, 8), 8)
            forcing = [
                force_ref[pl.ds(pl.multiple_of(c * NB + x * 8, 8), 8), :] for c in range(3)
            ]
            for q in range(19):
                cx, cy, _ = DIRS[q]
                value = buf_ref[q, rows, :]
                if cx == 1 and xx == 0:
                    value = jnp.where(x == 0, xp_ref[XP.index(q) * 8 : XP.index(q) * 8 + 8, :], value)
                if cx == -1 and xx == XS - 1:
                    value = jnp.where(x == 31, xm_ref[XM.index(q) * 8 : XM.index(q) * 8 + 8, :], value)
                if cy == 1:
                    value = jnp.where(sub == 0, yp_ref[pl.ds(YP.index(q) * 32 + x, 1), :], value)
                if cy == -1:
                    value = jnp.where(sub == 7, ym_ref[pl.ds(YM.index(q) * 32 + x, 1), :], value)
                along = combine(forcing, DIRS[q])
                if along is not None:
                    value = value + (3.0 * WEIGHTS[q]) * along
                next_ref[q, xx * 8 : (xx + 1) * 8, :] = value


def outputs_of(pq, back, weights, block_row, owner_row, rank_row, force, image, read, xp, xm, yp, ym):
    def record(i):
        return jnp.minimum(i, OREC - 1)

    def slab(i):
        return jnp.maximum(i - OREC, 0)

    row_spec = pl.BlockSpec((1, OB), lambda i: (0, record(i)))
    patch = pl.BlockSpec((3, NU, NV), lambda i: (0, 0, 0))
    lines = pl.BlockSpec((19, XS * 8, NK), lambda i: (0, slab(i), 0))
    x_face = pl.BlockSpec((40, NK), lambda i: (0, 0))
    y_face = pl.BlockSpec((160, NK), lambda i: (0, 0))
    return pl.pallas_call(
        next_kernel,
        grid=(OREC + OSTEPS,),
        in_specs=[
            pl.BlockSpec(memory_space=pltpu.SMEM),
            pl.BlockSpec((ND, 1, 8 * CAP), lambda i: (0, 0, 0)),
            pl.BlockSpec((NK, OB), lambda i: (0, record(i))),
            row_spec,
            row_spec,
            row_spec,
            patch,
            patch,
            pl.BlockSpec(memory_space=pl.ANY),
            x_face,
            x_face,
            y_face,
            y_face,
        ],
        out_specs=[lines, patch],
        out_shape=[
            jax.ShapeDtypeStruct((19, NB, NK), F32),
            jax.ShapeDtypeStruct((3, NU, NV), F32),
        ],
        scratch_shapes=[
            pltpu.VMEM((3 * CAP, 2 * ND), BF16),
            pltpu.VMEM((3 * NK, NB), F32),
            pltpu.VMEM((3 * NB, NK), F32),
            pltpu.VMEM((19, NB, NK), F32),
            pltpu.SemaphoreType.DMA((OSTEPS,)),
        ],
        compiler_params=pltpu.CompilerParams(vmem_limit_bytes=VMEM_LIMIT),
        name="outputs",
    )(pq, back, weights, block_row, owner_row, rank_row, force, image, read, xp, xm, yp, ym)


def pass_on(x, axis, shift):
    count = lax.axis_size(axis)
    return lax.ppermute(x, axis, [(i, (i + shift) % count) for i in range(count)])


def padded(field):
    for axis, dim in (("gx", 1), ("gy", 2)):
        size = field.shape[dim]
        head = lax.slice_in_dim(field, 0, 1, axis=dim)
        tail = lax.slice_in_dim(field, size - 1, size, axis=dim)
        field = jnp.concatenate([pass_on(tail, axis, 1), field, pass_on(head, axis, -1)], axis=dim)
    return field


def operate(field, mass, modulus, live, stiff):
    static = padded(jnp.stack([modulus, live.astype(F32)]))
    wide = padded(field)

    def corners(a):
        return a[..., :-1, :-1], a[..., 1:, :-1], a[..., :-1, 1:], a[..., 1:, 1:]

    c0, c1, c2, c3 = corners(static[0])
    scale = static[1, :-1, :-1] * (c0 + c1 + c2 + c3) * 0.25
    vector = jnp.concatenate(corners(wide), axis=0)
    result = scale[None] * jnp.einsum("kl,lab->kab", stiff, vector, precision=lax.Precision.HIGHEST)
    return (
        mass[None] * field
        + result[0:3, 1:, 1:]
        + result[3:6, :-1, 1:]
        + result[6:9, 1:, :-1]
        + result[9:12, :-1, :-1]
    )


def rim_of(force):
    before = pass_on(force[:, NU - 1 : NU, :], "gx", 1)
    after = pass_on(force[:, 0:2, :], "gx", -1)
    tall = jnp.concatenate([force, after, before], axis=1)
    left = pass_on(tall[:, :, NV - 1 : NV], "gy", 1)
    right = pass_on(tall[:, :, 0:2], "gy", -1)
    gap = jnp.zeros((3, EV - NV - 3), F32)
    rows = [
        jnp.concatenate([tall[:, r], right[:, r], gap, left[:, r]], axis=1) for r in (NU + 2, NU, NU + 1)
    ]
    beside = [
        jnp.concatenate([column[:, 0:NU], jnp.zeros((3, EV - NU), F32)], axis=1)
        for column in (left[:, :, 0], right[:, :, 0], right[:, :, 1])
    ]
    empty = jnp.zeros((3, EV), F32)
    return jnp.stack(rows + beside + [empty, empty], axis=1)


def exchange(x):
    return lax.all_to_all(x, ALL, 0, 0, tiled=True)


def per_device(populations, mass, modulus, live, stiff, rec_block, rec_owner, rec_node, weights):
    pops = populations.reshape(19, NB, NK)
    block_row = rec_block.reshape(1, R)
    owner_row = rec_owner.reshape(1, R)
    node_row = rec_node.reshape(1, R)

    send, rank_row, turned, xp, xm, yp, ym = loads_to_send(
        pops, weights, block_row, owner_row, node_row, mass, modulus, live
    )
    xp = pass_on(xp, "gx", 1)
    xm = pass_on(xm, "gx", -1)
    recv = exchange(send)
    yp, ym = sides_of(mass, modulus, live, xp, xm, yp, ym)
    yp = pass_on(yp, "gy", 1)
    ym = pass_on(ym, "gy", -1)
    rims = (xp, xm, yp, ym)

    force, rim = force_of(recv)
    image, ret = shell_of(stiff, force, rim, mass, modulus, live, rims, recv)
    ret, pops = lax.optimization_barrier((ret, pops))
    back = exchange(ret)
    read = collide_and_run(pops)
    back, read = lax.optimization_barrier((back, read))
    pq, sound = scalars_of(back)

    def quick(operands):
        return operands[0:3]

    def careful(operands):
        _, _, _, force, mass, modulus, live, stiff, rims, recv = operands
        image, ret = shell_of(stiff, force, rim_of(force), mass, modulus, live, rims, recv)
        back = exchange(ret)
        start = lax.psum(jnp.sum(force * force), ALL)
        first = start / lax.psum(jnp.sum(force * image), ALL)
        residual = force - first * image
        norm = lax.psum(jnp.sum(residual * residual), ALL)
        ratio = norm / start
        direction = residual + ratio * force
        along = operate(direction, mass, modulus, live, stiff)
        second = norm / lax.psum(jnp.sum(direction * along), ALL)
        return jnp.stack([first + second * (1.0 + ratio), -(first * second)]), image, back

    pq, image, back = lax.cond(
        sound[0] == 1, quick, careful, (pq, image, back, force, mass, modulus, live, stiff, rims, recv)
    )

    populations_next, displacement = outputs_of(
        pq, back, turned, block_row, owner_row, rank_row, force, image, read, xp, xm, yp, ym
    )
    return populations_next.reshape(19, 32, 8, NK), displacement


def solution(mesh):
    return jax.shard_map(
        per_device,
        mesh=mesh,
        in_specs=(
            P(None, "gx", "gy", None),
            P("gx", "gy"),
            P("gx", "gy"),
            P("gx", "gy"),
            P(),
            P(ALL),
            P(ALL, None),
            P(ALL),
            P(ALL, None),
        ),
        out_specs=(P(None, "gx", "gy", None), P(None, "gx", "gy")),
        check_vma=False,
    )
```

```python
import jax
import jax.numpy as jnp
from jax import lax
from jax.experimental import pallas as pl
from jax.experimental.pallas import tpu as pltpu
from jax.sharding import PartitionSpec as P

F32 = jnp.float32
BF16 = jnp.bfloat16
ALL = ("gx", "gy")
VMEM_LIMIT = 60 * 1024 * 1024
SMALL_LIMIT = 16 * 1024 * 1024

DIRS = (
    (0, 0, 0),
    (1, 0, 0),
    (-1, 0, 0),
    (0, 1, 0),
    (0, -1, 0),
    (0, 0, 1),
    (0, 0, -1),
    (1, 1, 0),
    (-1, -1, 0),
    (1, -1, 0),
    (-1, 1, 0),
    (1, 0, 1),
    (-1, 0, -1),
    (1, 0, -1),
    (-1, 0, 1),
    (0, 1, 1),
    (0, -1, -1),
    (0, 1, -1),
    (0, -1, 1),
)
WEIGHTS = (1.0 / 3.0,) + (1.0 / 18.0,) * 6 + (1.0 / 36.0,) * 12
RATE = 1.25
COUPLING = 0.1
XP = tuple(q for q in range(19) if DIRS[q][0] == 1)
XM = tuple(q for q in range(19) if DIRS[q][0] == -1)
YP = tuple(q for q in range(19) if DIRS[q][1] == 1)
YM = tuple(q for q in range(19) if DIRS[q][1] == -1)

R = 4096
NB = 256
NK = 256
ND = 128
CAP = 64
RIM = 32
MAIN = 4 * CAP
NU, NV = 64, 128
RB = 1024
EU, EV = 72, 256


def iota(shape, dim):
    return lax.broadcasted_iota(jnp.int32, shape, dim)


def halves(x):
    high = x.astype(BF16).astype(F32)
    return high, x - high


def combine(fields, direction):
    total = None
    for axis in range(3):
        if direction[axis] != 0:
            term = fields[axis] if direction[axis] == 1 else -fields[axis]
            total = term if total is None else total + term
    return total


def dot_t(a, b):
    return lax.dot_general(a, b, (((1,), (1,)), ((), ())), preferred_element_type=F32)


def dot(a, b):
    return lax.dot_general(a, b, (((1,), (0,)), ((), ())), preferred_element_type=F32)


def relaxed_of(pops, wanted):
    density = pops[0]
    for q in range(1, 19):
        density = density + pops[q]
    inverse = 1.0 / density
    velocity = []
    for axis in range(3):
        total = None
        for q in range(1, 19):
            if DIRS[q][axis] != 0:
                term = pops[q] if DIRS[q][axis] == 1 else -pops[q]
                total = term if total is None else total + term
        velocity.append(total * inverse)
    squared = velocity[0] * velocity[0] + velocity[1] * velocity[1] + velocity[2] * velocity[2]
    base = 1.0 - 1.5 * squared
    result = []
    for q in wanted:
        along = combine(velocity, DIRS[q])
        bracket = base if along is None else base + along * (3.0 + 4.5 * along)
        relaxed = pops[q] - RATE * (pops[q] - (WEIGHTS[q] * density) * bracket)
        if DIRS[q][2] != 0:
            relaxed = pltpu.roll(relaxed, 1 if DIRS[q][2] == 1 else NK - 1, 1)
        result.append(relaxed)
    return result


def turned_y(value, cy):
    return value if cy == 0 else pltpu.roll(value, 1 if cy == 1 else 7, 0)


XMSG = 48
YMSG = 168


CHUNKS = 4
CROWS = NB // CHUNKS
RSTEPS = R // RB


def match(count, row):
    lanes = row.shape[1]
    column = iota((count, 128), 0).astype(F32).astype(BF16)
    wanted = jnp.broadcast_to(row.astype(F32).astype(BF16), (count, lanes))
    return jnp.concatenate([column] * (lanes // 128), axis=1) == wanted


def hot(count, row):
    shape = (count, row.shape[1])
    return jnp.where(match(count, row), jnp.ones(shape, BF16), jnp.zeros(shape, BF16))


def pick(mask, row):
    return jnp.where(mask, jnp.broadcast_to(row, mask.shape), jnp.zeros(mask.shape, BF16))


def rim_rows(own, node):
    u, v = node >> 7, node & 127
    ox, oy = own >> 5, own & 31
    su = jnp.where(u == NU - 1, 1, jnp.where(u <= 1, -1, 0))
    sv = jnp.where(v == NV - 1, 1, jnp.where(v <= 1, -1, 0))
    ox2, oy2 = (ox + su) & 3, (oy + sv) & 31
    dests = [
        jnp.where(su != 0, ox2 * 32 + oy, -1),
        jnp.where(sv != 0, ox * 32 + oy2, -1),
        jnp.where((su != 0) & (sv != 0), ox2 * 32 + oy2, -1),
    ]
    row = jnp.where(u == NU - 1, 0, u + 1) * EV
    codes = [
        row + v,
        jnp.where(v == NV - 1, 3, v + 4) * EV + u,
        row + jnp.where(v == NV - 1, EV - 1, v + NV),
    ]
    return dests, codes


def load_kernel(
    pop_hbm, w_hbm, blk_ref, own_all_ref, node_all_ref, own_ref, node_ref, mass_ref, mod_ref, live_ref,
    send_ref, rank_ref, wt_ref, xp_ref, xm_ref, yp_ref, ym_ref,
    pop_ref, sems, w_ref, w_sems, m_ref, mt_ref, tri_ref, carry_ref, dest_ref, code_ref, place_ref, over_ref, main_ref, rims_ref,
):
    step = pl.program_id(0)

    def fetch(part):
        rows = pl.ds(part * CROWS, CROWS)
        return pltpu.make_async_copy(pop_hbm.at[:, rows, :], pop_ref.at[:, rows, :], sems.at[part])

    def fetch_w(part):
        rows = pl.ds(pl.multiple_of(part * RB, RB), RB)
        return pltpu.make_async_copy(w_hbm.at[rows, :], w_ref.at[rows, :], w_sems.at[part])

    @pl.when(step == 0)
    def _():
        for part in range(CHUNKS):
            fetch(part).start()
        before = (iota((256, 256), 0) < iota((256, 256), 1)).astype(F32)
        tri_ref[:, 0:256] = before.astype(BF16)
        tri_ref[:, 256:512] = jnp.ones((256, 256), BF16)
        carry_ref[...] = jnp.zeros_like(carry_ref)
        main_ref[...] = jnp.zeros_like(main_ref)
        rims_ref[...] = jnp.zeros_like(rims_ref)
        over_ref[...] = jnp.zeros_like(over_ref)
        dests, codes = rim_rows(own_all_ref[...], node_all_ref[...])
        for i in range(3):
            dest_ref[i : i + 1, :] = dests[i]
            code_ref[i : i + 1, :] = codes[i].astype(F32)
        for k in range(R // 256):
            cols = slice(k * 256, (k + 1) * 256)
            device = iota((ND, 256), 0)
            hots = [device == own_all_ref[:, cols]] + [device == dest_ref[i : i + 1, cols] for i in range(3)]
            main = jnp.where(hots[0], 1.0, 0.0).astype(BF16)
            rims = jnp.where(hots[1] | hots[2] | hots[3], 1.0, 0.0).astype(BF16)
            counts = dot(jnp.concatenate([main, rims], axis=0), tri_ref[...])
            upto = counts[:, 0:256] + carry_ref[...]
            carry_ref[...] += counts[:, 256:512]
            rank = jnp.sum(jnp.where(hots[0], upto[0:ND], 0.0), axis=0, keepdims=True)
            rank_ref[:, cols] = rank.astype(jnp.int32)
            for i in range(3):
                place = jnp.sum(jnp.where(hots[i + 1], upto[ND : 2 * ND], 0.0), axis=0, keepdims=True)
                over_ref[...] = jnp.maximum(over_ref[...], place)
                place_ref[i : i + 1, cols] = jnp.where(place < RIM - 1, place, 2.0 * RIM).astype(jnp.int32)

        def rows_of(i, _):
            rows = pl.ds(pl.multiple_of(i * 8, 8), 8)
            pops = [pop_ref[q, rows, :] for q in range(1, 19)]
            for axis in range(3):
                total = None
                for q in range(1, 19):
                    if DIRS[q][axis] != 0:
                        term = pops[q - 1] if DIRS[q][axis] == 1 else -pops[q - 1]
                        total = term if total is None else total + term
                m_ref[axis, rows, :] = total
            return 0

        sub = iota((8, NK), 0)
        for part in range(CHUNKS):
            fetch(part).wait()
            fetch_w(part).start()
            lax.fori_loop(part * CROWS // 8, (part + 1) * CROWS // 8, rows_of, 0, unroll=2)
            for face_ref, dirs, y in ((yp_ref, YP, 7), (ym_ref, YM, 0)):
                pops = []
                for q in range(19):
                    tile = None
                    for i in range(8):
                        row = jnp.broadcast_to(pop_ref[q, pl.ds(part * 64 + i * 8 + y, 1), :], (8, NK))
                        tile = row if tile is None else jnp.where(sub == i, row, tile)
                    pops.append(tile)
                values = relaxed_of(pops, dirs)
                for i in range(5):
                    face_ref[i * 32 + part * 8 : i * 32 + part * 8 + 8, :] = values[i]
        for face_ref, dirs in ((yp_ref, YP), (ym_ref, YM)):
            for i, q in enumerate(dirs):
                if DIRS[q][0] != 0:
                    face = face_ref[i * 32 : i * 32 + 32, :]
                    face_ref[i * 32 : i * 32 + 32, :] = pltpu.roll(face, 1 if DIRS[q][0] == 1 else 31, 0)
        for face_ref, dirs, x in ((xp_ref, XP, 31), (xm_ref, XM, 0)):
            values = relaxed_of([pop_ref[q, x * 8 : x * 8 + 8, :] for q in range(19)], dirs)
            for i, q in enumerate(dirs):
                face_ref[i * 8 : i * 8 + 8, :] = turned_y(values[i], DIRS[q][1])
            face_ref[40:XMSG, :] = jnp.zeros((XMSG - 40, NK), F32)
        for i, field in enumerate([mass_ref[...], mod_ref[...], live_ref[...].astype(F32)]):
            xp_ref[40 + i : 41 + i, 0:NV] = field[NU - 1 : NU, :]
            xm_ref[40 + 2 * i : 42 + 2 * i, 0:NV] = field[0:2, :]
        for axis in range(3):
            turned = m_ref[axis].T
            high = turned.astype(BF16)
            at = slice(axis * NK, (axis + 1) * NK)
            mt_ref[at, 0:NB] = high
            mt_ref[at, NB : 2 * NB] = (turned - high.astype(F32)).astype(BF16)

    @pl.when(step >= 1)
    def _():
        here = pl.ds(pl.multiple_of((step - 1) * RB, RB), RB)
        fetch_w(step - 1).wait()
        w_t = w_ref[here, :].T
        in_block = hot(NB, blk_ref[...])
        picked = dot(mt_ref[...], jnp.concatenate([in_block, in_block], axis=0))
        values = [
            jnp.sum(picked[axis * NK : (axis + 1) * NK, :] * w_t, axis=0, keepdims=True) for axis in range(3)
        ]

        def sides(value):
            return [side.astype(BF16) for side in halves(value)]

        parts = [sides(value) for value in values]

        def placed(count, slot, code):
            mask = match(count, slot)
            both = [pick(mask, part[side]) for side in range(2) for part in parts + [sides(code)]]
            return jnp.concatenate(both, axis=0)

        packed = placed(CAP, rank_ref[:, here], node_ref[...].astype(F32))
        main_ref[...] += dot_t(packed, hot(ND, own_ref[...]))
        packed = [placed(RIM, place_ref[i : i + 1, here], code_ref[i : i + 1, here]) for i in range(3)]
        named = [hot(ND, dest_ref[i : i + 1, here]) for i in range(3)]
        rims_ref[...] += dot_t(jnp.concatenate(packed, axis=1), jnp.concatenate(named, axis=1))
        wt_ref[...] = w_t

    @pl.when(step == RSTEPS)
    def _():
        most = jnp.max(over_ref[...], axis=1, keepdims=True)
        flag = jnp.where(most >= RIM - 1, 1.0, 0.0)
        send_ref[:, 0, 0:MAIN] = (main_ref[0:MAIN, :] + main_ref[MAIN : 2 * MAIN, :]).T
        tail = (rims_ref[0 : 4 * RIM, :] + rims_ref[4 * RIM : 8 * RIM, :]).T
        send_ref[:, 0, MAIN : MAIN + 4 * RIM] = jnp.where(iota((ND, 4 * RIM), 1) == 4 * RIM - 1, flag, tail)


def loads_to_send(pops, weights, block_row, owner_row, node_row, mass, modulus, live):
    def record(i):
        return jnp.maximum(i - 1, 0)

    row_spec = pl.BlockSpec((1, RB), lambda i: (0, record(i)))
    all_rows = pl.BlockSpec((1, R), lambda i: (0, 0))

    def whole(*shape):
        return pl.BlockSpec(shape, lambda i: (0, 0))

    return pl.pallas_call(
        load_kernel,
        grid=(1 + RSTEPS,),
        in_specs=[
            pl.BlockSpec(memory_space=pltpu.HBM),
            pl.BlockSpec(memory_space=pltpu.HBM),
            row_spec,
            all_rows,
            all_rows,
            row_spec,
            row_spec,
            whole(NU, NV),
            whole(NU, NV),
            whole(NU, NV),
        ],
        out_specs=[
            pl.BlockSpec((ND, 1, MAIN + 4 * RIM), lambda i: (0, 0, 0)),
            all_rows,
            pl.BlockSpec((NK, RB), lambda i: (0, record(i))),
            whole(XMSG, NK),
            whole(XMSG, NK),
            whole(160, NK),
            whole(160, NK),
        ],
        out_shape=[
            jax.ShapeDtypeStruct((ND, 1, MAIN + 4 * RIM), F32),
            jax.ShapeDtypeStruct((1, R), jnp.int32),
            jax.ShapeDtypeStruct((NK, R), F32),
            jax.ShapeDtypeStruct((XMSG, NK), F32),
            jax.ShapeDtypeStruct((XMSG, NK), F32),
            jax.ShapeDtypeStruct((160, NK), F32),
            jax.ShapeDtypeStruct((160, NK), F32),
        ],
        scratch_shapes=[
            pltpu.VMEM((19, NB, NK), F32),
            pltpu.SemaphoreType.DMA((CHUNKS,)),
            pltpu.VMEM((R, NK), F32),
            pltpu.SemaphoreType.DMA((RSTEPS,)),
            pltpu.VMEM((3, NB, NK), F32),
            pltpu.VMEM((3 * NK, 2 * NB), BF16),
            pltpu.VMEM((256, 512), BF16),
            pltpu.VMEM((2 * ND, 256), F32),
            pltpu.VMEM((8, R), jnp.int32),
            pltpu.VMEM((8, R), F32),
            pltpu.VMEM((8, R), jnp.int32),
            pltpu.VMEM((1, 256), F32),
            pltpu.VMEM((2 * MAIN, ND), F32),
            pltpu.VMEM((8 * RIM, ND), F32),
        ],
        compiler_params=pltpu.CompilerParams(vmem_limit_bytes=VMEM_LIMIT),
        name="loads",
    )(pops, weights, block_row, owner_row, node_row, owner_row, node_row, mass, modulus, live)


LINES = 8


def collide_kernel(pop_hbm, out_hbm, pop_ref, read_ref, in_sems, out_sems):
    chunks = 32 // LINES

    def fetch(part):
        rows = pl.ds(part * LINES * 8, LINES * 8)
        return pltpu.make_async_copy(pop_hbm.at[:, rows, :], pop_ref.at[:, rows, :], in_sems.at[part])

    def store(part):
        first = max(part * LINES - 1, 0) * 8
        last = NB if part == chunks - 1 else (part * LINES + LINES - 1) * 8
        rows = pl.ds(first, last - first)
        kept = pl.ds(first + 8, last - first)
        return pltpu.make_async_copy(read_ref.at[:, kept, :], out_hbm.at[:, rows, :], out_sems.at[part])

    def line(x, _):
        rows = pl.ds(pl.multiple_of(x * 8, 8), 8)
        values = relaxed_of([pop_ref[q, rows, :] for q in range(19)], range(19))
        for q in range(19):
            cx, cy, _ = DIRS[q]
            to = pl.ds(pl.multiple_of((x + cx + 1) * 8, 8), 8)
            read_ref[q, to, :] = turned_y(values[q], cy)
        return 0

    for part in range(chunks):
        fetch(part).start()
    for q in XP:
        read_ref[q, 8:16, :] = jnp.zeros((8, NK), F32)
    for q in XM:
        read_ref[q, NB : NB + 8, :] = jnp.zeros((8, NK), F32)
    for part in range(chunks):
        fetch(part).wait()
        lax.fori_loop(part * LINES, (part + 1) * LINES, line, 0, unroll=4)
        store(part).start()
    for part in range(chunks):
        store(part).wait()


def collide_and_run(pops):
    return pl.pallas_call(
        collide_kernel,
        in_specs=[pl.BlockSpec(memory_space=pltpu.HBM)],
        out_specs=pl.BlockSpec(memory_space=pltpu.HBM),
        out_shape=jax.ShapeDtypeStruct((19, NB, NK), F32),
        scratch_shapes=[
            pltpu.VMEM((19, NB, NK), F32),
            pltpu.VMEM((19, NB + 16, NK), F32),
            pltpu.SemaphoreType.DMA((32 // LINES,)),
            pltpu.SemaphoreType.DMA((32 // LINES,)),
        ],
        compiler_params=pltpu.CompilerParams(vmem_limit_bytes=VMEM_LIMIT),
        name="collide",
    )(pops)


def node_rows(recv_t):
    node = recv_t[3 * CAP : MAIN, :].astype(jnp.int32)
    return node >> 8, node & 255


def force_kernel(recv_ref, f_ref, rim_ref, u_ref, v_ref, hl_ref, ru_ref, rv_ref, rhl_ref):
    recv_t = recv_ref[:, 0, :].T
    u_ref[...], v_ref[...] = node_rows(recv_t)
    high, low = halves(recv_t[0 : 3 * CAP, :])
    hl_ref[0 : 3 * CAP, :] = high
    hl_ref[3 * CAP : 6 * CAP, :] = low
    code = recv_t[MAIN + 3 * RIM : MAIN + 4 * RIM, :].astype(jnp.int32)
    ru_ref[...] = code >> 8
    rv_ref[...] = code & 255
    high, low = halves(recv_t[MAIN : MAIN + 3 * RIM, :])
    rhl_ref[0 : 3 * RIM, :] = high
    rhl_ref[3 * RIM : 6 * RIM, :] = low

    def chunk_of(rows_ref, cols_ref, vals_ref, slots, height, width):
        def chunk(i, acc):
            at = pl.multiple_of(i * 8, 8)
            u8 = rows_ref[pl.ds(at, 8), :]
            v8 = cols_ref[pl.ds(at, 8), :]
            vals = [vals_ref[pl.ds(pl.multiple_of(part * slots + at, 8), 8), :].astype(BF16) for part in range(6)]
            lhs, rhs = [], []
            for r in range(8):
                here = match(max(height, 16), u8[r : r + 1, :])
                lhs.append(jnp.concatenate([pick(here, vals[part][r : r + 1, :]) for part in range(6)], axis=0))
                rhs.append(hot(width, v8[r : r + 1, :]))
            return acc + dot_t(jnp.concatenate(lhs, axis=1), jnp.concatenate(rhs, axis=1))

        return lax.fori_loop(0, slots // 8, chunk, jnp.zeros((6 * max(height, 16), width), F32), unroll=2)

    acc = chunk_of(u_ref, v_ref, hl_ref, CAP, NU // 2, 2 * NV)
    for c in range(3):
        pair = acc[c * 32 : (c + 1) * 32, :] + acc[(3 + c) * 32 : (4 + c) * 32, :]
        f_ref[c, pl.ds(0, 32, stride=2), :] = pair[:, 0:NV]
        f_ref[c, pl.ds(1, 32, stride=2), :] = pair[:, NV : 2 * NV]
    acc = chunk_of(ru_ref, rv_ref, rhl_ref, RIM, 8, EV)
    for c in range(3):
        rim_ref[c] = acc[c * 16 : c * 16 + 8, :] + acc[(3 + c) * 16 : (3 + c) * 16 + 8, :]


def force_of(recv):
    return pl.pallas_call(
        force_kernel,
        out_shape=[jax.ShapeDtypeStruct((3, NU, NV), F32), jax.ShapeDtypeStruct((3, 8, EV), F32)],
        scratch_shapes=[
            pltpu.VMEM((CAP, ND), jnp.int32),
            pltpu.VMEM((CAP, ND), jnp.int32),
            pltpu.VMEM((6 * CAP, ND), F32),
            pltpu.VMEM((RIM, ND), jnp.int32),
            pltpu.VMEM((RIM, ND), jnp.int32),
            pltpu.VMEM((6 * RIM, ND), F32),
        ],
        compiler_params=pltpu.CompilerParams(vmem_limit_bytes=SMALL_LIMIT),
        name="force",
    )(recv)


def rim_tile(i, low, high):
    sub = iota((8, 128), 0)
    tile = jnp.where(sub == 0, high[2 * i : 2 * i + 1, :], 0.0)
    tile = jnp.where(sub == 1, high[2 * i + 1 : 2 * i + 2, :], tile)
    return jnp.where(sub == 7, low[i : i + 1, :], tile)


def side_kernel(mass_ref, mod_ref, live_ref, xp_ref, xm_ref, yp_ref, ym_ref, to_p_ref, to_m_ref):
    to_p_ref[0:160, :] = yp_ref[...]
    to_m_ref[0:160, :] = ym_ref[...]
    for q, line, from_ref in ((7, 0, xp_ref), (10, 31, xm_ref)):
        face = (XP if line == 0 else XM).index(q) * 8
        at = YP.index(q) * 32 + line
        to_p_ref[at : at + 1, :] = from_ref[face : face + 1, :]
    for q, line, from_ref in ((9, 0, xp_ref), (8, 31, xm_ref)):
        face = (XP if line == 0 else XM).index(q) * 8 + 7
        at = YM.index(q) * 32 + line
        to_m_ref[at : at + 1, :] = from_ref[face : face + 1, :]
    to_p_ref[160:YMSG, :] = jnp.zeros((YMSG - 160, NK), F32)
    to_m_ref[160:YMSG, :] = jnp.zeros((YMSG - 160, NK), F32)
    low, high = xp_ref[40:XMSG, 0:NV], xm_ref[40:XMSG, 0:NV]
    for i, field in enumerate([mass_ref[...], mod_ref[...], live_ref[...].astype(F32)]):
        tall = jnp.concatenate([field, rim_tile(i, low, high), jnp.zeros((128 - EU, 128), F32)], axis=0)
        turned = tall.T
        to_p_ref[160 + i : 161 + i, 0:128] = turned[127:128, :]
        to_m_ref[160 + 2 * i : 162 + 2 * i, 0:128] = turned[0:2, :]


def sides_of(mass, modulus, live, xp, xm, yp, ym):
    return pl.pallas_call(
        side_kernel,
        out_shape=[jax.ShapeDtypeStruct((YMSG, NK), F32), jax.ShapeDtypeStruct((YMSG, NK), F32)],
        compiler_params=pltpu.CompilerParams(vmem_limit_bytes=VMEM_LIMIT),
        name="sides",
    )(mass, modulus, live, xp, xm, yp, ym)


def shell_kernel(
    stiff_ref, f_ref, rim_ref, mass_ref, mod_ref, live_ref, ulow_ref, uhigh_ref, vlow_ref, vhigh_ref, recv_ref,
    y_ref, ret_ref,
    e_ref, c_ref, g_ref, y_ext_ref, fy_ref, u_ref, v_ref, rt_ref,
):
    sub = iota((8, 128), 0)

    def columns(near, far, before):
        first = jnp.where(sub == 0, near, 0.0)
        first = jnp.where(sub == 1, far, first)
        last = jnp.where(sub == 7, before, 0.0)
        return jnp.concatenate([first, jnp.zeros((112, 128), F32), last], axis=0).T

    for i, field in enumerate([mass_ref[...], mod_ref[...], live_ref[...].astype(F32)]):
        e_ref[3 + i, 0:NU, 0:NV] = field
        e_ref[3 + i, NU:EU, 0:NV] = rim_tile(i, ulow_ref[:, 0:NV], uhigh_ref[:, 0:NV])
        side = columns(
            vhigh_ref[2 * i : 2 * i + 1, 0:128],
            vhigh_ref[2 * i + 1 : 2 * i + 2, 0:128],
            vlow_ref[i : i + 1, 0:128],
        )
        e_ref[3 + i, :, NV:EV] = side[0:EU, :]
    wide = iota((8, EV), 0)
    for i in range(3):
        e_ref[i, 0:NU, 0:NV] = f_ref[i]
        tile = jnp.where(wide == 0, rim_ref[i, 1:2, :], 0.0)
        tile = jnp.where(wide == 1, rim_ref[i, 2:3, :], tile)
        e_ref[i, NU:EU, :] = jnp.where(wide == 7, rim_ref[i, 0:1, :], tile)
        side = columns(rim_ref[i, 4:5, 0:128], rim_ref[i, 5:6, 0:128], rim_ref[i, 3:4, 0:128])
        e_ref[i, 0:NU, NV:EV] = side[0:NU, :]

    def up(x):
        return pltpu.roll(x, EU - 1, 0)

    def right(x):
        return pltpu.roll(x, EV - 1, 1)

    def down(x):
        return pltpu.roll(x, 1, 0)

    def left(x):
        return pltpu.roll(x, 1, 1)

    mod = e_ref[4]
    mod = mod + up(mod)
    e_ref[5] = e_ref[5] * (mod + right(mod)) * 0.25
    for c in range(3):
        field = e_ref[c]
        moved = up(field)
        c_ref[c] = field
        c_ref[3 + c] = moved
        c_ref[6 + c] = right(field)
        c_ref[9 + c] = right(moved)

    def cells(t, _):
        rows = pl.ds(pl.multiple_of(t * 8, 8), 8)
        corner = [c_ref[k, rows, :] for k in range(12)]
        scale = e_ref[5, rows, :]
        for k in range(12):
            total = stiff_ref[k, 0] * corner[0]
            for m in range(1, 12):
                total = total + stiff_ref[k, m] * corner[m]
            g_ref[k, rows, :] = scale * total
        return 0

    lax.fori_loop(0, EU // 8, cells, 0)
    mass = e_ref[3]
    for c in range(3):
        spread = g_ref[c] + down(g_ref[3 + c])
        beside = g_ref[6 + c] + down(g_ref[9 + c])
        y_ext_ref[c] = mass * e_ref[c] + spread + left(beside)
        y_ref[c] = y_ext_ref[c, 0:NU, 0:NV]
    for c in range(3):
        field = y_ext_ref[c]
        moved = up(field)
        c_ref[c] = field
        c_ref[3 + c] = moved
        c_ref[6 + c] = right(field)
        c_ref[9 + c] = right(moved)

    def energy(t, sums):
        rows = pl.ds(pl.multiple_of(t * 8, 8), 8)
        corner = [c_ref[k, rows, 0:NV] for k in range(12)]
        total = None
        for k in range(12):
            inner = stiff_ref[k, 0] * corner[0]
            for m in range(1, 12):
                inner = inner + stiff_ref[k, m] * corner[m]
            total = corner[k] * inner if total is None else total + corner[k] * inner
        m3 = e_ref[5, rows, 0:NV] * total
        m0, m1, m2 = None, None, None
        for c in range(3):
            f = e_ref[c, rows, 0:NV]
            y = corner[c]
            m0 = f * f if m0 is None else m0 + f * f
            m1 = f * y if m1 is None else m1 + f * y
            m2 = y * y if m2 is None else m2 + y * y
        m3 = m3 + e_ref[3, rows, 0:NV] * m2
        return tuple(s + m for s, m in zip(sums, (m0, m1, m2, m3)))

    zero = jnp.zeros((8, NV), F32)
    sums = lax.fori_loop(0, NU // 8, energy, (zero, zero, zero, zero))
    lane = iota((1, 128), 1)
    moments = jnp.zeros((1, 128), F32)
    for i in range(4):
        whole = jnp.sum(jnp.sum(sums[i], axis=0, keepdims=True), axis=1, keepdims=True)
        moments = jnp.where(lane == i, whole, moments)
    over = jnp.max(recv_ref[:, 0, MAIN + 3 * RIM :], axis=0, keepdims=True)[:, RIM - 1 :]
    moments = jnp.where(lane == 4, over, moments)

    for c in range(3):
        for part, field in ((c, f_ref), (3 + c, y_ref)):
            rows = slice(part * 32, part * 32 + 32)
            for odd in range(2):
                value = field[c, pl.ds(odd, 32, stride=2), :]
                high = value.astype(BF16)
                fy_ref[rows, odd * NV : (odd + 1) * NV] = high
                fy_ref[rows, (2 + odd) * NV : (3 + odd) * NV] = (value - high.astype(F32)).astype(BF16)
    u_ref[...], v_ref[...] = node_rows(recv_ref[:, 0, 0:MAIN].T)
    u_of = iota((NU // 2, ND), 0)

    def chunk(i, _):
        at = pl.multiple_of(i * 8, 8)
        u8 = u_ref[pl.ds(at, 8), :]
        v8 = v_ref[pl.ds(at, 8), :]
        rhs = jnp.concatenate([hot(2 * NV, v8[r : r + 1, :]) for r in range(8)], axis=1)
        picked = dot(fy_ref[...], jnp.concatenate([rhs, rhs], axis=0))
        tiles = [jnp.zeros((8, ND), F32) for _ in range(6)]
        for r in range(8):
            here = u_of == u8[r : r + 1, :]
            for part in range(6):
                block = picked[part * 32 : (part + 1) * 32, r * ND : (r + 1) * ND]
                row = jnp.sum(jnp.where(here, block, 0.0), axis=0, keepdims=True)
                tiles[part] = jnp.where(sub == r, row, tiles[part])
        for part in range(6):
            rt_ref[pl.ds(pl.multiple_of(part * CAP + at, 8), 8), :] = tiles[part]
        return 0

    lax.fori_loop(0, CAP // 8, chunk, 0, unroll=2)
    ret_ref[:, 0, 0 : 6 * CAP] = rt_ref[...].T
    ret_ref[:, 0, 6 * CAP : 8 * CAP] = jnp.broadcast_to(moments, (ND, 128))


def shell_of(stiff, force, rim, mass, modulus, live, rims, recv):
    vmem = pl.BlockSpec(memory_space=pltpu.VMEM)
    return pl.pallas_call(
        shell_kernel,
        grid=(1,),
        in_specs=[pl.BlockSpec(memory_space=pltpu.SMEM)]
        + [vmem] * 5
        + [pl.BlockSpec((8, NK), lambda i: (5, 0))] * 2
        + [pl.BlockSpec((8, NK), lambda i: (20, 0))] * 2
        + [vmem],
        out_specs=[vmem, vmem],
        out_shape=[
            jax.ShapeDtypeStruct((3, NU, NV), F32),
            jax.ShapeDtypeStruct((ND, 1, 8 * CAP), F32),
        ],
        scratch_shapes=[
            pltpu.VMEM((6, EU, EV), F32),
            pltpu.VMEM((12, EU, EV), F32),
            pltpu.VMEM((12, EU, EV), F32),
            pltpu.VMEM((3, EU, EV), F32),
            pltpu.VMEM((6 * NU // 2, 4 * NV), BF16),
            pltpu.VMEM((CAP, ND), jnp.int32),
            pltpu.VMEM((CAP, ND), jnp.int32),
            pltpu.VMEM((6 * CAP, ND), F32),
        ],
        compiler_params=pltpu.CompilerParams(vmem_limit_bytes=SMALL_LIMIT),
        name="shell",
    )(stiff, force, rim, mass, modulus, live, *rims, recv)


def scalar_kernel(part_ref, pq_ref, sound_ref):
    row = jnp.sum(part_ref[:, 0, :], axis=0, keepdims=True)
    lane = iota((1, 128), 1)
    m0, m1, m2, m3, over = [
        jnp.sum(jnp.where(lane == i, row, 0.0), axis=1, keepdims=True) for i in range(5)
    ]
    first = m0 / m1
    left_over = first * first * m2 - m0
    ratio = left_over / m0
    gain = 1.0 + ratio
    curve = gain * gain * m1 - 2.0 * gain * first * m2 + first * first * m3
    second = left_over / curve
    sound = (
        (over == 0.0)
        & (left_over > 1e-3 * m0)
        & (curve > 1e-2 * gain * gain * m1)
        & (curve < 1e30)
        & (m1 > 1e-30)
        & (m0 > 1e-30)
    )
    pq_ref[0] = (first + second * gain)[0, 0]
    pq_ref[1] = -(first * second)[0, 0]
    sound_ref[0] = jnp.where(sound, 1, 0)[0, 0]


def scalars_of(back):
    smem = pl.BlockSpec(memory_space=pltpu.SMEM)
    return pl.pallas_call(
        scalar_kernel,
        grid=(1,),
        in_specs=[pl.BlockSpec((ND, 1, 128), lambda i: (0, 0, 3))],
        out_specs=[smem, smem],
        out_shape=[jax.ShapeDtypeStruct((2,), F32), jax.ShapeDtypeStruct((1,), jnp.int32)],
        compiler_params=pltpu.CompilerParams(vmem_limit_bytes=VMEM_LIMIT),
        name="scalars",
    )(back)


OB = 2048
OREC = R // OB
XS = 8
OSTEPS = 32 // XS


def next_kernel(
    pq_ref, back_ref, w_ref, blk_ref, own_ref, rank_ref, f_ref, y_ref, read_ref, xp_ref, xm_ref, yp_ref, ym_ref,
    next_ref, disp_ref,
    x_ref, turned_ref, force_ref, buf_ref, sems,
):
    step = pl.program_id(0)

    def fetch(slab):
        rows = pl.ds(pl.multiple_of(slab * XS * 8, XS * 8), XS * 8)
        return pltpu.make_async_copy(read_ref.at[:, rows, :], buf_ref.at[:, rows, :], sems.at[slab])

    @pl.when(step == 0)
    def _():
        for slab in range(OSTEPS):
            fetch(slab).start()
        p = pq_ref[0]
        q = pq_ref[1]
        back = p * back_ref[:, 0, 0 : 3 * CAP] + q * back_ref[:, 0, 3 * CAP : 6 * CAP]
        turned = back.T * COUPLING
        high = turned.astype(BF16)
        x_ref[:, 0:ND] = high
        x_ref[:, ND : 2 * ND] = (turned - high.astype(F32)).astype(BF16)
        disp_ref[...] = p * f_ref[...] + q * y_ref[...]
        turned_ref[...] = jnp.zeros_like(turned_ref)

    @pl.when(step < OREC)
    def _():
        named = hot(ND, own_ref[...])
        picked = dot(x_ref[...], jnp.concatenate([named, named], axis=0))
        in_slot = iota((CAP, OB), 0) == rank_ref[...]
        w_t = w_ref[...]
        highs, lows = [], []
        for c in range(3):
            moved = jnp.sum(
                jnp.where(in_slot, picked[c * CAP : (c + 1) * CAP, :], 0.0), axis=0, keepdims=True
            )
            part = w_t * moved
            high = part.astype(BF16)
            highs.append(high)
            lows.append((part - high.astype(F32)).astype(BF16))
        in_block = hot(NB, blk_ref[...])
        parts = jnp.concatenate([jnp.concatenate(highs, axis=0), jnp.concatenate(lows, axis=0)], axis=1)
        turned_ref[...] += dot_t(parts, jnp.concatenate([in_block, in_block], axis=1))

    @pl.when(step == OREC)
    def _():
        for c in range(3):
            force_ref[c * NB : (c + 1) * NB, :] = turned_ref[c * NK : (c + 1) * NK, :].T

    @pl.when(step >= OREC)
    def _():
        slab = step - OREC
        fetch(slab).wait()
        sub = iota((8, NK), 0)
        for xx in range(XS):
            x = slab * XS + xx
            rows = pl.ds(pl.multiple_of(x * 8, 8), 8)
            forcing = [
                force_ref[pl.ds(pl.multiple_of(c * NB + x * 8, 8), 8), :] for c in range(3)
            ]
            for q in range(19):
                cx, cy, _ = DIRS[q]
                value = buf_ref[q, rows, :]
                if cx == 1 and xx == 0:
                    value = jnp.where(x == 0, xp_ref[XP.index(q) * 8 : XP.index(q) * 8 + 8, :], value)
                if cx == -1 and xx == XS - 1:
                    value = jnp.where(x == 31, xm_ref[XM.index(q) * 8 : XM.index(q) * 8 + 8, :], value)
                if cy == 1:
                    value = jnp.where(sub == 0, yp_ref[pl.ds(YP.index(q) * 32 + x, 1), :], value)
                if cy == -1:
                    value = jnp.where(sub == 7, ym_ref[pl.ds(YM.index(q) * 32 + x, 1), :], value)
                along = combine(forcing, DIRS[q])
                if along is not None:
                    value = value + (3.0 * WEIGHTS[q]) * along
                next_ref[q, xx * 8 : (xx + 1) * 8, :] = value


def outputs_of(pq, back, weights, block_row, owner_row, rank_row, force, image, read, xp, xm, yp, ym):
    def record(i):
        return jnp.minimum(i, OREC - 1)

    def slab(i):
        return jnp.maximum(i - OREC, 0)

    row_spec = pl.BlockSpec((1, OB), lambda i: (0, record(i)))
    patch = pl.BlockSpec((3, NU, NV), lambda i: (0, 0, 0))
    lines = pl.BlockSpec((19, XS * 8, NK), lambda i: (0, slab(i), 0))
    x_face = pl.BlockSpec((40, NK), lambda i: (0, 0))
    y_face = pl.BlockSpec((160, NK), lambda i: (0, 0))
    return pl.pallas_call(
        next_kernel,
        grid=(OREC + OSTEPS,),
        in_specs=[
            pl.BlockSpec(memory_space=pltpu.SMEM),
            pl.BlockSpec((ND, 1, 8 * CAP), lambda i: (0, 0, 0)),
            pl.BlockSpec((NK, OB), lambda i: (0, record(i))),
            row_spec,
            row_spec,
            row_spec,
            patch,
            patch,
            pl.BlockSpec(memory_space=pltpu.HBM),
            x_face,
            x_face,
            y_face,
            y_face,
        ],
        out_specs=[lines, patch],
        out_shape=[
            jax.ShapeDtypeStruct((19, NB, NK), F32),
            jax.ShapeDtypeStruct((3, NU, NV), F32),
        ],
        scratch_shapes=[
            pltpu.VMEM((3 * CAP, 2 * ND), BF16),
            pltpu.VMEM((3 * NK, NB), F32),
            pltpu.VMEM((3 * NB, NK), F32),
            pltpu.VMEM((19, NB, NK), F32),
            pltpu.SemaphoreType.DMA((OSTEPS,)),
        ],
        compiler_params=pltpu.CompilerParams(vmem_limit_bytes=VMEM_LIMIT),
        name="outputs",
    )(pq, back, weights, block_row, owner_row, rank_row, force, image, read, xp, xm, yp, ym)


def pass_on(x, axis, shift):
    count = lax.axis_size(axis)
    return lax.ppermute(x, axis, [(i, (i + shift) % count) for i in range(count)])


def padded(field):
    for axis, dim in (("gx", 1), ("gy", 2)):
        size = field.shape[dim]
        head = lax.slice_in_dim(field, 0, 1, axis=dim)
        tail = lax.slice_in_dim(field, size - 1, size, axis=dim)
        field = jnp.concatenate([pass_on(tail, axis, 1), field, pass_on(head, axis, -1)], axis=dim)
    return field


def operate(field, mass, modulus, live, stiff):
    static = padded(jnp.stack([modulus, live.astype(F32)]))
    wide = padded(field)

    def corners(a):
        return a[..., :-1, :-1], a[..., 1:, :-1], a[..., :-1, 1:], a[..., 1:, 1:]

    c0, c1, c2, c3 = corners(static[0])
    scale = static[1, :-1, :-1] * (c0 + c1 + c2 + c3) * 0.25
    vector = jnp.concatenate(corners(wide), axis=0)
    result = scale[None] * jnp.einsum("kl,lab->kab", stiff, vector, precision=lax.Precision.HIGHEST)
    return (
        mass[None] * field
        + result[0:3, 1:, 1:]
        + result[3:6, :-1, 1:]
        + result[6:9, 1:, :-1]
        + result[9:12, :-1, :-1]
    )


def rim_of(force):
    before = pass_on(force[:, NU - 1 : NU, :], "gx", 1)
    after = pass_on(force[:, 0:2, :], "gx", -1)
    tall = jnp.concatenate([force, after, before], axis=1)
    left = pass_on(tall[:, :, NV - 1 : NV], "gy", 1)
    right = pass_on(tall[:, :, 0:2], "gy", -1)
    gap = jnp.zeros((3, EV - NV - 3), F32)
    rows = [
        jnp.concatenate([tall[:, r], right[:, r], gap, left[:, r]], axis=1) for r in (NU + 2, NU, NU + 1)
    ]
    beside = [
        jnp.concatenate([column[:, 0:NU], jnp.zeros((3, EV - NU), F32)], axis=1)
        for column in (left[:, :, 0], right[:, :, 0], right[:, :, 1])
    ]
    empty = jnp.zeros((3, EV), F32)
    return jnp.stack(rows + beside + [empty, empty], axis=1)


def exchange(x):
    return lax.all_to_all(x, ALL, 0, 0, tiled=True)


def per_device(populations, mass, modulus, live, stiff, rec_block, rec_owner, rec_node, weights):
    pops = populations.reshape(19, NB, NK)
    block_row = rec_block.reshape(1, R)
    owner_row = rec_owner.reshape(1, R)
    node_row = rec_node.reshape(1, R)

    send, rank_row, turned, xp, xm, yp, ym = loads_to_send(
        pops, weights, block_row, owner_row, node_row, mass, modulus, live
    )
    xp = pass_on(xp, "gx", 1)
    xm = pass_on(xm, "gx", -1)
    recv = exchange(send)
    yp, ym = sides_of(mass, modulus, live, xp, xm, yp, ym)
    yp = pass_on(yp, "gy", 1)
    ym = pass_on(ym, "gy", -1)
    rims = (xp, xm, yp, ym)

    force, rim = force_of(recv)
    image, ret = shell_of(stiff, force, rim, mass, modulus, live, rims, recv)
    ret, pops = lax.optimization_barrier((ret, pops))
    back = exchange(ret)
    read = collide_and_run(pops)
    back, read = lax.optimization_barrier((back, read))
    pq, sound = scalars_of(back)

    def quick(operands):
        return operands[0:3]

    def careful(operands):
        _, _, _, force, mass, modulus, live, stiff, rims, recv = operands
        image, ret = shell_of(stiff, force, rim_of(force), mass, modulus, live, rims, recv)
        back = exchange(ret)
        start = lax.psum(jnp.sum(force * force), ALL)
        first = start / lax.psum(jnp.sum(force * image), ALL)
        residual = force - first * image
        norm = lax.psum(jnp.sum(residual * residual), ALL)
        ratio = norm / start
        direction = residual + ratio * force
        along = operate(direction, mass, modulus, live, stiff)
        second = norm / lax.psum(jnp.sum(direction * along), ALL)
        return jnp.stack([first + second * (1.0 + ratio), -(first * second)]), image, back

    pq, image, back = lax.cond(
        sound[0] == 1, quick, careful, (pq, image, back, force, mass, modulus, live, stiff, rims, recv)
    )

    populations_next, displacement = outputs_of(
        pq, back, turned, block_row, owner_row, rank_row, force, image, read, xp, xm, yp, ym
    )
    return populations_next.reshape(19, 32, 8, NK), displacement


def solution(mesh):
    return jax.shard_map(
        per_device,
        mesh=mesh,
        in_specs=(
            P(None, "gx", "gy", None),
            P("gx", "gy"),
            P("gx", "gy"),
            P("gx", "gy"),
            P(),
            P(ALL),
            P(ALL, None),
            P(ALL),
            P(ALL, None),
        ),
        out_specs=(P(None, "gx", "gy", None), P(None, "gx", "gy")),
        check_vma=False,
    )
```

```python
import jax
import jax.numpy as jnp
from jax import lax
from jax.experimental import pallas as pl
from jax.experimental.pallas import tpu as pltpu
from jax.sharding import PartitionSpec as P

F32 = jnp.float32
BF16 = jnp.bfloat16
ALL = ("gx", "gy")
VMEM_LIMIT = 60 * 1024 * 1024
SMALL_LIMIT = 16 * 1024 * 1024

DIRS = (
    (0, 0, 0),
    (1, 0, 0),
    (-1, 0, 0),
    (0, 1, 0),
    (0, -1, 0),
    (0, 0, 1),
    (0, 0, -1),
    (1, 1, 0),
    (-1, -1, 0),
    (1, -1, 0),
    (-1, 1, 0),
    (1, 0, 1),
    (-1, 0, -1),
    (1, 0, -1),
    (-1, 0, 1),
    (0, 1, 1),
    (0, -1, -1),
    (0, 1, -1),
    (0, -1, 1),
)
WEIGHTS = (1.0 / 3.0,) + (1.0 / 18.0,) * 6 + (1.0 / 36.0,) * 12
RATE = 1.25
COUPLING = 0.1
XP = tuple(q for q in range(19) if DIRS[q][0] == 1)
XM = tuple(q for q in range(19) if DIRS[q][0] == -1)
YP = tuple(q for q in range(19) if DIRS[q][1] == 1)
YM = tuple(q for q in range(19) if DIRS[q][1] == -1)

R = 4096
NB = 256
NK = 256
ND = 128
CAP = 64
RIM = 32
MAIN = 4 * CAP
NU, NV = 64, 128
RB = 1024
EU, EV = 72, 256


def iota(shape, dim):
    return lax.broadcasted_iota(jnp.int32, shape, dim)


def halves(x):
    high = x.astype(BF16).astype(F32)
    return high, x - high


def combine(fields, direction):
    total = None
    for axis in range(3):
        if direction[axis] != 0:
            term = fields[axis] if direction[axis] == 1 else -fields[axis]
            total = term if total is None else total + term
    return total


def dot_t(a, b):
    return lax.dot_general(a, b, (((1,), (1,)), ((), ())), preferred_element_type=F32)


def dot(a, b):
    return lax.dot_general(a, b, (((1,), (0,)), ((), ())), preferred_element_type=F32)


def relaxed_of(pops, wanted):
    density = pops[0]
    for q in range(1, 19):
        density = density + pops[q]
    inverse = 1.0 / density
    velocity = []
    for axis in range(3):
        total = None
        for q in range(1, 19):
            if DIRS[q][axis] != 0:
                term = pops[q] if DIRS[q][axis] == 1 else -pops[q]
                total = term if total is None else total + term
        velocity.append(total * inverse)
    squared = velocity[0] * velocity[0] + velocity[1] * velocity[1] + velocity[2] * velocity[2]
    base = 1.0 - 1.5 * squared
    result = []
    for q in wanted:
        along = combine(velocity, DIRS[q])
        bracket = base if along is None else base + along * (3.0 + 4.5 * along)
        relaxed = pops[q] - RATE * (pops[q] - (WEIGHTS[q] * density) * bracket)
        if DIRS[q][2] != 0:
            relaxed = pltpu.roll(relaxed, 1 if DIRS[q][2] == 1 else NK - 1, 1)
        result.append(relaxed)
    return result


def turned_y(value, cy):
    return value if cy == 0 else pltpu.roll(value, 1 if cy == 1 else 7, 0)


XMSG = 48
YMSG = 168


CHUNKS = 4
CROWS = NB // CHUNKS
RSTEPS = R // RB


def match(count, row):
    lanes = row.shape[1]
    column = iota((count, 128), 0).astype(F32).astype(BF16)
    wanted = jnp.broadcast_to(row.astype(F32).astype(BF16), (count, lanes))
    return jnp.concatenate([column] * (lanes // 128), axis=1) == wanted


def hot(count, row):
    shape = (count, row.shape[1])
    return jnp.where(match(count, row), jnp.ones(shape, BF16), jnp.zeros(shape, BF16))


def pick(mask, row):
    return jnp.where(mask, jnp.broadcast_to(row, mask.shape), jnp.zeros(mask.shape, BF16))


def rim_rows(own, node):
    u, v = node >> 7, node & 127
    ox, oy = own >> 5, own & 31
    su = jnp.where(u == NU - 1, 1, jnp.where(u <= 1, -1, 0))
    sv = jnp.where(v == NV - 1, 1, jnp.where(v <= 1, -1, 0))
    ox2, oy2 = (ox + su) & 3, (oy + sv) & 31
    dests = [
        jnp.where(su != 0, ox2 * 32 + oy, -1),
        jnp.where(sv != 0, ox * 32 + oy2, -1),
        jnp.where((su != 0) & (sv != 0), ox2 * 32 + oy2, -1),
    ]
    row = jnp.where(u == NU - 1, 0, u + 1) * EV
    codes = [
        row + v,
        jnp.where(v == NV - 1, 3, v + 4) * EV + u,
        row + jnp.where(v == NV - 1, EV - 1, v + NV),
    ]
    return dests, codes


def load_kernel(
    pop_hbm, w_hbm, blk_ref, own_all_ref, node_all_ref, own_ref, node_ref, mass_ref, mod_ref, live_ref,
    send_ref, rank_ref, wt_ref, xp_ref, xm_ref, yp_ref, ym_ref,
    pop_ref, sems, w_ref, w_sems, m_ref, mt_ref, tri_ref, carry_ref, dest_ref, code_ref, place_ref, over_ref, main_ref, rims_ref,
):
    step = pl.program_id(0)

    def fetch(part):
        rows = pl.ds(part * CROWS, CROWS)
        return pltpu.make_async_copy(pop_hbm.at[:, rows, :], pop_ref.at[:, rows, :], sems.at[part])

    def fetch_w(part):
        rows = pl.ds(pl.multiple_of(part * RB, RB), RB)
        return pltpu.make_async_copy(w_hbm.at[rows, :], w_ref.at[rows, :], w_sems.at[part])

    @pl.when(step == 0)
    def _():
        for part in range(CHUNKS):
            fetch(part).start()
        before = (iota((256, 256), 0) < iota((256, 256), 1)).astype(F32)
        tri_ref[:, 0:256] = before.astype(BF16)
        tri_ref[:, 256:512] = jnp.ones((256, 256), BF16)
        carry_ref[...] = jnp.zeros_like(carry_ref)
        main_ref[...] = jnp.zeros_like(main_ref)
        rims_ref[...] = jnp.zeros_like(rims_ref)
        over_ref[...] = jnp.zeros_like(over_ref)
        dests, codes = rim_rows(own_all_ref[...], node_all_ref[...])
        for i in range(3):
            dest_ref[i : i + 1, :] = dests[i]
            code_ref[i : i + 1, :] = codes[i].astype(F32)
        for k in range(R // 256):
            cols = slice(k * 256, (k + 1) * 256)
            device = iota((ND, 256), 0)
            hots = [device == own_all_ref[:, cols]] + [device == dest_ref[i : i + 1, cols] for i in range(3)]
            main = jnp.where(hots[0], 1.0, 0.0).astype(BF16)
            rims = jnp.where(hots[1] | hots[2] | hots[3], 1.0, 0.0).astype(BF16)
            counts = dot(jnp.concatenate([main, rims], axis=0), tri_ref[...])
            upto = counts[:, 0:256] + carry_ref[...]
            carry_ref[...] += counts[:, 256:512]
            rank = jnp.sum(jnp.where(hots[0], upto[0:ND], 0.0), axis=0, keepdims=True)
            rank_ref[:, cols] = rank.astype(jnp.int32)
            for i in range(3):
                place = jnp.sum(jnp.where(hots[i + 1], upto[ND : 2 * ND], 0.0), axis=0, keepdims=True)
                over_ref[...] = jnp.maximum(over_ref[...], place)
                place_ref[i : i + 1, cols] = jnp.where(place < RIM - 1, place, 2.0 * RIM).astype(jnp.int32)

        def rows_of(i, _):
            rows = pl.ds(pl.multiple_of(i * 8, 8), 8)
            pops = [pop_ref[q, rows, :] for q in range(1, 19)]
            for axis in range(3):
                total = None
                for q in range(1, 19):
                    if DIRS[q][axis] != 0:
                        term = pops[q - 1] if DIRS[q][axis] == 1 else -pops[q - 1]
                        total = term if total is None else total + term
                m_ref[axis, rows, :] = total
            return 0

        sub = iota((8, NK), 0)
        for part in range(CHUNKS):
            fetch(part).wait()
            fetch_w(part).start()
            lax.fori_loop(part * CROWS // 8, (part + 1) * CROWS // 8, rows_of, 0, unroll=2)
            for face_ref, dirs, y in ((yp_ref, YP, 7), (ym_ref, YM, 0)):
                pops = []
                for q in range(19):
                    tile = None
                    for i in range(8):
                        row = jnp.broadcast_to(pop_ref[q, pl.ds(part * 64 + i * 8 + y, 1), :], (8, NK))
                        tile = row if tile is None else jnp.where(sub == i, row, tile)
                    pops.append(tile)
                values = relaxed_of(pops, dirs)
                for i in range(5):
                    face_ref[i * 32 + part * 8 : i * 32 + part * 8 + 8, :] = values[i]
        for face_ref, dirs in ((yp_ref, YP), (ym_ref, YM)):
            for i, q in enumerate(dirs):
                if DIRS[q][0] != 0:
                    face = face_ref[i * 32 : i * 32 + 32, :]
                    face_ref[i * 32 : i * 32 + 32, :] = pltpu.roll(face, 1 if DIRS[q][0] == 1 else 31, 0)
        for face_ref, dirs, x in ((xp_ref, XP, 31), (xm_ref, XM, 0)):
            values = relaxed_of([pop_ref[q, x * 8 : x * 8 + 8, :] for q in range(19)], dirs)
            for i, q in enumerate(dirs):
                face_ref[i * 8 : i * 8 + 8, :] = turned_y(values[i], DIRS[q][1])
            face_ref[40:XMSG, :] = jnp.zeros((XMSG - 40, NK), F32)
        for i, field in enumerate([mass_ref[...], mod_ref[...], live_ref[...].astype(F32)]):
            xp_ref[40 + i : 41 + i, 0:NV] = field[NU - 1 : NU, :]
            xm_ref[40 + 2 * i : 42 + 2 * i, 0:NV] = field[0:2, :]
        for axis in range(3):
            turned = m_ref[axis].T
            high = turned.astype(BF16)
            at = slice(axis * NK, (axis + 1) * NK)
            mt_ref[at, 0:NB] = high
            mt_ref[at, NB : 2 * NB] = (turned - high.astype(F32)).astype(BF16)

    @pl.when(step >= 1)
    def _():
        here = pl.ds(pl.multiple_of((step - 1) * RB, RB), RB)
        fetch_w(step - 1).wait()
        w_t = w_ref[here, :].T
        in_block = hot(NB, blk_ref[...])
        picked = dot(mt_ref[...], jnp.concatenate([in_block, in_block], axis=0))
        values = [
            jnp.sum(picked[axis * NK : (axis + 1) * NK, :] * w_t, axis=0, keepdims=True) for axis in range(3)
        ]

        def sides(value):
            return [side.astype(BF16) for side in halves(value)]

        parts = [sides(value) for value in values]

        def placed(count, slot, code):
            mask = match(count, slot)
            both = [pick(mask, part[side]) for side in range(2) for part in parts + [sides(code)]]
            return jnp.concatenate(both, axis=0)

        packed = placed(CAP, rank_ref[:, here], node_ref[...].astype(F32))
        main_ref[...] += dot_t(packed, hot(ND, own_ref[...]))
        packed = [placed(RIM, place_ref[i : i + 1, here], code_ref[i : i + 1, here]) for i in range(3)]
        named = [hot(ND, dest_ref[i : i + 1, here]) for i in range(3)]
        rims_ref[...] += dot_t(jnp.concatenate(packed, axis=1), jnp.concatenate(named, axis=1))
        wt_ref[...] = w_t

    @pl.when(step == RSTEPS)
    def _():
        most = jnp.max(over_ref[...], axis=1, keepdims=True)
        flag = jnp.where(most >= RIM - 1, 1.0, 0.0)
        send_ref[:, 0, 0:MAIN] = (main_ref[0:MAIN, :] + main_ref[MAIN : 2 * MAIN, :]).T
        tail = (rims_ref[0 : 4 * RIM, :] + rims_ref[4 * RIM : 8 * RIM, :]).T
        send_ref[:, 0, MAIN : MAIN + 4 * RIM] = jnp.where(iota((ND, 4 * RIM), 1) == 4 * RIM - 1, flag, tail)


def loads_to_send(pops, weights, block_row, owner_row, node_row, mass, modulus, live):
    def record(i):
        return jnp.maximum(i - 1, 0)

    row_spec = pl.BlockSpec((1, RB), lambda i: (0, record(i)))
    all_rows = pl.BlockSpec((1, R), lambda i: (0, 0))

    def whole(*shape):
        return pl.BlockSpec(shape, lambda i: (0, 0))

    return pl.pallas_call(
        load_kernel,
        grid=(1 + RSTEPS,),
        in_specs=[
            pl.BlockSpec(memory_space=pltpu.HBM),
            pl.BlockSpec(memory_space=pltpu.HBM),
            row_spec,
            all_rows,
            all_rows,
            row_spec,
            row_spec,
            whole(NU, NV),
            whole(NU, NV),
            whole(NU, NV),
        ],
        out_specs=[
            pl.BlockSpec((ND, 1, MAIN + 4 * RIM), lambda i: (0, 0, 0)),
            all_rows,
            pl.BlockSpec((NK, RB), lambda i: (0, record(i))),
            whole(XMSG, NK),
            whole(XMSG, NK),
            whole(160, NK),
            whole(160, NK),
        ],
        out_shape=[
            jax.ShapeDtypeStruct((ND, 1, MAIN + 4 * RIM), F32),
            jax.ShapeDtypeStruct((1, R), jnp.int32),
            jax.ShapeDtypeStruct((NK, R), F32),
            jax.ShapeDtypeStruct((XMSG, NK), F32),
            jax.ShapeDtypeStruct((XMSG, NK), F32),
            jax.ShapeDtypeStruct((160, NK), F32),
            jax.ShapeDtypeStruct((160, NK), F32),
        ],
        scratch_shapes=[
            pltpu.VMEM((19, NB, NK), F32),
            pltpu.SemaphoreType.DMA((CHUNKS,)),
            pltpu.VMEM((R, NK), F32),
            pltpu.SemaphoreType.DMA((RSTEPS,)),
            pltpu.VMEM((3, NB, NK), F32),
            pltpu.VMEM((3 * NK, 2 * NB), BF16),
            pltpu.VMEM((256, 512), BF16),
            pltpu.VMEM((2 * ND, 256), F32),
            pltpu.VMEM((8, R), jnp.int32),
            pltpu.VMEM((8, R), F32),
            pltpu.VMEM((8, R), jnp.int32),
            pltpu.VMEM((1, 256), F32),
            pltpu.VMEM((2 * MAIN, ND), F32),
            pltpu.VMEM((8 * RIM, ND), F32),
        ],
        compiler_params=pltpu.CompilerParams(vmem_limit_bytes=VMEM_LIMIT),
        name="loads",
    )(pops, weights, block_row, owner_row, node_row, owner_row, node_row, mass, modulus, live)


LINES = 8


def collide_kernel(pop_hbm, out_hbm, pop_ref, read_ref, in_sems, out_sems):
    chunks = 32 // LINES

    def fetch(part):
        rows = pl.ds(part * LINES * 8, LINES * 8)
        return pltpu.make_async_copy(pop_hbm.at[:, rows, :], pop_ref.at[:, rows, :], in_sems.at[part])

    def store(part):
        first = max(part * LINES - 1, 0) * 8
        last = NB if part == chunks - 1 else (part * LINES + LINES - 1) * 8
        rows = pl.ds(first, last - first)
        kept = pl.ds(first + 8, last - first)
        return pltpu.make_async_copy(read_ref.at[:, kept, :], out_hbm.at[:, rows, :], out_sems.at[part])

    def line(x, _):
        rows = pl.ds(pl.multiple_of(x * 8, 8), 8)
        values = relaxed_of([pop_ref[q, rows, :] for q in range(19)], range(19))
        for q in range(19):
            cx, cy, _ = DIRS[q]
            to = pl.ds(pl.multiple_of((x + cx + 1) * 8, 8), 8)
            read_ref[q, to, :] = turned_y(values[q], cy)
        return 0

    for part in range(chunks):
        fetch(part).start()
    for q in XP:
        read_ref[q, 8:16, :] = jnp.zeros((8, NK), F32)
    for q in XM:
        read_ref[q, NB : NB + 8, :] = jnp.zeros((8, NK), F32)
    for part in range(chunks):
        fetch(part).wait()
        lax.fori_loop(part * LINES, (part + 1) * LINES, line, 0, unroll=4)
        store(part).start()
    for part in range(chunks):
        store(part).wait()


def collide_and_run(pops):
    return pl.pallas_call(
        collide_kernel,
        in_specs=[pl.BlockSpec(memory_space=pltpu.HBM)],
        out_specs=pl.BlockSpec(memory_space=pltpu.HBM),
        out_shape=jax.ShapeDtypeStruct((19, NB, NK), F32),
        scratch_shapes=[
            pltpu.VMEM((19, NB, NK), F32),
            pltpu.VMEM((19, NB + 16, NK), F32),
            pltpu.SemaphoreType.DMA((32 // LINES,)),
            pltpu.SemaphoreType.DMA((32 // LINES,)),
        ],
        compiler_params=pltpu.CompilerParams(vmem_limit_bytes=VMEM_LIMIT),
        name="collide",
    )(pops)


def node_rows(recv_t):
    node = recv_t[3 * CAP : MAIN, :].astype(jnp.int32)
    return node >> 8, node & 255


def force_kernel(recv_ref, f_ref, rim_ref, u_ref, v_ref, hl_ref, ru_ref, rv_ref, rhl_ref):
    recv_t = recv_ref[:, 0, :].T
    u_ref[...], v_ref[...] = node_rows(recv_t)
    high, low = halves(recv_t[0 : 3 * CAP, :])
    hl_ref[0 : 3 * CAP, :] = high
    hl_ref[3 * CAP : 6 * CAP, :] = low
    code = recv_t[MAIN + 3 * RIM : MAIN + 4 * RIM, :].astype(jnp.int32)
    ru_ref[...] = code >> 8
    rv_ref[...] = code & 255
    high, low = halves(recv_t[MAIN : MAIN + 3 * RIM, :])
    rhl_ref[0 : 3 * RIM, :] = high
    rhl_ref[3 * RIM : 6 * RIM, :] = low

    def chunk_of(rows_ref, cols_ref, vals_ref, slots, height, width):
        def chunk(i, acc):
            at = pl.multiple_of(i * 8, 8)
            u8 = rows_ref[pl.ds(at, 8), :]
            v8 = cols_ref[pl.ds(at, 8), :]
            vals = [vals_ref[pl.ds(pl.multiple_of(part * slots + at, 8), 8), :].astype(BF16) for part in range(6)]
            lhs, rhs = [], []
            for r in range(8):
                here = match(max(height, 16), u8[r : r + 1, :])
                lhs.append(jnp.concatenate([pick(here, vals[part][r : r + 1, :]) for part in range(6)], axis=0))
                rhs.append(hot(width, v8[r : r + 1, :]))
            return acc + dot_t(jnp.concatenate(lhs, axis=1), jnp.concatenate(rhs, axis=1))

        return lax.fori_loop(0, slots // 8, chunk, jnp.zeros((6 * max(height, 16), width), F32), unroll=4)

    acc = chunk_of(u_ref, v_ref, hl_ref, CAP, NU // 2, 2 * NV)
    for c in range(3):
        pair = acc[c * 32 : (c + 1) * 32, :] + acc[(3 + c) * 32 : (4 + c) * 32, :]
        f_ref[c, pl.ds(0, 32, stride=2), :] = pair[:, 0:NV]
        f_ref[c, pl.ds(1, 32, stride=2), :] = pair[:, NV : 2 * NV]
    acc = chunk_of(ru_ref, rv_ref, rhl_ref, RIM, 8, EV)
    for c in range(3):
        rim_ref[c] = acc[c * 16 : c * 16 + 8, :] + acc[(3 + c) * 16 : (3 + c) * 16 + 8, :]


def force_of(recv):
    return pl.pallas_call(
        force_kernel,
        out_shape=[jax.ShapeDtypeStruct((3, NU, NV), F32), jax.ShapeDtypeStruct((3, 8, EV), F32)],
        scratch_shapes=[
            pltpu.VMEM((CAP, ND), jnp.int32),
            pltpu.VMEM((CAP, ND), jnp.int32),
            pltpu.VMEM((6 * CAP, ND), F32),
            pltpu.VMEM((RIM, ND), jnp.int32),
            pltpu.VMEM((RIM, ND), jnp.int32),
            pltpu.VMEM((6 * RIM, ND), F32),
        ],
        compiler_params=pltpu.CompilerParams(vmem_limit_bytes=SMALL_LIMIT),
        name="force",
    )(recv)


def rim_tile(i, low, high):
    sub = iota((8, 128), 0)
    tile = jnp.where(sub == 0, high[2 * i : 2 * i + 1, :], 0.0)
    tile = jnp.where(sub == 1, high[2 * i + 1 : 2 * i + 2, :], tile)
    return jnp.where(sub == 7, low[i : i + 1, :], tile)


def side_kernel(mass_ref, mod_ref, live_ref, xp_ref, xm_ref, yp_ref, ym_ref, to_p_ref, to_m_ref):
    to_p_ref[0:160, :] = yp_ref[...]
    to_m_ref[0:160, :] = ym_ref[...]
    for q, line, from_ref in ((7, 0, xp_ref), (10, 31, xm_ref)):
        face = (XP if line == 0 else XM).index(q) * 8
        at = YP.index(q) * 32 + line
        to_p_ref[at : at + 1, :] = from_ref[face : face + 1, :]
    for q, line, from_ref in ((9, 0, xp_ref), (8, 31, xm_ref)):
        face = (XP if line == 0 else XM).index(q) * 8 + 7
        at = YM.index(q) * 32 + line
        to_m_ref[at : at + 1, :] = from_ref[face : face + 1, :]
    to_p_ref[160:YMSG, :] = jnp.zeros((YMSG - 160, NK), F32)
    to_m_ref[160:YMSG, :] = jnp.zeros((YMSG - 160, NK), F32)
    low, high = xp_ref[40:XMSG, 0:NV], xm_ref[40:XMSG, 0:NV]
    for i, field in enumerate([mass_ref[...], mod_ref[...], live_ref[...].astype(F32)]):
        tall = jnp.concatenate([field, rim_tile(i, low, high), jnp.zeros((128 - EU, 128), F32)], axis=0)
        turned = tall.T
        to_p_ref[160 + i : 161 + i, 0:128] = turned[127:128, :]
        to_m_ref[160 + 2 * i : 162 + 2 * i, 0:128] = turned[0:2, :]


def sides_of(mass, modulus, live, xp, xm, yp, ym):
    return pl.pallas_call(
        side_kernel,
        out_shape=[jax.ShapeDtypeStruct((YMSG, NK), F32), jax.ShapeDtypeStruct((YMSG, NK), F32)],
        compiler_params=pltpu.CompilerParams(vmem_limit_bytes=VMEM_LIMIT),
        name="sides",
    )(mass, modulus, live, xp, xm, yp, ym)


def shell_kernel(
    stiff_ref, f_ref, rim_ref, mass_ref, mod_ref, live_ref, ulow_ref, uhigh_ref, vlow_ref, vhigh_ref, recv_ref,
    y_ref, ret_ref,
    e_ref, c_ref, g_ref, y_ext_ref, fy_ref, u_ref, v_ref, rt_ref,
):
    sub = iota((8, 128), 0)

    def columns(near, far, before):
        first = jnp.where(sub == 0, near, 0.0)
        first = jnp.where(sub == 1, far, first)
        last = jnp.where(sub == 7, before, 0.0)
        return jnp.concatenate([first, jnp.zeros((112, 128), F32), last], axis=0).T

    for i, field in enumerate([mass_ref[...], mod_ref[...], live_ref[...].astype(F32)]):
        e_ref[3 + i, 0:NU, 0:NV] = field
        e_ref[3 + i, NU:EU, 0:NV] = rim_tile(i, ulow_ref[:, 0:NV], uhigh_ref[:, 0:NV])
        side = columns(
            vhigh_ref[2 * i : 2 * i + 1, 0:128],
            vhigh_ref[2 * i + 1 : 2 * i + 2, 0:128],
            vlow_ref[i : i + 1, 0:128],
        )
        e_ref[3 + i, :, NV:EV] = side[0:EU, :]
    wide = iota((8, EV), 0)
    for i in range(3):
        e_ref[i, 0:NU, 0:NV] = f_ref[i]
        tile = jnp.where(wide == 0, rim_ref[i, 1:2, :], 0.0)
        tile = jnp.where(wide == 1, rim_ref[i, 2:3, :], tile)
        e_ref[i, NU:EU, :] = jnp.where(wide == 7, rim_ref[i, 0:1, :], tile)
        side = columns(rim_ref[i, 4:5, 0:128], rim_ref[i, 5:6, 0:128], rim_ref[i, 3:4, 0:128])
        e_ref[i, 0:NU, NV:EV] = side[0:NU, :]

    def up(x):
        return pltpu.roll(x, EU - 1, 0)

    def right(x):
        return pltpu.roll(x, EV - 1, 1)

    def down(x):
        return pltpu.roll(x, 1, 0)

    def left(x):
        return pltpu.roll(x, 1, 1)

    mod = e_ref[4]
    mod = mod + up(mod)
    e_ref[5] = e_ref[5] * (mod + right(mod)) * 0.25
    for c in range(3):
        field = e_ref[c]
        moved = up(field)
        c_ref[c] = field
        c_ref[3 + c] = moved
        c_ref[6 + c] = right(field)
        c_ref[9 + c] = right(moved)

    def cells(t, _):
        rows = pl.ds(pl.multiple_of(t * 8, 8), 8)
        corner = [c_ref[k, rows, :] for k in range(12)]
        scale = e_ref[5, rows, :]
        for k in range(12):
            total = stiff_ref[k, 0] * corner[0]
            for m in range(1, 12):
                total = total + stiff_ref[k, m] * corner[m]
            g_ref[k, rows, :] = scale * total
        return 0

    lax.fori_loop(0, EU // 8, cells, 0, unroll=3)
    mass = e_ref[3]
    for c in range(3):
        spread = g_ref[c] + down(g_ref[3 + c])
        beside = g_ref[6 + c] + down(g_ref[9 + c])
        y_ext_ref[c] = mass * e_ref[c] + spread + left(beside)
        y_ref[c] = y_ext_ref[c, 0:NU, 0:NV]
    for c in range(3):
        field = y_ext_ref[c]
        moved = up(field)
        c_ref[c] = field
        c_ref[3 + c] = moved
        c_ref[6 + c] = right(field)
        c_ref[9 + c] = right(moved)

    def energy(t, sums):
        rows = pl.ds(pl.multiple_of(t * 8, 8), 8)
        corner = [c_ref[k, rows, 0:NV] for k in range(12)]
        total = None
        for k in range(12):
            inner = stiff_ref[k, 0] * corner[0]
            for m in range(1, 12):
                inner = inner + stiff_ref[k, m] * corner[m]
            total = corner[k] * inner if total is None else total + corner[k] * inner
        m3 = e_ref[5, rows, 0:NV] * total
        m0, m1, m2 = None, None, None
        for c in range(3):
            f = e_ref[c, rows, 0:NV]
            y = corner[c]
            m0 = f * f if m0 is None else m0 + f * f
            m1 = f * y if m1 is None else m1 + f * y
            m2 = y * y if m2 is None else m2 + y * y
        m3 = m3 + e_ref[3, rows, 0:NV] * m2
        return tuple(s + m for s, m in zip(sums, (m0, m1, m2, m3)))

    zero = jnp.zeros((8, NV), F32)
    sums = lax.fori_loop(0, NU // 8, energy, (zero, zero, zero, zero), unroll=2)
    lane = iota((1, 128), 1)
    moments = jnp.zeros((1, 128), F32)
    for i in range(4):
        whole = jnp.sum(jnp.sum(sums[i], axis=0, keepdims=True), axis=1, keepdims=True)
        moments = jnp.where(lane == i, whole, moments)
    over = jnp.max(recv_ref[:, 0, MAIN + 3 * RIM :], axis=0, keepdims=True)[:, RIM - 1 :]
    moments = jnp.where(lane == 4, over, moments)

    for c in range(3):
        for part, field in ((c, f_ref), (3 + c, y_ref)):
            rows = slice(part * 32, part * 32 + 32)
            for odd in range(2):
                value = field[c, pl.ds(odd, 32, stride=2), :]
                high = value.astype(BF16)
                fy_ref[rows, odd * NV : (odd + 1) * NV] = high
                fy_ref[rows, (2 + odd) * NV : (3 + odd) * NV] = (value - high.astype(F32)).astype(BF16)
    u_ref[...], v_ref[...] = node_rows(recv_ref[:, 0, 0:MAIN].T)
    u_of = iota((NU // 2, ND), 0)

    def chunk(i, _):
        at = pl.multiple_of(i * 8, 8)
        u8 = u_ref[pl.ds(at, 8), :]
        v8 = v_ref[pl.ds(at, 8), :]
        rhs = jnp.concatenate([hot(2 * NV, v8[r : r + 1, :]) for r in range(8)], axis=1)
        picked = dot(fy_ref[...], jnp.concatenate([rhs, rhs], axis=0))
        tiles = [jnp.zeros((8, ND), F32) for _ in range(6)]
        for r in range(8):
            here = u_of == u8[r : r + 1, :]
            for part in range(6):
                block = picked[part * 32 : (part + 1) * 32, r * ND : (r + 1) * ND]
                row = jnp.sum(jnp.where(here, block, 0.0), axis=0, keepdims=True)
                tiles[part] = jnp.where(sub == r, row, tiles[part])
        for part in range(6):
            rt_ref[pl.ds(pl.multiple_of(part * CAP + at, 8), 8), :] = tiles[part]
        return 0

    lax.fori_loop(0, CAP // 8, chunk, 0, unroll=8)
    ret_ref[:, 0, 0 : 6 * CAP] = rt_ref[...].T
    ret_ref[:, 0, 6 * CAP : 8 * CAP] = jnp.broadcast_to(moments, (ND, 128))


def shell_of(stiff, force, rim, mass, modulus, live, rims, recv):
    vmem = pl.BlockSpec(memory_space=pltpu.VMEM)
    return pl.pallas_call(
        shell_kernel,
        grid=(1,),
        in_specs=[pl.BlockSpec(memory_space=pltpu.SMEM)]
        + [vmem] * 5
        + [pl.BlockSpec((8, NK), lambda i: (5, 0))] * 2
        + [pl.BlockSpec((8, NK), lambda i: (20, 0))] * 2
        + [vmem],
        out_specs=[vmem, vmem],
        out_shape=[
            jax.ShapeDtypeStruct((3, NU, NV), F32),
            jax.ShapeDtypeStruct((ND, 1, 8 * CAP), F32),
        ],
        scratch_shapes=[
            pltpu.VMEM((6, EU, EV), F32),
            pltpu.VMEM((12, EU, EV), F32),
            pltpu.VMEM((12, EU, EV), F32),
            pltpu.VMEM((3, EU, EV), F32),
            pltpu.VMEM((6 * NU // 2, 4 * NV), BF16),
            pltpu.VMEM((CAP, ND), jnp.int32),
            pltpu.VMEM((CAP, ND), jnp.int32),
            pltpu.VMEM((6 * CAP, ND), F32),
        ],
        compiler_params=pltpu.CompilerParams(vmem_limit_bytes=SMALL_LIMIT),
        name="shell",
    )(stiff, force, rim, mass, modulus, live, *rims, recv)


def scalar_kernel(part_ref, pq_ref, sound_ref):
    row = jnp.sum(part_ref[:, 0, :], axis=0, keepdims=True)
    lane = iota((1, 128), 1)
    m0, m1, m2, m3, over = [
        jnp.sum(jnp.where(lane == i, row, 0.0), axis=1, keepdims=True) for i in range(5)
    ]
    first = m0 / m1
    left_over = first * first * m2 - m0
    ratio = left_over / m0
    gain = 1.0 + ratio
    curve = gain * gain * m1 - 2.0 * gain * first * m2 + first * first * m3
    second = left_over / curve
    sound = (
        (over == 0.0)
        & (left_over > 1e-3 * m0)
        & (curve > 1e-2 * gain * gain * m1)
        & (curve < 1e30)
        & (m1 > 1e-30)
        & (m0 > 1e-30)
    )
    pq_ref[0] = (first + second * gain)[0, 0]
    pq_ref[1] = -(first * second)[0, 0]
    sound_ref[0] = jnp.where(sound, 1, 0)[0, 0]


def scalars_of(back):
    smem = pl.BlockSpec(memory_space=pltpu.SMEM)
    return pl.pallas_call(
        scalar_kernel,
        grid=(1,),
        in_specs=[pl.BlockSpec((ND, 1, 128), lambda i: (0, 0, 3))],
        out_specs=[smem, smem],
        out_shape=[jax.ShapeDtypeStruct((2,), F32), jax.ShapeDtypeStruct((1,), jnp.int32)],
        compiler_params=pltpu.CompilerParams(vmem_limit_bytes=VMEM_LIMIT),
        name="scalars",
    )(back)


OB = 2048
OREC = R // OB
XS = 8
OSTEPS = 32 // XS


def next_kernel(
    pq_ref, back_ref, w_ref, blk_ref, own_ref, rank_ref, f_ref, y_ref, read_ref, xp_ref, xm_ref, yp_ref, ym_ref,
    next_ref, disp_ref,
    x_ref, turned_ref, force_ref, buf_ref, sems,
):
    step = pl.program_id(0)

    def fetch(slab):
        rows = pl.ds(pl.multiple_of(slab * XS * 8, XS * 8), XS * 8)
        return pltpu.make_async_copy(read_ref.at[:, rows, :], buf_ref.at[:, rows, :], sems.at[slab])

    @pl.when(step == 0)
    def _():
        for slab in range(OSTEPS):
            fetch(slab).start()
        p = pq_ref[0]
        q = pq_ref[1]
        back = p * back_ref[:, 0, 0 : 3 * CAP] + q * back_ref[:, 0, 3 * CAP : 6 * CAP]
        turned = back.T * COUPLING
        high = turned.astype(BF16)
        x_ref[:, 0:ND] = high
        x_ref[:, ND : 2 * ND] = (turned - high.astype(F32)).astype(BF16)
        disp_ref[...] = p * f_ref[...] + q * y_ref[...]
        turned_ref[...] = jnp.zeros_like(turned_ref)

    @pl.when(step < OREC)
    def _():
        named = hot(ND, own_ref[...])
        picked = dot(x_ref[...], jnp.concatenate([named, named], axis=0))
        in_slot = iota((CAP, OB), 0) == rank_ref[...]
        w_t = w_ref[...]
        highs, lows = [], []
        for c in range(3):
            moved = jnp.sum(
                jnp.where(in_slot, picked[c * CAP : (c + 1) * CAP, :], 0.0), axis=0, keepdims=True
            )
            part = w_t * moved
            high = part.astype(BF16)
            highs.append(high)
            lows.append((part - high.astype(F32)).astype(BF16))
        in_block = hot(NB, blk_ref[...])
        parts = jnp.concatenate([jnp.concatenate(highs, axis=0), jnp.concatenate(lows, axis=0)], axis=1)
        turned_ref[...] += dot_t(parts, jnp.concatenate([in_block, in_block], axis=1))

    @pl.when(step == OREC)
    def _():
        for c in range(3):
            force_ref[c * NB : (c + 1) * NB, :] = turned_ref[c * NK : (c + 1) * NK, :].T

    @pl.when(step >= OREC)
    def _():
        slab = step - OREC
        fetch(slab).wait()
        sub = iota((8, NK), 0)
        for xx in range(XS):
            x = slab * XS + xx
            rows = pl.ds(pl.multiple_of(x * 8, 8), 8)
            forcing = [
                force_ref[pl.ds(pl.multiple_of(c * NB + x * 8, 8), 8), :] for c in range(3)
            ]
            for q in range(19):
                cx, cy, _ = DIRS[q]
                value = buf_ref[q, rows, :]
                if cx == 1 and xx == 0:
                    value = jnp.where(x == 0, xp_ref[XP.index(q) * 8 : XP.index(q) * 8 + 8, :], value)
                if cx == -1 and xx == XS - 1:
                    value = jnp.where(x == 31, xm_ref[XM.index(q) * 8 : XM.index(q) * 8 + 8, :], value)
                if cy == 1:
                    value = jnp.where(sub == 0, yp_ref[pl.ds(YP.index(q) * 32 + x, 1), :], value)
                if cy == -1:
                    value = jnp.where(sub == 7, ym_ref[pl.ds(YM.index(q) * 32 + x, 1), :], value)
                along = combine(forcing, DIRS[q])
                if along is not None:
                    value = value + (3.0 * WEIGHTS[q]) * along
                next_ref[q, xx * 8 : (xx + 1) * 8, :] = value


def outputs_of(pq, back, weights, block_row, owner_row, rank_row, force, image, read, xp, xm, yp, ym):
    def record(i):
        return jnp.minimum(i, OREC - 1)

    def slab(i):
        return jnp.maximum(i - OREC, 0)

    row_spec = pl.BlockSpec((1, OB), lambda i: (0, record(i)))
    patch = pl.BlockSpec((3, NU, NV), lambda i: (0, 0, 0))
    lines = pl.BlockSpec((19, XS * 8, NK), lambda i: (0, slab(i), 0))
    x_face = pl.BlockSpec((40, NK), lambda i: (0, 0))
    y_face = pl.BlockSpec((160, NK), lambda i: (0, 0))
    return pl.pallas_call(
        next_kernel,
        grid=(OREC + OSTEPS,),
        in_specs=[
            pl.BlockSpec(memory_space=pltpu.SMEM),
            pl.BlockSpec((ND, 1, 8 * CAP), lambda i: (0, 0, 0)),
            pl.BlockSpec((NK, OB), lambda i: (0, record(i))),
            row_spec,
            row_spec,
            row_spec,
            patch,
            patch,
            pl.BlockSpec(memory_space=pltpu.HBM),
            x_face,
            x_face,
            y_face,
            y_face,
        ],
        out_specs=[lines, patch],
        out_shape=[
            jax.ShapeDtypeStruct((19, NB, NK), F32),
            jax.ShapeDtypeStruct((3, NU, NV), F32),
        ],
        scratch_shapes=[
            pltpu.VMEM((3 * CAP, 2 * ND), BF16),
            pltpu.VMEM((3 * NK, NB), F32),
            pltpu.VMEM((3 * NB, NK), F32),
            pltpu.VMEM((19, NB, NK), F32),
            pltpu.SemaphoreType.DMA((OSTEPS,)),
        ],
        compiler_params=pltpu.CompilerParams(vmem_limit_bytes=VMEM_LIMIT),
        name="outputs",
    )(pq, back, weights, block_row, owner_row, rank_row, force, image, read, xp, xm, yp, ym)


def pass_on(x, axis, shift):
    count = lax.axis_size(axis)
    return lax.ppermute(x, axis, [(i, (i + shift) % count) for i in range(count)])


def padded(field):
    for axis, dim in (("gx", 1), ("gy", 2)):
        size = field.shape[dim]
        head = lax.slice_in_dim(field, 0, 1, axis=dim)
        tail = lax.slice_in_dim(field, size - 1, size, axis=dim)
        field = jnp.concatenate([pass_on(tail, axis, 1), field, pass_on(head, axis, -1)], axis=dim)
    return field


def operate(field, mass, modulus, live, stiff):
    static = padded(jnp.stack([modulus, live.astype(F32)]))
    wide = padded(field)

    def corners(a):
        return a[..., :-1, :-1], a[..., 1:, :-1], a[..., :-1, 1:], a[..., 1:, 1:]

    c0, c1, c2, c3 = corners(static[0])
    scale = static[1, :-1, :-1] * (c0 + c1 + c2 + c3) * 0.25
    vector = jnp.concatenate(corners(wide), axis=0)
    result = scale[None] * jnp.einsum("kl,lab->kab", stiff, vector, precision=lax.Precision.HIGHEST)
    return (
        mass[None] * field
        + result[0:3, 1:, 1:]
        + result[3:6, :-1, 1:]
        + result[6:9, 1:, :-1]
        + result[9:12, :-1, :-1]
    )


def rim_of(force):
    before = pass_on(force[:, NU - 1 : NU, :], "gx", 1)
    after = pass_on(force[:, 0:2, :], "gx", -1)
    tall = jnp.concatenate([force, after, before], axis=1)
    left = pass_on(tall[:, :, NV - 1 : NV], "gy", 1)
    right = pass_on(tall[:, :, 0:2], "gy", -1)
    gap = jnp.zeros((3, EV - NV - 3), F32)
    rows = [
        jnp.concatenate([tall[:, r], right[:, r], gap, left[:, r]], axis=1) for r in (NU + 2, NU, NU + 1)
    ]
    beside = [
        jnp.concatenate([column[:, 0:NU], jnp.zeros((3, EV - NU), F32)], axis=1)
        for column in (left[:, :, 0], right[:, :, 0], right[:, :, 1])
    ]
    empty = jnp.zeros((3, EV), F32)
    return jnp.stack(rows + beside + [empty, empty], axis=1)


def exchange(x):
    return lax.all_to_all(x, ALL, 0, 0, tiled=True)


def per_device(populations, mass, modulus, live, stiff, rec_block, rec_owner, rec_node, weights):
    pops = populations.reshape(19, NB, NK)
    block_row = rec_block.reshape(1, R)
    owner_row = rec_owner.reshape(1, R)
    node_row = rec_node.reshape(1, R)

    send, rank_row, turned, xp, xm, yp, ym = loads_to_send(
        pops, weights, block_row, owner_row, node_row, mass, modulus, live
    )
    xp = pass_on(xp, "gx", 1)
    xm = pass_on(xm, "gx", -1)
    recv = exchange(send)
    yp, ym = sides_of(mass, modulus, live, xp, xm, yp, ym)
    yp = pass_on(yp, "gy", 1)
    ym = pass_on(ym, "gy", -1)
    rims = (xp, xm, yp, ym)

    force, rim = force_of(recv)
    image, ret = shell_of(stiff, force, rim, mass, modulus, live, rims, recv)
    ret, pops = lax.optimization_barrier((ret, pops))
    back = exchange(ret)
    read = collide_and_run(pops)
    back, read = lax.optimization_barrier((back, read))
    pq, sound = scalars_of(back)

    def quick(operands):
        return operands[0:3]

    def careful(operands):
        _, _, _, force, mass, modulus, live, stiff, rims, recv = operands
        image, ret = shell_of(stiff, force, rim_of(force), mass, modulus, live, rims, recv)
        back = exchange(ret)
        start = lax.psum(jnp.sum(force * force), ALL)
        first = start / lax.psum(jnp.sum(force * image), ALL)
        residual = force - first * image
        norm = lax.psum(jnp.sum(residual * residual), ALL)
        ratio = norm / start
        direction = residual + ratio * force
        along = operate(direction, mass, modulus, live, stiff)
        second = norm / lax.psum(jnp.sum(direction * along), ALL)
        return jnp.stack([first + second * (1.0 + ratio), -(first * second)]), image, back

    pq, image, back = lax.cond(
        sound[0] == 1, quick, careful, (pq, image, back, force, mass, modulus, live, stiff, rims, recv)
    )

    populations_next, displacement = outputs_of(
        pq, back, turned, block_row, owner_row, rank_row, force, image, read, xp, xm, yp, ym
    )
    return populations_next.reshape(19, 32, 8, NK), displacement


def solution(mesh):
    return jax.shard_map(
        per_device,
        mesh=mesh,
        in_specs=(
            P(None, "gx", "gy", None),
            P("gx", "gy"),
            P("gx", "gy"),
            P("gx", "gy"),
            P(),
            P(ALL),
            P(ALL, None),
            P(ALL),
            P(ALL, None),
        ),
        out_specs=(P(None, "gx", "gy", None), P(None, "gx", "gy")),
        check_vma=False,
    )
```

```python
import jax
import jax.numpy as jnp
from jax import lax
from jax.experimental import pallas as pl
from jax.experimental.pallas import tpu as pltpu
from jax.sharding import PartitionSpec as P

F32 = jnp.float32
BF16 = jnp.bfloat16
ALL = ("gx", "gy")
VMEM_LIMIT = 60 * 1024 * 1024
SMALL_LIMIT = 16 * 1024 * 1024

DIRS = (
    (0, 0, 0),
    (1, 0, 0),
    (-1, 0, 0),
    (0, 1, 0),
    (0, -1, 0),
    (0, 0, 1),
    (0, 0, -1),
    (1, 1, 0),
    (-1, -1, 0),
    (1, -1, 0),
    (-1, 1, 0),
    (1, 0, 1),
    (-1, 0, -1),
    (1, 0, -1),
    (-1, 0, 1),
    (0, 1, 1),
    (0, -1, -1),
    (0, 1, -1),
    (0, -1, 1),
)
WEIGHTS = (1.0 / 3.0,) + (1.0 / 18.0,) * 6 + (1.0 / 36.0,) * 12
RATE = 1.25
COUPLING = 0.1
XP = tuple(q for q in range(19) if DIRS[q][0] == 1)
XM = tuple(q for q in range(19) if DIRS[q][0] == -1)
YP = tuple(q for q in range(19) if DIRS[q][1] == 1)
YM = tuple(q for q in range(19) if DIRS[q][1] == -1)

R = 4096
NB = 256
NK = 256
ND = 128
CAP = 64
RIM = 32
MAIN = 4 * CAP
NU, NV = 64, 128
RB = 1024
EU, EV = 72, 256


def iota(shape, dim):
    return lax.broadcasted_iota(jnp.int32, shape, dim)


def halves(x):
    high = x.astype(BF16).astype(F32)
    return high, x - high


def combine(fields, direction):
    total = None
    for axis in range(3):
        if direction[axis] != 0:
            term = fields[axis] if direction[axis] == 1 else -fields[axis]
            total = term if total is None else total + term
    return total


def dot_t(a, b):
    return lax.dot_general(a, b, (((1,), (1,)), ((), ())), preferred_element_type=F32)


def dot(a, b):
    return lax.dot_general(a, b, (((1,), (0,)), ((), ())), preferred_element_type=F32)


def relaxed_of(pops, wanted):
    density = pops[0]
    for q in range(1, 19):
        density = density + pops[q]
    inverse = 1.0 / density
    velocity = []
    for axis in range(3):
        total = None
        for q in range(1, 19):
            if DIRS[q][axis] != 0:
                term = pops[q] if DIRS[q][axis] == 1 else -pops[q]
                total = term if total is None else total + term
        velocity.append(total * inverse)
    squared = velocity[0] * velocity[0] + velocity[1] * velocity[1] + velocity[2] * velocity[2]
    base = 1.0 - 1.5 * squared
    result = []
    for q in wanted:
        along = combine(velocity, DIRS[q])
        bracket = base if along is None else base + along * (3.0 + 4.5 * along)
        relaxed = pops[q] - RATE * (pops[q] - (WEIGHTS[q] * density) * bracket)
        if DIRS[q][2] != 0:
            relaxed = pltpu.roll(relaxed, 1 if DIRS[q][2] == 1 else NK - 1, 1)
        result.append(relaxed)
    return result


def turned_y(value, cy):
    return value if cy == 0 else pltpu.roll(value, 1 if cy == 1 else 7, 0)


XMSG = 48
YMSG = 168


CHUNKS = 4
CROWS = NB // CHUNKS
RSTEPS = R // RB


def match(count, row):
    lanes = row.shape[1]
    column = iota((count, 128), 0).astype(F32).astype(BF16)
    wanted = jnp.broadcast_to(row.astype(F32).astype(BF16), (count, lanes))
    return jnp.concatenate([column] * (lanes // 128), axis=1) == wanted


def hot(count, row):
    shape = (count, row.shape[1])
    return jnp.where(match(count, row), jnp.ones(shape, BF16), jnp.zeros(shape, BF16))


def pick(mask, row):
    return jnp.where(mask, jnp.broadcast_to(row, mask.shape), jnp.zeros(mask.shape, BF16))


def rim_rows(own, node):
    u, v = node >> 7, node & 127
    ox, oy = own >> 5, own & 31
    su = jnp.where(u == NU - 1, 1, jnp.where(u <= 1, -1, 0))
    sv = jnp.where(v == NV - 1, 1, jnp.where(v <= 1, -1, 0))
    ox2, oy2 = (ox + su) & 3, (oy + sv) & 31
    dests = [
        jnp.where(su != 0, ox2 * 32 + oy, -1),
        jnp.where(sv != 0, ox * 32 + oy2, -1),
        jnp.where((su != 0) & (sv != 0), ox2 * 32 + oy2, -1),
    ]
    row = jnp.where(u == NU - 1, 0, u + 1) * EV
    codes = [
        row + v,
        jnp.where(v == NV - 1, 3, v + 4) * EV + u,
        row + jnp.where(v == NV - 1, EV - 1, v + NV),
    ]
    return dests, codes


def load_kernel(
    pop_hbm, w_hbm, blk_ref, own_all_ref, node_all_ref, own_ref, node_ref, mass_ref, mod_ref, live_ref,
    send_ref, rank_ref, wt_ref, xp_ref, xm_ref, yp_ref, ym_ref,
    pop_ref, sems, w_ref, w_sems, m_ref, mt_ref, tri_ref, carry_ref, dest_ref, code_ref, place_ref, over_ref, main_ref, rims_ref,
):
    step = pl.program_id(0)

    def fetch(part):
        rows = pl.ds(part * CROWS, CROWS)
        return pltpu.make_async_copy(pop_hbm.at[:, rows, :], pop_ref.at[:, rows, :], sems.at[part])

    def fetch_w(part):
        rows = pl.ds(pl.multiple_of(part * RB, RB), RB)
        return pltpu.make_async_copy(w_hbm.at[rows, :], w_ref.at[rows, :], w_sems.at[part])

    @pl.when(step == 0)
    def _():
        for part in range(CHUNKS):
            fetch(part).start()
        before = (iota((256, 256), 0) < iota((256, 256), 1)).astype(F32)
        tri_ref[:, 0:256] = before.astype(BF16)
        tri_ref[:, 256:512] = jnp.ones((256, 256), BF16)
        carry_ref[...] = jnp.zeros_like(carry_ref)
        main_ref[...] = jnp.zeros_like(main_ref)
        rims_ref[...] = jnp.zeros_like(rims_ref)
        over_ref[...] = jnp.zeros_like(over_ref)
        dests, codes = rim_rows(own_all_ref[...], node_all_ref[...])
        for i in range(3):
            dest_ref[i : i + 1, :] = dests[i]
            code_ref[i : i + 1, :] = codes[i].astype(F32)
        for k in range(R // 256):
            cols = slice(k * 256, (k + 1) * 256)
            device = iota((ND, 256), 0)
            hots = [device == own_all_ref[:, cols]] + [device == dest_ref[i : i + 1, cols] for i in range(3)]
            main = jnp.where(hots[0], 1.0, 0.0).astype(BF16)
            rims = jnp.where(hots[1] | hots[2] | hots[3], 1.0, 0.0).astype(BF16)
            counts = dot(jnp.concatenate([main, rims], axis=0), tri_ref[...])
            upto = counts[:, 0:256] + carry_ref[...]
            carry_ref[...] += counts[:, 256:512]
            rank = jnp.sum(jnp.where(hots[0], upto[0:ND], 0.0), axis=0, keepdims=True)
            rank_ref[:, cols] = rank.astype(jnp.int32)
            for i in range(3):
                place = jnp.sum(jnp.where(hots[i + 1], upto[ND : 2 * ND], 0.0), axis=0, keepdims=True)
                over_ref[...] = jnp.maximum(over_ref[...], place)
                place_ref[i : i + 1, cols] = jnp.where(place < RIM - 1, place, 2.0 * RIM).astype(jnp.int32)

        def rows_of(i, _):
            rows = pl.ds(pl.multiple_of(i * 8, 8), 8)
            pops = [pop_ref[q, rows, :] for q in range(1, 19)]
            for axis in range(3):
                total = None
                for q in range(1, 19):
                    if DIRS[q][axis] != 0:
                        term = pops[q - 1] if DIRS[q][axis] == 1 else -pops[q - 1]
                        total = term if total is None else total + term
                m_ref[axis, rows, :] = total
            return 0

        sub = iota((8, NK), 0)
        for part in range(CHUNKS):
            fetch(part).wait()
            fetch_w(part).start()
            lax.fori_loop(part * CROWS // 8, (part + 1) * CROWS // 8, rows_of, 0, unroll=4)
            for face_ref, dirs, y in ((yp_ref, YP, 7), (ym_ref, YM, 0)):
                pops = []
                for q in range(19):
                    tile = None
                    for i in range(8):
                        row = jnp.broadcast_to(pop_ref[q, pl.ds(part * 64 + i * 8 + y, 1), :], (8, NK))
                        tile = row if tile is None else jnp.where(sub == i, row, tile)
                    pops.append(tile)
                values = relaxed_of(pops, dirs)
                for i in range(5):
                    face_ref[i * 32 + part * 8 : i * 32 + part * 8 + 8, :] = values[i]
        for face_ref, dirs in ((yp_ref, YP), (ym_ref, YM)):
            for i, q in enumerate(dirs):
                if DIRS[q][0] != 0:
                    face = face_ref[i * 32 : i * 32 + 32, :]
                    face_ref[i * 32 : i * 32 + 32, :] = pltpu.roll(face, 1 if DIRS[q][0] == 1 else 31, 0)
        for face_ref, dirs, x in ((xp_ref, XP, 31), (xm_ref, XM, 0)):
            values = relaxed_of([pop_ref[q, x * 8 : x * 8 + 8, :] for q in range(19)], dirs)
            for i, q in enumerate(dirs):
                face_ref[i * 8 : i * 8 + 8, :] = turned_y(values[i], DIRS[q][1])
            face_ref[40:XMSG, :] = jnp.zeros((XMSG - 40, NK), F32)
        for i, field in enumerate([mass_ref[...], mod_ref[...], live_ref[...].astype(F32)]):
            xp_ref[40 + i : 41 + i, 0:NV] = field[NU - 1 : NU, :]
            xm_ref[40 + 2 * i : 42 + 2 * i, 0:NV] = field[0:2, :]
        for axis in range(3):
            turned = m_ref[axis].T
            high = turned.astype(BF16)
            at = slice(axis * NK, (axis + 1) * NK)
            mt_ref[at, 0:NB] = high
            mt_ref[at, NB : 2 * NB] = (turned - high.astype(F32)).astype(BF16)

    @pl.when(step >= 1)
    def _():
        here = pl.ds(pl.multiple_of((step - 1) * RB, RB), RB)
        fetch_w(step - 1).wait()
        w_t = w_ref[here, :].T
        in_block = hot(NB, blk_ref[...])
        picked = dot(mt_ref[...], jnp.concatenate([in_block, in_block], axis=0))
        values = [
            jnp.sum(picked[axis * NK : (axis + 1) * NK, :] * w_t, axis=0, keepdims=True) for axis in range(3)
        ]

        def sides(value):
            return [side.astype(BF16) for side in halves(value)]

        parts = [sides(value) for value in values]

        def placed(count, slot, code):
            mask = match(count, slot)
            both = [pick(mask, part[side]) for side in range(2) for part in parts + [sides(code)]]
            return jnp.concatenate(both, axis=0)

        packed = placed(CAP, rank_ref[:, here], node_ref[...].astype(F32))
        main_ref[...] += dot_t(packed, hot(ND, own_ref[...]))
        packed = [placed(RIM, place_ref[i : i + 1, here], code_ref[i : i + 1, here]) for i in range(3)]
        named = [hot(ND, dest_ref[i : i + 1, here]) for i in range(3)]
        rims_ref[...] += dot_t(jnp.concatenate(packed, axis=1), jnp.concatenate(named, axis=1))
        wt_ref[...] = w_t

    @pl.when(step == RSTEPS)
    def _():
        most = jnp.max(over_ref[...], axis=1, keepdims=True)
        flag = jnp.where(most >= RIM - 1, 1.0, 0.0)
        send_ref[:, 0, 0:MAIN] = (main_ref[0:MAIN, :] + main_ref[MAIN : 2 * MAIN, :]).T
        tail = (rims_ref[0 : 4 * RIM, :] + rims_ref[4 * RIM : 8 * RIM, :]).T
        send_ref[:, 0, MAIN : MAIN + 4 * RIM] = jnp.where(iota((ND, 4 * RIM), 1) == 4 * RIM - 1, flag, tail)


def loads_to_send(pops, weights, block_row, owner_row, node_row, mass, modulus, live):
    def record(i):
        return jnp.maximum(i - 1, 0)

    row_spec = pl.BlockSpec((1, RB), lambda i: (0, record(i)))
    all_rows = pl.BlockSpec((1, R), lambda i: (0, 0))

    def whole(*shape):
        return pl.BlockSpec(shape, lambda i: (0, 0))

    return pl.pallas_call(
        load_kernel,
        grid=(1 + RSTEPS,),
        in_specs=[
            pl.BlockSpec(memory_space=pltpu.HBM),
            pl.BlockSpec(memory_space=pltpu.HBM),
            row_spec,
            all_rows,
            all_rows,
            row_spec,
            row_spec,
            whole(NU, NV),
            whole(NU, NV),
            whole(NU, NV),
        ],
        out_specs=[
            pl.BlockSpec((ND, 1, MAIN + 4 * RIM), lambda i: (0, 0, 0)),
            all_rows,
            pl.BlockSpec((NK, RB), lambda i: (0, record(i))),
            whole(XMSG, NK),
            whole(XMSG, NK),
            whole(160, NK),
            whole(160, NK),
        ],
        out_shape=[
            jax.ShapeDtypeStruct((ND, 1, MAIN + 4 * RIM), F32),
            jax.ShapeDtypeStruct((1, R), jnp.int32),
            jax.ShapeDtypeStruct((NK, R), F32),
            jax.ShapeDtypeStruct((XMSG, NK), F32),
            jax.ShapeDtypeStruct((XMSG, NK), F32),
            jax.ShapeDtypeStruct((160, NK), F32),
            jax.ShapeDtypeStruct((160, NK), F32),
        ],
        scratch_shapes=[
            pltpu.VMEM((19, NB, NK), F32),
            pltpu.SemaphoreType.DMA((CHUNKS,)),
            pltpu.VMEM((R, NK), F32),
            pltpu.SemaphoreType.DMA((RSTEPS,)),
            pltpu.VMEM((3, NB, NK), F32),
            pltpu.VMEM((3 * NK, 2 * NB), BF16),
            pltpu.VMEM((256, 512), BF16),
            pltpu.VMEM((2 * ND, 256), F32),
            pltpu.VMEM((8, R), jnp.int32),
            pltpu.VMEM((8, R), F32),
            pltpu.VMEM((8, R), jnp.int32),
            pltpu.VMEM((1, 256), F32),
            pltpu.VMEM((2 * MAIN, ND), F32),
            pltpu.VMEM((8 * RIM, ND), F32),
        ],
        compiler_params=pltpu.CompilerParams(vmem_limit_bytes=VMEM_LIMIT),
        name="loads",
    )(pops, weights, block_row, owner_row, node_row, owner_row, node_row, mass, modulus, live)


LINES = 8


def collide_kernel(pop_hbm, out_hbm, pop_ref, read_ref, in_sems, out_sems):
    chunks = 32 // LINES

    def fetch(part):
        rows = pl.ds(part * LINES * 8, LINES * 8)
        return pltpu.make_async_copy(pop_hbm.at[:, rows, :], pop_ref.at[:, rows, :], in_sems.at[part])

    def store(part):
        first = max(part * LINES - 1, 0) * 8
        last = NB if part == chunks - 1 else (part * LINES + LINES - 1) * 8
        rows = pl.ds(first, last - first)
        kept = pl.ds(first + 8, last - first)
        return pltpu.make_async_copy(read_ref.at[:, kept, :], out_hbm.at[:, rows, :], out_sems.at[part])

    def line(x, _):
        rows = pl.ds(pl.multiple_of(x * 8, 8), 8)
        values = relaxed_of([pop_ref[q, rows, :] for q in range(19)], range(19))
        for q in range(19):
            cx, cy, _ = DIRS[q]
            to = pl.ds(pl.multiple_of((x + cx + 1) * 8, 8), 8)
            read_ref[q, to, :] = turned_y(values[q], cy)
        return 0

    for part in range(chunks):
        fetch(part).start()
    for q in XP:
        read_ref[q, 8:16, :] = jnp.zeros((8, NK), F32)
    for q in XM:
        read_ref[q, NB : NB + 8, :] = jnp.zeros((8, NK), F32)
    for part in range(chunks):
        fetch(part).wait()
        lax.fori_loop(part * LINES, (part + 1) * LINES, line, 0, unroll=4)
        store(part).start()
    for part in range(chunks):
        store(part).wait()


def collide_and_run(pops):
    return pl.pallas_call(
        collide_kernel,
        in_specs=[pl.BlockSpec(memory_space=pltpu.HBM)],
        out_specs=pl.BlockSpec(memory_space=pltpu.HBM),
        out_shape=jax.ShapeDtypeStruct((19, NB, NK), F32),
        scratch_shapes=[
            pltpu.VMEM((19, NB, NK), F32),
            pltpu.VMEM((19, NB + 16, NK), F32),
            pltpu.SemaphoreType.DMA((32 // LINES,)),
            pltpu.SemaphoreType.DMA((32 // LINES,)),
        ],
        compiler_params=pltpu.CompilerParams(vmem_limit_bytes=VMEM_LIMIT),
        name="collide",
    )(pops)


def node_rows(recv_t):
    node = recv_t[3 * CAP : MAIN, :].astype(jnp.int32)
    return node >> 8, node & 255


def force_kernel(recv_ref, f_ref, rim_ref, u_ref, v_ref, hl_ref, ru_ref, rv_ref, rhl_ref):
    recv_t = recv_ref[:, 0, :].T
    u_ref[...], v_ref[...] = node_rows(recv_t)
    high, low = halves(recv_t[0 : 3 * CAP, :])
    hl_ref[0 : 3 * CAP, :] = high
    hl_ref[3 * CAP : 6 * CAP, :] = low
    code = recv_t[MAIN + 3 * RIM : MAIN + 4 * RIM, :].astype(jnp.int32)
    ru_ref[...] = code >> 8
    rv_ref[...] = code & 255
    high, low = halves(recv_t[MAIN : MAIN + 3 * RIM, :])
    rhl_ref[0 : 3 * RIM, :] = high
    rhl_ref[3 * RIM : 6 * RIM, :] = low

    def chunk_of(rows_ref, cols_ref, vals_ref, slots, height, width):
        def chunk(i, acc):
            at = pl.multiple_of(i * 8, 8)
            u8 = rows_ref[pl.ds(at, 8), :]
            v8 = cols_ref[pl.ds(at, 8), :]
            vals = [vals_ref[pl.ds(pl.multiple_of(part * slots + at, 8), 8), :].astype(BF16) for part in range(6)]
            lhs, rhs = [], []
            for r in range(8):
                here = match(max(height, 16), u8[r : r + 1, :])
                lhs.append(jnp.concatenate([pick(here, vals[part][r : r + 1, :]) for part in range(6)], axis=0))
                rhs.append(hot(width, v8[r : r + 1, :]))
            return acc + dot_t(jnp.concatenate(lhs, axis=1), jnp.concatenate(rhs, axis=1))

        return lax.fori_loop(0, slots // 8, chunk, jnp.zeros((6 * max(height, 16), width), F32), unroll=4)

    acc = chunk_of(u_ref, v_ref, hl_ref, CAP, NU // 2, 2 * NV)
    for c in range(3):
        pair = acc[c * 32 : (c + 1) * 32, :] + acc[(3 + c) * 32 : (4 + c) * 32, :]
        f_ref[c, pl.ds(0, 32, stride=2), :] = pair[:, 0:NV]
        f_ref[c, pl.ds(1, 32, stride=2), :] = pair[:, NV : 2 * NV]
    acc = chunk_of(ru_ref, rv_ref, rhl_ref, RIM, 8, EV)
    for c in range(3):
        rim_ref[c] = acc[c * 16 : c * 16 + 8, :] + acc[(3 + c) * 16 : (3 + c) * 16 + 8, :]


def force_of(recv):
    return pl.pallas_call(
        force_kernel,
        out_shape=[jax.ShapeDtypeStruct((3, NU, NV), F32), jax.ShapeDtypeStruct((3, 8, EV), F32)],
        scratch_shapes=[
            pltpu.VMEM((CAP, ND), jnp.int32),
            pltpu.VMEM((CAP, ND), jnp.int32),
            pltpu.VMEM((6 * CAP, ND), F32),
            pltpu.VMEM((RIM, ND), jnp.int32),
            pltpu.VMEM((RIM, ND), jnp.int32),
            pltpu.VMEM((6 * RIM, ND), F32),
        ],
        compiler_params=pltpu.CompilerParams(vmem_limit_bytes=SMALL_LIMIT),
        name="force",
    )(recv)


def rim_tile(i, low, high):
    sub = iota((8, 128), 0)
    tile = jnp.where(sub == 0, high[2 * i : 2 * i + 1, :], 0.0)
    tile = jnp.where(sub == 1, high[2 * i + 1 : 2 * i + 2, :], tile)
    return jnp.where(sub == 7, low[i : i + 1, :], tile)


def side_kernel(mass_ref, mod_ref, live_ref, xp_ref, xm_ref, yp_ref, ym_ref, to_p_ref, to_m_ref):
    to_p_ref[0:160, :] = yp_ref[...]
    to_m_ref[0:160, :] = ym_ref[...]
    for q, line, from_ref in ((7, 0, xp_ref), (10, 31, xm_ref)):
        face = (XP if line == 0 else XM).index(q) * 8
        at = YP.index(q) * 32 + line
        to_p_ref[at : at + 1, :] = from_ref[face : face + 1, :]
    for q, line, from_ref in ((9, 0, xp_ref), (8, 31, xm_ref)):
        face = (XP if line == 0 else XM).index(q) * 8 + 7
        at = YM.index(q) * 32 + line
        to_m_ref[at : at + 1, :] = from_ref[face : face + 1, :]
    to_p_ref[160:YMSG, :] = jnp.zeros((YMSG - 160, NK), F32)
    to_m_ref[160:YMSG, :] = jnp.zeros((YMSG - 160, NK), F32)
    low, high = xp_ref[40:XMSG, 0:NV], xm_ref[40:XMSG, 0:NV]
    for i, field in enumerate([mass_ref[...], mod_ref[...], live_ref[...].astype(F32)]):
        tall = jnp.concatenate([field, rim_tile(i, low, high), jnp.zeros((128 - EU, 128), F32)], axis=0)
        turned = tall.T
        to_p_ref[160 + i : 161 + i, 0:128] = turned[127:128, :]
        to_m_ref[160 + 2 * i : 162 + 2 * i, 0:128] = turned[0:2, :]


def sides_of(mass, modulus, live, xp, xm, yp, ym):
    return pl.pallas_call(
        side_kernel,
        out_shape=[jax.ShapeDtypeStruct((YMSG, NK), F32), jax.ShapeDtypeStruct((YMSG, NK), F32)],
        compiler_params=pltpu.CompilerParams(vmem_limit_bytes=VMEM_LIMIT),
        name="sides",
    )(mass, modulus, live, xp, xm, yp, ym)


def shell_kernel(
    stiff_ref, f_ref, rim_ref, mass_ref, mod_ref, live_ref, ulow_ref, uhigh_ref, vlow_ref, vhigh_ref, recv_ref,
    y_ref, ret_ref,
    e_ref, c_ref, g_ref, y_ext_ref, fy_ref, u_ref, v_ref, rt_ref,
):
    sub = iota((8, 128), 0)

    def columns(near, far, before):
        first = jnp.where(sub == 0, near, 0.0)
        first = jnp.where(sub == 1, far, first)
        last = jnp.where(sub == 7, before, 0.0)
        return jnp.concatenate([first, jnp.zeros((112, 128), F32), last], axis=0).T

    for i, field in enumerate([mass_ref[...], mod_ref[...], live_ref[...].astype(F32)]):
        e_ref[3 + i, 0:NU, 0:NV] = field
        e_ref[3 + i, NU:EU, 0:NV] = rim_tile(i, ulow_ref[:, 0:NV], uhigh_ref[:, 0:NV])
        side = columns(
            vhigh_ref[2 * i : 2 * i + 1, 0:128],
            vhigh_ref[2 * i + 1 : 2 * i + 2, 0:128],
            vlow_ref[i : i + 1, 0:128],
        )
        e_ref[3 + i, :, NV:EV] = side[0:EU, :]
    wide = iota((8, EV), 0)
    for i in range(3):
        e_ref[i, 0:NU, 0:NV] = f_ref[i]
        tile = jnp.where(wide == 0, rim_ref[i, 1:2, :], 0.0)
        tile = jnp.where(wide == 1, rim_ref[i, 2:3, :], tile)
        e_ref[i, NU:EU, :] = jnp.where(wide == 7, rim_ref[i, 0:1, :], tile)
        side = columns(rim_ref[i, 4:5, 0:128], rim_ref[i, 5:6, 0:128], rim_ref[i, 3:4, 0:128])
        e_ref[i, 0:NU, NV:EV] = side[0:NU, :]

    def up(x):
        return pltpu.roll(x, EU - 1, 0)

    def right(x):
        return pltpu.roll(x, EV - 1, 1)

    def down(x):
        return pltpu.roll(x, 1, 0)

    def left(x):
        return pltpu.roll(x, 1, 1)

    mod = e_ref[4]
    mod = mod + up(mod)
    e_ref[5] = e_ref[5] * (mod + right(mod)) * 0.25
    for c in range(3):
        field = e_ref[c]
        moved = up(field)
        c_ref[c] = field
        c_ref[3 + c] = moved
        c_ref[6 + c] = right(field)
        c_ref[9 + c] = right(moved)

    def cells(t, _):
        rows = pl.ds(pl.multiple_of(t * 8, 8), 8)
        corner = [c_ref[k, rows, :] for k in range(12)]
        scale = e_ref[5, rows, :]
        for k in range(12):
            total = stiff_ref[k, 0] * corner[0]
            for m in range(1, 12):
                total = total + stiff_ref[k, m] * corner[m]
            g_ref[k, rows, :] = scale * total
        return 0

    lax.fori_loop(0, EU // 8, cells, 0, unroll=3)
    mass = e_ref[3]
    for c in range(3):
        spread = g_ref[c] + down(g_ref[3 + c])
        beside = g_ref[6 + c] + down(g_ref[9 + c])
        y_ext_ref[c] = mass * e_ref[c] + spread + left(beside)
        y_ref[c] = y_ext_ref[c, 0:NU, 0:NV]
    for c in range(3):
        field = y_ext_ref[c]
        moved = up(field)
        c_ref[c] = field
        c_ref[3 + c] = moved
        c_ref[6 + c] = right(field)
        c_ref[9 + c] = right(moved)

    def energy(t, sums):
        rows = pl.ds(pl.multiple_of(t * 8, 8), 8)
        corner = [c_ref[k, rows, 0:NV] for k in range(12)]
        total = None
        for k in range(12):
            inner = stiff_ref[k, 0] * corner[0]
            for m in range(1, 12):
                inner = inner + stiff_ref[k, m] * corner[m]
            total = corner[k] * inner if total is None else total + corner[k] * inner
        m3 = e_ref[5, rows, 0:NV] * total
        m0, m1, m2 = None, None, None
        for c in range(3):
            f = e_ref[c, rows, 0:NV]
            y = corner[c]
            m0 = f * f if m0 is None else m0 + f * f
            m1 = f * y if m1 is None else m1 + f * y
            m2 = y * y if m2 is None else m2 + y * y
        m3 = m3 + e_ref[3, rows, 0:NV] * m2
        return tuple(s + m for s, m in zip(sums, (m0, m1, m2, m3)))

    zero = jnp.zeros((8, NV), F32)
    sums = lax.fori_loop(0, NU // 8, energy, (zero, zero, zero, zero), unroll=2)
    lane = iota((1, 128), 1)
    moments = jnp.zeros((1, 128), F32)
    for i in range(4):
        whole = jnp.sum(jnp.sum(sums[i], axis=0, keepdims=True), axis=1, keepdims=True)
        moments = jnp.where(lane == i, whole, moments)
    over = jnp.max(recv_ref[:, 0, MAIN + 3 * RIM :], axis=0, keepdims=True)[:, RIM - 1 :]
    moments = jnp.where(lane == 4, over, moments)

    for c in range(3):
        for part, field in ((c, f_ref), (3 + c, y_ref)):
            rows = slice(part * 32, part * 32 + 32)
            for odd in range(2):
                value = field[c, pl.ds(odd, 32, stride=2), :]
                high = value.astype(BF16)
                fy_ref[rows, odd * NV : (odd + 1) * NV] = high
                fy_ref[rows, (2 + odd) * NV : (3 + odd) * NV] = (value - high.astype(F32)).astype(BF16)
    u_ref[...], v_ref[...] = node_rows(recv_ref[:, 0, 0:MAIN].T)
    u_of = iota((NU // 2, ND), 0)

    def chunk(i, _):
        at = pl.multiple_of(i * 8, 8)
        u8 = u_ref[pl.ds(at, 8), :]
        v8 = v_ref[pl.ds(at, 8), :]
        rhs = jnp.concatenate([hot(2 * NV, v8[r : r + 1, :]) for r in range(8)], axis=1)
        picked = dot(fy_ref[...], jnp.concatenate([rhs, rhs], axis=0))
        tiles = [jnp.zeros((8, ND), F32) for _ in range(6)]
        for r in range(8):
            here = u_of == u8[r : r + 1, :]
            for part in range(6):
                block = picked[part * 32 : (part + 1) * 32, r * ND : (r + 1) * ND]
                row = jnp.sum(jnp.where(here, block, 0.0), axis=0, keepdims=True)
                tiles[part] = jnp.where(sub == r, row, tiles[part])
        for part in range(6):
            rt_ref[pl.ds(pl.multiple_of(part * CAP + at, 8), 8), :] = tiles[part]
        return 0

    lax.fori_loop(0, CAP // 8, chunk, 0, unroll=8)
    ret_ref[:, 0, 0 : 6 * CAP] = rt_ref[...].T
    ret_ref[:, 0, 6 * CAP : 8 * CAP] = jnp.broadcast_to(moments, (ND, 128))


def shell_of(stiff, force, rim, mass, modulus, live, rims, recv):
    vmem = pl.BlockSpec(memory_space=pltpu.VMEM)
    return pl.pallas_call(
        shell_kernel,
        grid=(1,),
        in_specs=[pl.BlockSpec(memory_space=pltpu.SMEM)]
        + [vmem] * 5
        + [pl.BlockSpec((8, NK), lambda i: (5, 0))] * 2
        + [pl.BlockSpec((8, NK), lambda i: (20, 0))] * 2
        + [vmem],
        out_specs=[vmem, vmem],
        out_shape=[
            jax.ShapeDtypeStruct((3, NU, NV), F32),
            jax.ShapeDtypeStruct((ND, 1, 8 * CAP), F32),
        ],
        scratch_shapes=[
            pltpu.VMEM((6, EU, EV), F32),
            pltpu.VMEM((12, EU, EV), F32),
            pltpu.VMEM((12, EU, EV), F32),
            pltpu.VMEM((3, EU, EV), F32),
            pltpu.VMEM((6 * NU // 2, 4 * NV), BF16),
            pltpu.VMEM((CAP, ND), jnp.int32),
            pltpu.VMEM((CAP, ND), jnp.int32),
            pltpu.VMEM((6 * CAP, ND), F32),
        ],
        compiler_params=pltpu.CompilerParams(vmem_limit_bytes=SMALL_LIMIT),
        name="shell",
    )(stiff, force, rim, mass, modulus, live, *rims, recv)


def scalar_kernel(part_ref, pq_ref, sound_ref):
    row = jnp.sum(part_ref[:, 0, :], axis=0, keepdims=True)
    lane = iota((1, 128), 1)
    m0, m1, m2, m3, over = [
        jnp.sum(jnp.where(lane == i, row, 0.0), axis=1, keepdims=True) for i in range(5)
    ]
    first = m0 / m1
    left_over = first * first * m2 - m0
    ratio = left_over / m0
    gain = 1.0 + ratio
    curve = gain * gain * m1 - 2.0 * gain * first * m2 + first * first * m3
    second = left_over / curve
    sound = (
        (over == 0.0)
        & (left_over > 1e-3 * m0)
        & (curve > 1e-2 * gain * gain * m1)
        & (curve < 1e30)
        & (m1 > 1e-30)
        & (m0 > 1e-30)
    )
    pq_ref[0] = (first + second * gain)[0, 0]
    pq_ref[1] = -(first * second)[0, 0]
    sound_ref[0] = jnp.where(sound, 1, 0)[0, 0]


def scalars_of(back):
    smem = pl.BlockSpec(memory_space=pltpu.SMEM)
    return pl.pallas_call(
        scalar_kernel,
        grid=(1,),
        in_specs=[pl.BlockSpec((ND, 1, 128), lambda i: (0, 0, 3))],
        out_specs=[smem, smem],
        out_shape=[jax.ShapeDtypeStruct((2,), F32), jax.ShapeDtypeStruct((1,), jnp.int32)],
        compiler_params=pltpu.CompilerParams(vmem_limit_bytes=VMEM_LIMIT),
        name="scalars",
    )(back)


OB = 2048
OREC = R // OB
XS = 16
OSTEPS = 32 // XS


def next_kernel(
    pq_ref, back_ref, w_ref, blk_ref, own_ref, rank_ref, f_ref, y_ref, read_ref, xp_ref, xm_ref, yp_ref, ym_ref,
    next_ref, disp_ref,
    x_ref, turned_ref, force_ref, buf_ref, sems,
):
    step = pl.program_id(0)

    def fetch(slab):
        rows = pl.ds(pl.multiple_of(slab * XS * 8, XS * 8), XS * 8)
        return pltpu.make_async_copy(read_ref.at[:, rows, :], buf_ref.at[:, rows, :], sems.at[slab])

    @pl.when(step == 0)
    def _():
        for slab in range(OSTEPS):
            fetch(slab).start()
        p = pq_ref[0]
        q = pq_ref[1]
        back = p * back_ref[:, 0, 0 : 3 * CAP] + q * back_ref[:, 0, 3 * CAP : 6 * CAP]
        turned = back.T * COUPLING
        high = turned.astype(BF16)
        x_ref[:, 0:ND] = high
        x_ref[:, ND : 2 * ND] = (turned - high.astype(F32)).astype(BF16)
        disp_ref[...] = p * f_ref[...] + q * y_ref[...]
        turned_ref[...] = jnp.zeros_like(turned_ref)

    @pl.when(step < OREC)
    def _():
        named = hot(ND, own_ref[...])
        picked = dot(x_ref[...], jnp.concatenate([named, named], axis=0))
        in_slot = iota((CAP, OB), 0) == rank_ref[...]
        w_t = w_ref[...]
        highs, lows = [], []
        for c in range(3):
            moved = jnp.sum(
                jnp.where(in_slot, picked[c * CAP : (c + 1) * CAP, :], 0.0), axis=0, keepdims=True
            )
            part = w_t * moved
            high = part.astype(BF16)
            highs.append(high)
            lows.append((part - high.astype(F32)).astype(BF16))
        in_block = hot(NB, blk_ref[...])
        parts = jnp.concatenate([jnp.concatenate(highs, axis=0), jnp.concatenate(lows, axis=0)], axis=1)
        turned_ref[...] += dot_t(parts, jnp.concatenate([in_block, in_block], axis=1))

    @pl.when(step == OREC)
    def _():
        for c in range(3):
            force_ref[c * NB : (c + 1) * NB, :] = turned_ref[c * NK : (c + 1) * NK, :].T

    @pl.when(step >= OREC)
    def _():
        slab = step - OREC
        fetch(slab).wait()
        sub = iota((8, NK), 0)
        for xx in range(XS):
            x = slab * XS + xx
            rows = pl.ds(pl.multiple_of(x * 8, 8), 8)
            forcing = [
                force_ref[pl.ds(pl.multiple_of(c * NB + x * 8, 8), 8), :] for c in range(3)
            ]
            for q in range(19):
                cx, cy, _ = DIRS[q]
                value = buf_ref[q, rows, :]
                if cx == 1 and xx == 0:
                    value = jnp.where(x == 0, xp_ref[XP.index(q) * 8 : XP.index(q) * 8 + 8, :], value)
                if cx == -1 and xx == XS - 1:
                    value = jnp.where(x == 31, xm_ref[XM.index(q) * 8 : XM.index(q) * 8 + 8, :], value)
                if cy == 1:
                    value = jnp.where(sub == 0, yp_ref[pl.ds(YP.index(q) * 32 + x, 1), :], value)
                if cy == -1:
                    value = jnp.where(sub == 7, ym_ref[pl.ds(YM.index(q) * 32 + x, 1), :], value)
                along = combine(forcing, DIRS[q])
                if along is not None:
                    value = value + (3.0 * WEIGHTS[q]) * along
                next_ref[q, xx * 8 : (xx + 1) * 8, :] = value


def outputs_of(pq, back, weights, block_row, owner_row, rank_row, force, image, read, xp, xm, yp, ym):
    def record(i):
        return jnp.minimum(i, OREC - 1)

    def slab(i):
        return jnp.maximum(i - OREC, 0)

    row_spec = pl.BlockSpec((1, OB), lambda i: (0, record(i)))
    patch = pl.BlockSpec((3, NU, NV), lambda i: (0, 0, 0))
    lines = pl.BlockSpec((19, XS * 8, NK), lambda i: (0, slab(i), 0))
    x_face = pl.BlockSpec((40, NK), lambda i: (0, 0))
    y_face = pl.BlockSpec((160, NK), lambda i: (0, 0))
    return pl.pallas_call(
        next_kernel,
        grid=(OREC + OSTEPS,),
        in_specs=[
            pl.BlockSpec(memory_space=pltpu.SMEM),
            pl.BlockSpec((ND, 1, 8 * CAP), lambda i: (0, 0, 0)),
            pl.BlockSpec((NK, OB), lambda i: (0, record(i))),
            row_spec,
            row_spec,
            row_spec,
            patch,
            patch,
            pl.BlockSpec(memory_space=pltpu.HBM),
            x_face,
            x_face,
            y_face,
            y_face,
        ],
        out_specs=[lines, patch],
        out_shape=[
            jax.ShapeDtypeStruct((19, NB, NK), F32),
            jax.ShapeDtypeStruct((3, NU, NV), F32),
        ],
        scratch_shapes=[
            pltpu.VMEM((3 * CAP, 2 * ND), BF16),
            pltpu.VMEM((3 * NK, NB), F32),
            pltpu.VMEM((3 * NB, NK), F32),
            pltpu.VMEM((19, NB, NK), F32),
            pltpu.SemaphoreType.DMA((OSTEPS,)),
        ],
        compiler_params=pltpu.CompilerParams(vmem_limit_bytes=VMEM_LIMIT),
        name="outputs",
    )(pq, back, weights, block_row, owner_row, rank_row, force, image, read, xp, xm, yp, ym)


def pass_on(x, axis, shift):
    count = lax.axis_size(axis)
    return lax.ppermute(x, axis, [(i, (i + shift) % count) for i in range(count)])


def padded(field):
    for axis, dim in (("gx", 1), ("gy", 2)):
        size = field.shape[dim]
        head = lax.slice_in_dim(field, 0, 1, axis=dim)
        tail = lax.slice_in_dim(field, size - 1, size, axis=dim)
        field = jnp.concatenate([pass_on(tail, axis, 1), field, pass_on(head, axis, -1)], axis=dim)
    return field


def operate(field, mass, modulus, live, stiff):
    static = padded(jnp.stack([modulus, live.astype(F32)]))
    wide = padded(field)

    def corners(a):
        return a[..., :-1, :-1], a[..., 1:, :-1], a[..., :-1, 1:], a[..., 1:, 1:]

    c0, c1, c2, c3 = corners(static[0])
    scale = static[1, :-1, :-1] * (c0 + c1 + c2 + c3) * 0.25
    vector = jnp.concatenate(corners(wide), axis=0)
    result = scale[None] * jnp.einsum("kl,lab->kab", stiff, vector, precision=lax.Precision.HIGHEST)
    return (
        mass[None] * field
        + result[0:3, 1:, 1:]
        + result[3:6, :-1, 1:]
        + result[6:9, 1:, :-1]
        + result[9:12, :-1, :-1]
    )


def rim_of(force):
    before = pass_on(force[:, NU - 1 : NU, :], "gx", 1)
    after = pass_on(force[:, 0:2, :], "gx", -1)
    tall = jnp.concatenate([force, after, before], axis=1)
    left = pass_on(tall[:, :, NV - 1 : NV], "gy", 1)
    right = pass_on(tall[:, :, 0:2], "gy", -1)
    gap = jnp.zeros((3, EV - NV - 3), F32)
    rows = [
        jnp.concatenate([tall[:, r], right[:, r], gap, left[:, r]], axis=1) for r in (NU + 2, NU, NU + 1)
    ]
    beside = [
        jnp.concatenate([column[:, 0:NU], jnp.zeros((3, EV - NU), F32)], axis=1)
        for column in (left[:, :, 0], right[:, :, 0], right[:, :, 1])
    ]
    empty = jnp.zeros((3, EV), F32)
    return jnp.stack(rows + beside + [empty, empty], axis=1)


def exchange(x):
    return lax.all_to_all(x, ALL, 0, 0, tiled=True)


def per_device(populations, mass, modulus, live, stiff, rec_block, rec_owner, rec_node, weights):
    pops = populations.reshape(19, NB, NK)
    block_row = rec_block.reshape(1, R)
    owner_row = rec_owner.reshape(1, R)
    node_row = rec_node.reshape(1, R)

    send, rank_row, turned, xp, xm, yp, ym = loads_to_send(
        pops, weights, block_row, owner_row, node_row, mass, modulus, live
    )
    xp = pass_on(xp, "gx", 1)
    xm = pass_on(xm, "gx", -1)
    recv = exchange(send)
    yp, ym = sides_of(mass, modulus, live, xp, xm, yp, ym)
    yp = pass_on(yp, "gy", 1)
    ym = pass_on(ym, "gy", -1)
    rims = (xp, xm, yp, ym)

    force, rim = force_of(recv)
    image, ret = shell_of(stiff, force, rim, mass, modulus, live, rims, recv)
    ret, pops = lax.optimization_barrier((ret, pops))
    back = exchange(ret)
    read = collide_and_run(pops)
    back, read = lax.optimization_barrier((back, read))
    pq, sound = scalars_of(back)

    def quick(operands):
        return operands[0:3]

    def careful(operands):
        _, _, _, force, mass, modulus, live, stiff, rims, recv = operands
        image, ret = shell_of(stiff, force, rim_of(force), mass, modulus, live, rims, recv)
        back = exchange(ret)
        start = lax.psum(jnp.sum(force * force), ALL)
        first = start / lax.psum(jnp.sum(force * image), ALL)
        residual = force - first * image
        norm = lax.psum(jnp.sum(residual * residual), ALL)
        ratio = norm / start
        direction = residual + ratio * force
        along = operate(direction, mass, modulus, live, stiff)
        second = norm / lax.psum(jnp.sum(direction * along), ALL)
        return jnp.stack([first + second * (1.0 + ratio), -(first * second)]), image, back

    pq, image, back = lax.cond(
        sound[0] == 1, quick, careful, (pq, image, back, force, mass, modulus, live, stiff, rims, recv)
    )

    populations_next, displacement = outputs_of(
        pq, back, turned, block_row, owner_row, rank_row, force, image, read, xp, xm, yp, ym
    )
    return populations_next.reshape(19, 32, 8, NK), displacement


def solution(mesh):
    return jax.shard_map(
        per_device,
        mesh=mesh,
        in_specs=(
            P(None, "gx", "gy", None),
            P("gx", "gy"),
            P("gx", "gy"),
            P("gx", "gy"),
            P(),
            P(ALL),
            P(ALL, None),
            P(ALL),
            P(ALL, None),
        ),
        out_specs=(P(None, "gx", "gy", None), P(None, "gx", "gy")),
        check_vma=False,
    )
```
